128 devices in a mesh: row: 16 (over x, z_hi, core), col: 8 (over z_lo, y).
Axes of the slice: x: 4, y: 4, z: 4 (z_hi: 2, z_lo: 2; z = z_hi * 2 + z_lo), core: 2. Of those that a mesh axis runs over, the one named last changes fastest.
Arguments:
- pair: bfloat16 [1024, 1024, 128], P('row', 'col'), may hold values from -6 to 6
- bias_weight: bfloat16 [128, 16], replicated
- single: bfloat16 [48, 1024, 768], P('col', 'row'), may hold values from -6 to 6
- w_qkv: bfloat16 [768, 2304], replicated, may hold values from -0.21875 to 0.21875
- w_out: bfloat16 [768, 768], replicated, may hold values from -0.21875 to 0.21875
- w_gate_up: bfloat16 [768, 3072], replicated, may hold values from -0.21875 to 0.21875
- w_down: bfloat16 [1536, 768], replicated, may hold values from -0.15625 to 0.15625
- cotangent: bfloat16 [48, 1024, 768], P('col', 'row'), may hold values from -300 to 300
Outputs:
- updated: bfloat16 [48, 1024, 768], P('col', 'row')
- pair_grad: float32 [1024, 1024, 128], P('row', 'col')
The draws below stay inside these ranges and needn't reach their ends.
All inputs are finite; a program needn't handle non-finite values.
Results may differ from the reference program's by a relative error of at most 0.012.
The reference program's roundings to bfloat16 on the way count: a program that leaves them out, or rounds other values in their place, can miss the bound.
Values may be sent and summed in bfloat16 or wider, within the bound.
No kernel may reach another device: no remote copies, remote signals or barrier semaphores. Data moves between devices by JAX's collectives and lax.ppermute only.
A program may use at most 192 MiB of HBM per device.

```python
import math
import jax
import jax.numpy as jnp
from jax import lax

D = 768
HEADS = 16
C = 128
TRANS = 1536
TOKENS = 1024
SAMPLES = 48


def draw_bias_weight(key, part):
    base = jnp.clip(jax.random.normal(jax.random.fold_in(key, 11), (C, HEADS), jnp.float32), -4.0, 4.0) * C ** (-0.5)
    return base.astype(jnp.bfloat16)


def steps_of(rng, extent, cuts, low, top_value):
    def one(axis_at, parts):
        steps = jax.random.uniform(jax.random.fold_in(jax.random.fold_in(rng, 6), axis_at), (parts,), jnp.float32, low / len(cuts), top_value / len(cuts))
        return jnp.repeat(jnp.exp(steps), extent[axis_at] // parts).reshape((-1,) + (1,) * (len(extent) - axis_at - 1))

    level = one(*cuts[0])
    for cut in cuts[1:]:
        level = level * one(*cut)
    return level


def gaussian(key, shape, deviation, reach, pieces=(), held_as=jnp.bfloat16):
    drawn = deviation * jax.random.normal(key, shape, jnp.float32)
    if pieces:
        drawn = drawn * steps_of(key, shape, pieces, -0.22, 0.18)
    return jnp.clip(drawn, -reach, reach).astype(held_as)


def setup_inputs(seed: int = 0) -> dict:
    keys = jax.random.split(jax.random.key(seed), 9)
    pair = gaussian(keys[0], (TOKENS, TOKENS, C), 1.0, 6.0, ((0, 16), (1, 8)))
    bias_weight = draw_bias_weight(jax.random.fold_in(keys[8], 71), 0)
    single = gaussian(keys[2], (SAMPLES, TOKENS, D), 1.0, 6.0, ((0, 8), (1, 16)))
    w_qkv = gaussian(keys[3], (D, 3 * D), D ** -0.5, 0.21875)
    w_out = gaussian(keys[4], (D, D), D ** -0.5, 0.21875)
    w_gate_up = gaussian(keys[5], (D, 2 * TRANS), D ** -0.5, 0.21875)
    w_down = gaussian(keys[6], (TRANS, D), TRANS ** -0.5, 0.15625)
    cotangent = gaussian(keys[7], (SAMPLES, TOKENS, D), 50.0, 300.0, ((0, 8), (1, 16)))
    return {"pair": pair, "bias_weight": bias_weight, "single": single, "w_qkv": w_qkv, "w_out": w_out, "w_gate_up": w_gate_up, "w_down": w_down, "cotangent": cotangent}


def normalize(values):
    mean_val = lax.optimization_barrier(jnp.mean(values, axis=-1, keepdims=True))
    centred = values - mean_val
    variance = lax.optimization_barrier(jnp.mean(centred * centred, axis=-1, keepdims=True))
    scaled = lax.rsqrt(variance + 1e-05)
    return (centred * scaled, scaled)

def project_pair(piece, bias_weight):
    normed_pair, scaled = normalize(piece.astype(jnp.float32))
    row_count, col_count, chans = normed_pair.shape
    flat = jnp.dot(normed_pair.reshape(row_count * col_count, chans), bias_weight.astype(jnp.float32), precision=lax.Precision.HIGHEST)
    return jnp.transpose(flat.reshape(row_count, col_count, -1), (2, 0, 1)).astype(jnp.bfloat16)

def attend_sample(queries, key_rows, value_rows, cotan, bias, head_count):
    row_count, width = queries.shape
    head_size = width // head_count
    high = lax.Precision.HIGHEST
    query_h = queries.astype(jnp.float32).reshape(row_count, head_count, head_size)
    key_h = key_rows.astype(jnp.float32).reshape(-1, head_count, head_size)
    value_h = value_rows.astype(jnp.float32).reshape(-1, head_count, head_size)
    cotan_h = cotan.astype(jnp.float32).reshape(row_count, head_count, head_size)
    scores = jnp.einsum('ihe,jhe->hij', query_h, key_h, precision=high) / math.sqrt(head_size) + bias.astype(jnp.float32)
    weights = jax.nn.softmax(scores, axis=-1)
    rounded = weights.astype(jnp.bfloat16).astype(jnp.float32)
    attended = jnp.einsum('hij,jhe->ihe', rounded, value_h, precision=high)
    dprob = jnp.einsum('ihe,jhe->hij', cotan_h, value_h, precision=high)
    row_delta = lax.optimization_barrier(jnp.sum(cotan_h * attended, axis=2))
    grad_term = weights * (dprob - jnp.transpose(row_delta)[:, :, None])
    return (attended.reshape(row_count, width), grad_term)

def transition(single, attended, w_out, w_gate_up, w_down):
    width = single.shape[-1]
    flat_in = single.reshape(-1, width).astype(jnp.float32)
    mid = flat_in + jnp.dot(attended.reshape(-1, width).astype(jnp.bfloat16), w_out, preferred_element_type=jnp.float32)
    normed_mid = normalize(mid)[0].astype(jnp.bfloat16)
    gate_up = jnp.dot(normed_mid, w_gate_up, preferred_element_type=jnp.float32)
    half = gate_up.shape[1] // 2
    hidden = (jax.nn.silu(gate_up[:, :half]) * gate_up[:, half:]).astype(jnp.bfloat16)
    result = mid + jnp.dot(hidden, w_down, preferred_element_type=jnp.float32)
    return result.astype(jnp.bfloat16).reshape(single.shape)

def back_norm(normed_grad, normed_pair, scaled):
    centred = normed_grad - lax.optimization_barrier(jnp.mean(normed_grad, axis=-1, keepdims=True))
    along = lax.optimization_barrier(jnp.mean(normed_grad * normed_pair, axis=-1, keepdims=True))
    return (centred - normed_pair * along) * scaled

def reference(pair, bias_weight, single, w_qkv, w_out, w_gate_up, w_down, cotangent):
    bias = project_pair(pair, bias_weight)
    normed = normalize(single.astype(jnp.float32))[0].astype(jnp.bfloat16)
    projected = jnp.dot(normed.reshape(-1, D), w_qkv, preferred_element_type=jnp.float32).astype(jnp.bfloat16)
    projected = projected.reshape(SAMPLES, TOKENS, 3 * D)

    def one_sample(carry, inputs):
        proj_s, cotan_s = inputs
        attended, grad_term = attend_sample(proj_s[:, :D], proj_s[:, D:2 * D], proj_s[:, 2 * D:], cotan_s, bias, HEADS)
        return (carry + grad_term, attended)
    start_grad = jnp.zeros((HEADS, TOKENS, TOKENS), jnp.float32)
    bias_grad, attended = lax.scan(one_sample, start_grad, (projected, cotangent))
    updated = transition(single, attended, w_out, w_gate_up, w_down)
    normed_pair, scaled = normalize(pair.astype(jnp.float32))
    flat_grad = jnp.transpose(bias_grad, (1, 2, 0)).reshape(TOKENS * TOKENS, HEADS)
    normed_grad = jnp.dot(flat_grad, jnp.transpose(bias_weight.astype(jnp.float32)), precision=lax.Precision.HIGHEST)
    normed_grad = normed_grad.reshape(TOKENS, TOKENS, C)
    pair_grad = back_norm(normed_grad, normed_pair, scaled)
    return (updated, pair_grad)
```

```python
import functools
import math

import jax
import jax.numpy as jnp
from jax import lax
from jax.experimental import pallas as pl
from jax.experimental.pallas import tpu as pltpu
from jax.sharding import PartitionSpec as P

BF = jnp.bfloat16
F32 = jnp.float32
LOG2E = 1.4426950408889634


def normalize(values):
    mean_val = jnp.mean(values, axis=-1, keepdims=True)
    centred = values - mean_val
    variance = jnp.mean(centred * centred, axis=-1, keepdims=True)
    scaled = lax.rsqrt(variance + 1e-05)
    return (centred * scaled, scaled)


def project_pair(piece, bias_weight):
    normed_pair, scaled = normalize(piece.astype(F32))
    row_count, col_count, chans = normed_pair.shape
    flat = jnp.dot(
        normed_pair.reshape(row_count * col_count, chans),
        bias_weight.astype(F32),
        precision=lax.Precision.HIGHEST,
    )
    return jnp.transpose(flat.reshape(row_count, col_count, -1), (2, 0, 1)).astype(BF)


def attend_kernel(n_col, n_chip, n_samp, size, c_ref, blk_ref, *refs):
    bias_refs = refs[:n_col]
    att_ref = refs[n_col]
    out_refs = refs[n_col + 1 : 2 * n_col + 1]
    bias2, acc, kt, vt = refs[2 * n_col + 1 :]
    samp = pl.program_id(0)
    me = c_ref[0]
    block = blk_ref.shape[2]
    wide = block * n_col

    @pl.when(samp == 0)
    def _():
        for k in range(n_col):
            bias2[:, k * block : (k + 1) * block] = bias_refs[k][...].astype(F32) * LOG2E
        acc[...] = jnp.zeros_like(acc)
        kt[2 * size :, :] = jnp.zeros((kt.shape[0] - 2 * size, wide), BF)
        row = lax.broadcasted_iota(jnp.int32, (vt.shape[0] - size, wide), 0)
        vt[size:, :] = jnp.where(row < 3, 1.0, 0.0).astype(BF)

    for k in range(n_col):
        owner = jnp.bitwise_xor(me, k)
        cols = slice(k * block, (k + 1) * block)
        keys = blk_ref[owner, size : 2 * size, :]
        kt[:size, cols] = keys
        kt[size : 2 * size, cols] = keys
        vt[:size, cols] = blk_ref[owner, 2 * size : 3 * size, :]

    scale = LOG2E / math.sqrt(size)

    def one_block(b, carry):
        rows = pl.ds(pl.multiple_of(b * block, block), block)
        query = blk_ref[b, :size, :].astype(F32) * scale
        high = query.astype(BF).astype(F32)
        rest = jnp.zeros((block - 2 * size, block), F32)
        lhs = jnp.concatenate([high, query - high, rest], axis=0).T.astype(BF)
        scores = jnp.dot(lhs, kt[...], preferred_element_type=F32) + bias2[rows, :]
        top = jnp.max(scores, axis=1, keepdims=True)
        probs = jnp.exp2(scores - top)
        total = jnp.sum(probs, axis=1, keepdims=True)
        probs = probs * (1.0 / total)
        attended = lax.dot_general(
            probs.astype(BF), vt[...], (((1,), (1,)), ((), ())), preferred_element_type=F32
        )
        attended_t = attended.T[:size]
        att_ref[b, :, :] = attended_t.astype(BF)
        cotan = blk_ref[b, 3 * size :, :].astype(F32)
        delta = -jnp.sum(cotan * attended_t, axis=0, keepdims=True)
        d0 = delta.astype(BF).astype(F32)
        d1 = (delta - d0).astype(BF).astype(F32)
        d2 = delta - d0 - d1
        row = lax.broadcasted_iota(jnp.int32, (block - size, block), 0)
        tail = jnp.where(row == 0, d0, jnp.where(row == 1, d1, jnp.where(row == 2, d2, 0.0)))
        lhs2 = jnp.concatenate([cotan, tail], axis=0).T.astype(BF)
        dprob = jnp.dot(lhs2, vt[...], preferred_element_type=F32)
        acc[rows, :] += probs * dprob
        return carry

    lax.fori_loop(0, n_chip, one_block, 0)

    @pl.when(samp == n_samp - 1)
    def _():
        for k in range(n_col):
            out_refs[k][...] = acc[:, k * block : (k + 1) * block].astype(BF)


def attend(me, qkvc, biases, n_samp, size):
    n_chip, _, _, lanes = qkvc.shape
    per = n_samp // 2
    block = lanes // per
    n_col = len(biases)
    tokens = n_chip * block
    wide = n_col * block
    whole = pl.BlockSpec((tokens, block), lambda s, c: (0, 0))
    spec = lambda feats: pl.BlockSpec((n_chip, None, feats, block), lambda s, c: (0, s // per, 0, s % per))
    return pl.pallas_call(
        functools.partial(attend_kernel, n_col, n_chip, n_samp, size),
        grid_spec=pltpu.PrefetchScalarGridSpec(
            num_scalar_prefetch=1,
            grid=(n_samp,),
            in_specs=[spec(4 * size)] + [whole] * n_col,
            out_specs=[spec(size)] + [whole] * n_col,
            scratch_shapes=[
                pltpu.VMEM((tokens, wide), F32),
                pltpu.VMEM((tokens, wide), F32),
                pltpu.VMEM((block, wide), BF),
                pltpu.VMEM((block, wide), BF),
            ],
        ),
        out_shape=[jax.ShapeDtypeStruct((n_chip, 2, size, lanes), BF)]
        + [jax.ShapeDtypeStruct((tokens, block), BF)] * n_col,
        compiler_params=pltpu.CompilerParams(
            dimension_semantics=("arbitrary",), vmem_limit_bytes=48 * 1024 * 1024
        ),
    )(me, qkvc, *biases)


def transition(flat_in, attended_t, w_out, w_gate_up, w_down):
    mid = flat_in.astype(F32) + lax.dot_general(
        attended_t, w_out, (((0,), (0,)), ((), ())), preferred_element_type=F32
    )
    normed_mid = normalize(mid)[0].astype(BF)
    gate_up = jnp.dot(normed_mid, w_gate_up, preferred_element_type=F32)
    half = gate_up.shape[1] // 2
    hidden = (jax.nn.silu(gate_up[:, :half]) * gate_up[:, half:]).astype(BF)
    result = mid + jnp.dot(hidden, w_down, preferred_element_type=F32)
    return result.astype(BF)


def swap_cores(axis, size):
    return [(i, i ^ 1) for i in range(size)]


def back_pair(pair, bias_grad, bias_weight):
    normed_pair, scaled = normalize(pair.astype(F32))
    normed_grad = lax.dot_general(
        bias_grad, bias_weight, (((0,), (1,)), ((), ())), preferred_element_type=F32
    )
    centred = normed_grad - jnp.mean(normed_grad, axis=-1, keepdims=True)
    along = jnp.mean(normed_grad * normed_pair, axis=-1, keepdims=True)
    return (centred - normed_pair * along) * scaled


def shards(n_row, n_col, pair, bias_weight, single, w_qkv, w_out, w_gate_up, w_down, cotangent):
    samp, rows, width = single.shape
    heads = bias_weight.shape[1]
    size = width // heads
    half = samp // 2
    block = 2 * rows
    n_chip = n_row // 2
    core = lax.rem(lax.axis_index("row"), 2)
    me = lax.axis_index("col").astype(jnp.int32).reshape(1)
    cores = [(i, i ^ 1) for i in range(n_row)]

    def join(values):
        keep = lax.dynamic_slice_in_dim(values, core * half, half, 0)
        send = lax.dynamic_slice_in_dim(values, (1 - core) * half, half, 0)
        got = lax.ppermute(send, "row", cores)
        first = jnp.where(core == 0, keep, got)
        second = jnp.where(core == 0, got, keep)
        return jnp.concatenate([first, second], axis=1)

    tokens = join(single).reshape(half * block, width)
    cotan = join(cotangent).reshape(half * block, width)

    bias = lax.all_to_all(project_pair(pair, bias_weight), "row", 0, 0, tiled=True)
    bias, tokens = lax.optimization_barrier((bias, tokens))
    bias = bias.reshape(n_row * rows, pair.shape[1])
    biases = [bias] + [
        lax.ppermute(bias, "col", [(i, i ^ k) for i in range(n_col)]) for k in range(1, n_col)
    ]

    normed = normalize(tokens.astype(F32))[0].astype(BF)
    projected = lax.dot_general(
        w_qkv, normed, (((0,), (1,)), ((), ())), preferred_element_type=F32
    ).astype(BF)
    projected = projected.reshape(3, heads, size, half * block)
    cotan_t = cotan.T.reshape(heads, size, half * block)
    packed = jnp.concatenate([projected[0], projected[1], projected[2], cotan_t], axis=1)
    packed = lax.all_to_all(packed, "row", 0, 0, tiled=True)
    packed = packed.reshape(n_chip, 2, 4 * size, half * block)
    attended, *grads = attend(me, packed, biases, samp, size)

    grads = [grads[0]] + [
        lax.ppermute(grads[k], "col", [(i, i ^ k) for i in range(n_col)]) for k in range(1, n_col)
    ]
    attended = attended.reshape(n_row, size, half * block)
    attended = lax.all_to_all(attended, "row", 0, 0, tiled=True)
    updated = transition(tokens, attended.reshape(width, half * block), w_out, w_gate_up, w_down)
    updated = updated.reshape(half, block, width)
    mine = lax.dynamic_slice_in_dim(updated, core * rows, rows, 1)
    theirs = lax.dynamic_slice_in_dim(updated, (1 - core) * rows, rows, 1)
    got = lax.ppermute(theirs, "row", cores)
    updated = jnp.concatenate([jnp.where(core == 0, mine, got), jnp.where(core == 0, got, mine)], axis=0)

    bias_grad = grads[0].astype(F32)
    for k in range(1, n_col):
        bias_grad = bias_grad + grads[k].astype(F32)
    bias_grad = bias_grad.astype(BF).reshape(n_row, rows, pair.shape[1])
    bias_grad = lax.all_to_all(bias_grad, "row", 0, 0, tiled=True)
    pair_grad = back_pair(pair, bias_grad, bias_weight)
    return (updated, pair_grad)


def solution(mesh):
    sizes = dict(mesh.shape)
    return jax.shard_map(
        functools.partial(shards, sizes["row"], sizes["col"]),
        mesh=mesh,
        in_specs=(
            P("row", "col", None),
            P(),
            P("col", "row", None),
            P(),
            P(),
            P(),
            P(),
            P("col", "row", None),
        ),
        out_specs=(P("col", "row", None), P("row", "col", None)),
        check_vma=False,
    )
```

```python
import functools
import math

import jax
import jax.numpy as jnp
from jax import lax
from jax.experimental import pallas as pl
from jax.experimental.pallas import tpu as pltpu
from jax.sharding import PartitionSpec as P

BF = jnp.bfloat16
F32 = jnp.float32
LOG2E = 1.4426950408889634


def unit(values):
    mean_val = jnp.mean(values, axis=-1, keepdims=True)
    centred = values - mean_val
    variance = jnp.mean(centred * centred, axis=-1, keepdims=True)
    scaled = lax.rsqrt(variance + 1e-05)
    return centred * scaled, scaled

def pair_kernel(pair_ref, w_ref, out_ref):
    rows, cols, chans = pair_ref.shape
    heads = w_ref.shape[0]
    normed, _ = unit(pair_ref[...].astype(F32).reshape(rows * cols, chans))
    high = normed.astype(BF)
    low = (normed - high.astype(F32)).astype(BF)
    both = jnp.concatenate([high, low], axis=1)
    flat = lax.dot_general(w_ref[...], both, (((1,), (1,)), ((), ())), preferred_element_type=F32)
    out_ref[...] = flat.reshape(heads, rows, cols).astype(BF)

def pair_bias(pair, bias_weight, step=16):
    rows, cols, chans = pair.shape
    heads = bias_weight.shape[1]
    w = bias_weight.T
    w = jnp.concatenate([w, w], axis=1)
    return pl.pallas_call(
        pair_kernel, grid=(rows // step,),
        in_specs=[pl.BlockSpec((step, cols, chans), lambda i: (i, 0, 0)),
                  pl.BlockSpec((heads, 2 * chans), lambda i: (0, 0))],
        out_specs=pl.BlockSpec((heads, step, cols), lambda i: (0, i, 0)),
        out_shape=jax.ShapeDtypeStruct((heads, rows, cols), BF),
        compiler_params=pltpu.CompilerParams(dimension_semantics=("arbitrary",), vmem_limit_bytes=48 << 20),
    )(pair, w)

def back_kernel(pair_ref, grad_ref, w_ref, out_ref):
    rows, cols, chans = pair_ref.shape
    heads = w_ref.shape[0]
    normed, scaled = unit(pair_ref[...].astype(F32).reshape(rows * cols, chans))
    grad = grad_ref[...].reshape(heads, rows * cols)
    normed_grad = lax.dot_general(grad, w_ref[...], (((0,), (0,)), ((), ())), preferred_element_type=F32)
    centred = normed_grad - jnp.mean(normed_grad, axis=-1, keepdims=True)
    along = jnp.mean(normed_grad * normed, axis=-1, keepdims=True)
    out_ref[...] = ((centred - normed * along) * scaled).reshape(rows, cols, chans)

def pair_back(pair, grad, bias_weight, step=16):
    rows, cols, chans = pair.shape
    heads = bias_weight.shape[1]
    return pl.pallas_call(
        back_kernel, grid=(rows // step,),
        in_specs=[pl.BlockSpec((step, cols, chans), lambda i: (i, 0, 0)),
                  pl.BlockSpec((heads, step, cols), lambda i: (0, i, 0)),
                  pl.BlockSpec((heads, chans), lambda i: (0, 0))],
        out_specs=pl.BlockSpec((step, cols, chans), lambda i: (i, 0, 0)),
        out_shape=jax.ShapeDtypeStruct((rows, cols, chans), F32),
        compiler_params=pltpu.CompilerParams(dimension_semantics=("arbitrary",), vmem_limit_bytes=48 << 20),
    )(pair, grad, bias_weight.T)

def project_kernel(core_ref, single_ref, got_ref, cot_ref, gotc_ref, w_ref, packed_ref, tokens_ref, normed, cotan):
    half, block, width = tokens_ref.shape
    heads, _, lanes = packed_ref.shape
    size = width // heads
    rows = block // 2
    step = pl.program_id(0)
    core = core_ref[0]

    @pl.when(step == 0)
    def _():
        mine = pl.ds(pl.multiple_of(core * rows, rows), rows)
        other = pl.ds(pl.multiple_of((1 - core) * rows, rows), rows)
        for u in range(half):
            for src, far, dst in ((single_ref, got_ref, tokens_ref), (cot_ref, gotc_ref, cotan)):
                dst[u, mine, :] = src[core * half + u]
                dst[u, other, :] = far[core * half + u]
        normed[...] = unit(tokens_ref[...].reshape(lanes, width).astype(F32))[0].astype(BF)
        turned = cotan[...].reshape(lanes, width).astype(F32).T.astype(BF)
        for h in range(heads):
            packed_ref[h, 3 * size : 4 * size, :] = turned[h * size : (h + 1) * size]

    cols = w_ref.shape[1]
    out = jnp.dot(normed[...], w_ref[...], preferred_element_type=F32).T.astype(BF)
    for p in range(3):
        @pl.when(step // 2 == p)
        def _():
            base = (step % 2) * (cols // size)
            for h in range(cols // size):
                packed_ref[base + h, p * size : (p + 1) * size, :] = out[h * size : (h + 1) * size]

def project(core, single, got, cot, gotc, w_qkv, heads):
    samp, rows, width = single.shape
    half, block = samp // 2, 2 * rows
    lanes = half * block
    size = width // heads
    whole = pl.BlockSpec((samp, rows, width), lambda i, c: (0, 0, 0))
    return pl.pallas_call(
        project_kernel,
        grid_spec=pltpu.PrefetchScalarGridSpec(
            num_scalar_prefetch=1, grid=(6,),
            in_specs=[whole] * 4 + [pl.BlockSpec((width, width // 2), lambda i, c: (0, i))],
            out_specs=[pl.BlockSpec((heads, 4 * size, lanes), lambda i, c: (0, 0, 0)),
                       pl.BlockSpec((half, block, width), lambda i, c: (0, 0, 0))],
            scratch_shapes=[pltpu.VMEM((lanes, width), BF), pltpu.VMEM((half, block, width), BF)],
        ),
        out_shape=[jax.ShapeDtypeStruct((heads, 4 * size, lanes), BF), jax.ShapeDtypeStruct((half, block, width), BF)],
        compiler_params=pltpu.CompilerParams(dimension_semantics=("arbitrary",), vmem_limit_bytes=48 << 20),
    )(core, single, got, cot, gotc, w_qkv)


def attend_kernel(n_col, n_chip, n_samp, size, span, unroll, c_ref, blk_ref, *refs):
    bias_refs = refs[:n_col]
    att_ref = refs[n_col]
    out_refs = refs[n_col + 1 : 2 * n_col + 1]
    bias2, acc, kt, vt = refs[2 * n_col + 1 :]
    samp = pl.program_id(0)
    me = c_ref[0]
    block = blk_ref.shape[2]
    wide = block * n_col

    @pl.when(samp == 0)
    def _():
        for k in range(n_col):
            bias2[:, k * block : (k + 1) * block] = bias_refs[k][...].astype(F32) * LOG2E
        acc[...] = jnp.zeros_like(acc)
        rest = block - 2 * size
        kt[2 * size :, :] = jnp.zeros((rest, wide), BF)
        row = lax.broadcasted_iota(jnp.int32, (rest, wide), 0)
        vt[2 * size :, :] = jnp.where(row < 3, 1.0, 0.0).astype(BF)

    for k in range(n_col):
        owner = jnp.bitwise_xor(me, k)
        cols = slice(k * block, (k + 1) * block)
        keys = blk_ref[owner, size : 2 * size, :]
        kt[:size, cols] = keys
        kt[size : 2 * size, cols] = keys
        vals = blk_ref[owner, 2 * size : 3 * size, :]
        vt[:size, cols] = vals
        vt[size : 2 * size, cols] = vals

    scale = LOG2E / math.sqrt(size)
    rest = block - 2 * size
    row = lax.broadcasted_iota(jnp.int32, (rest, block), 0)

    def split(v):
        high = v.astype(BF).astype(F32)
        return high, v - high

    def one_block(b, carry):
        rows = pl.ds(pl.multiple_of(b * (block * span), block * span), block * span)
        lhs = []
        for i in range(span):
            high, low = split(blk_ref[b * span + i, :size, :].astype(F32) * scale)
            lhs.append(jnp.concatenate([high, low, jnp.zeros((rest, block), F32)], axis=0).T.astype(BF))
        lhs = jnp.concatenate(lhs, axis=0) if span > 1 else lhs[0]
        scores = jnp.dot(lhs, kt[...], preferred_element_type=F32) + bias2[rows, :]
        top = jnp.max(scores, axis=1, keepdims=True)
        probs = jnp.exp2(scores - top)
        mixed = lax.dot_general(
            probs.astype(BF), vt[...], (((1,), (1,)), ((), ())), preferred_element_type=F32
        )
        lhs2 = []
        for i in range(span):
            mixed_t = mixed[i * block : (i + 1) * block].T
            inv = 1.0 / mixed_t[2 * size : 2 * size + 1]
            att = mixed_t[:size] * inv
            att_ref[b * span + i, :, :] = att.astype(BF)
            cotan = blk_ref[b * span + i, 3 * size :, :].astype(F32)
            delta = -jnp.sum(cotan * att, axis=0, keepdims=True) * inv
            high, low = split(cotan * inv)
            d0, rem = split(delta)
            d1, d2 = split(rem)
            tail = jnp.where(row == 0, d0, jnp.where(row == 1, d1, jnp.where(row == 2, d2, 0.0)))
            lhs2.append(jnp.concatenate([high, low, tail], axis=0).T.astype(BF))
        lhs2 = jnp.concatenate(lhs2, axis=0) if span > 1 else lhs2[0]
        acc[rows, :] += probs * jnp.dot(lhs2, vt[...], preferred_element_type=F32)
        return carry

    lax.fori_loop(0, n_chip // span, one_block, 0, unroll=unroll)

    @pl.when(samp == n_samp - 1)
    def _():
        for k in range(n_col):
            out_refs[k][...] = acc[:, k * block : (k + 1) * block].astype(BF)


def attend(me, qkvc, biases, n_samp, size, span=1, unroll=1):
    n_chip, _, _, lanes = qkvc.shape
    per = n_samp // 2
    block = lanes // per
    n_col = len(biases)
    tokens = n_chip * block
    wide = n_col * block
    whole = pl.BlockSpec((tokens, block), lambda s, c: (0, 0))
    spec = lambda feats: pl.BlockSpec((n_chip, None, feats, block), lambda s, c: (0, s // per, 0, s % per))
    return pl.pallas_call(
        functools.partial(attend_kernel, n_col, n_chip, n_samp, size, span, unroll),
        grid_spec=pltpu.PrefetchScalarGridSpec(
            num_scalar_prefetch=1,
            grid=(n_samp,),
            in_specs=[spec(4 * size)] + [whole] * n_col,
            out_specs=[spec(size)] + [whole] * n_col,
            scratch_shapes=[
                pltpu.VMEM((tokens, wide), F32),
                pltpu.VMEM((tokens, wide), F32),
                pltpu.VMEM((block, wide), BF),
                pltpu.VMEM((block, wide), BF),
            ],
        ),
        out_shape=[jax.ShapeDtypeStruct((n_chip, 2, size, lanes), BF)]
        + [jax.ShapeDtypeStruct((tokens, block), BF)] * n_col,
        compiler_params=pltpu.CompilerParams(
            dimension_semantics=("arbitrary",), vmem_limit_bytes=56 * 1024 * 1024
        ),
    )(me, qkvc, *biases)


def transition(flat_in, attended_t, w_out, w_gate_up, w_down):
    mid = flat_in.astype(F32) + lax.dot_general(
        attended_t, w_out, (((0,), (0,)), ((), ())), preferred_element_type=F32
    )
    normed_mid = unit(mid)[0].astype(BF)
    gate_up = jnp.dot(normed_mid, w_gate_up, preferred_element_type=F32)
    half = gate_up.shape[1] // 2
    hidden = (jax.nn.silu(gate_up[:, :half]) * gate_up[:, half:]).astype(BF)
    result = mid + jnp.dot(hidden, w_down, preferred_element_type=F32)
    return result.astype(BF)


def shards(n_row, n_col, pair, bias_weight, single, w_qkv, w_out, w_gate_up, w_down, cotangent):
    samp, rows, width = single.shape
    heads = bias_weight.shape[1]
    size = width // heads
    half = samp // 2
    block = 2 * rows
    n_chip = n_row // 2
    core = lax.rem(lax.axis_index("row"), 2).astype(jnp.int32)
    me = lax.axis_index("col").astype(jnp.int32).reshape(1)
    cores = [(i, i ^ 1) for i in range(n_row)]
    flip = lambda k: [(i, i ^ k) for i in range(n_col)]

    got = lax.ppermute(single, "row", cores)
    got_cot = lax.ppermute(cotangent, "row", cores)
    bias = lax.all_to_all(pair_bias(pair, bias_weight, 32), "row", 0, 0, tiled=True)
    bias = bias.reshape(n_row * rows, pair.shape[1])
    packed, tokens = project(core.reshape(1), single, got, cotangent, got_cot, w_qkv, heads)

    far = lax.ppermute(bias, "col", flip(n_col // 2))
    biases = [bias] + [lax.ppermute(bias, "col", flip(k)) for k in range(1, n_col // 2)]
    biases += [far] + [lax.ppermute(far, "col", flip(k)) for k in range(1, n_col // 2)]

    packed = lax.all_to_all(packed, "row", 0, 0, tiled=True)
    packed = packed.reshape(n_chip, 2, 4 * size, half * block)
    attended, *grads = attend(me, packed, biases, samp, size, n_chip)

    grads = [grads[0]] + [lax.ppermute(grads[k], "col", flip(k)) for k in range(1, n_col)]
    attended = attended.reshape(n_row, size, half * block)
    attended = lax.all_to_all(attended, "row", 0, 0, tiled=True)

    bias_grad = grads[0].astype(F32)
    for k in range(1, n_col):
        bias_grad = bias_grad + grads[k].astype(F32)
    attended, bias_grad = lax.optimization_barrier((attended, bias_grad.astype(BF)))
    bias_grad = bias_grad.reshape(n_row, rows, pair.shape[1])
    bias_grad = lax.all_to_all(bias_grad, "row", 0, 0, tiled=True)

    updated = transition(
        tokens.reshape(half * block, width), attended.reshape(width, half * block), w_out, w_gate_up, w_down
    )
    updated, bias_grad = lax.optimization_barrier((updated, bias_grad))
    updated = updated.reshape(half, block, width)
    mine = lax.dynamic_slice_in_dim(updated, core * rows, rows, 1)
    theirs = lax.dynamic_slice_in_dim(updated, (1 - core) * rows, rows, 1)
    got = lax.ppermute(theirs, "row", cores)
    updated = jnp.concatenate([jnp.where(core == 0, mine, got), jnp.where(core == 0, got, mine)], axis=0)
    pair_grad = pair_back(pair, bias_grad, bias_weight, 16)
    return (updated, pair_grad)


def solution(mesh):
    sizes = dict(mesh.shape)
    return jax.shard_map(
        functools.partial(shards, sizes["row"], sizes["col"]),
        mesh=mesh,
        in_specs=(
            P("row", "col", None),
            P(),
            P("col", "row", None),
            P(),
            P(),
            P(),
            P(),
            P("col", "row", None),
        ),
        out_specs=(P("col", "row", None), P("row", "col", None)),
        check_vma=False,
    )
```

```python
import functools
import math

import jax
import jax.numpy as jnp
from jax import lax
from jax.experimental import pallas as pl
from jax.experimental.pallas import tpu as pltpu
from jax.sharding import PartitionSpec as P

BF = jnp.bfloat16
F32 = jnp.float32
LOG2E = 1.4426950408889634


def unit(values):
    mean_val = jnp.mean(values, axis=-1, keepdims=True)
    centred = values - mean_val
    variance = jnp.mean(centred * centred, axis=-1, keepdims=True)
    scaled = lax.rsqrt(variance + 1e-05)
    return centred * scaled, scaled

def pair_kernel(pair_ref, w_ref, out_ref):
    rows, cols, chans = pair_ref.shape
    heads = w_ref.shape[1]
    normed, _ = unit(pair_ref[...].astype(F32).reshape(rows * cols, chans))
    high = normed.astype(BF)
    low = (normed - high.astype(F32)).astype(BF)
    weight = w_ref[...].astype(F32).T.astype(BF)
    both = jnp.concatenate([high, low], axis=1)
    weight = jnp.concatenate([weight, weight], axis=1)
    flat = lax.dot_general(weight, both, (((1,), (1,)), ((), ())), preferred_element_type=F32)
    out_ref[...] = flat.reshape(heads, rows, cols).astype(BF)

def pair_bias(pair, bias_weight, step=16):
    rows, cols, chans = pair.shape
    heads = bias_weight.shape[1]
    return pl.pallas_call(
        pair_kernel, grid=(rows // step,),
        in_specs=[pl.BlockSpec((step, cols, chans), lambda i: (i, 0, 0)),
                  pl.BlockSpec((chans, heads), lambda i: (0, 0))],
        out_specs=pl.BlockSpec((heads, step, cols), lambda i: (0, i, 0)),
        out_shape=jax.ShapeDtypeStruct((heads, rows, cols), BF),
        compiler_params=pltpu.CompilerParams(dimension_semantics=("arbitrary",), vmem_limit_bytes=60 << 20),
    )(pair, bias_weight)

def back_kernel(pair_ref, grad_ref, w_ref, out_ref):
    rows, cols, chans = pair_ref.shape
    heads, parts = grad_ref.shape[:2]
    normed, scaled = unit(pair_ref[...].astype(F32).reshape(rows * cols, chans))
    grad = grad_ref[:, 0].astype(F32)
    for g in range(1, parts):
        grad = grad + grad_ref[:, g].astype(F32)
    grad = grad.reshape(heads, rows * cols)
    high = grad.astype(BF)
    low = (grad - high.astype(F32)).astype(BF)
    weight = w_ref[...].astype(F32).T.astype(BF)
    both = jnp.concatenate([high, low], axis=0)
    weight = jnp.concatenate([weight, weight], axis=0)
    normed_grad = lax.dot_general(both, weight, (((0,), (0,)), ((), ())), preferred_element_type=F32)
    centred = normed_grad - jnp.mean(normed_grad, axis=-1, keepdims=True)
    along = jnp.mean(normed_grad * normed, axis=-1, keepdims=True)
    out_ref[...] = ((centred - normed * along) * scaled).reshape(rows, cols, chans)

def pair_back(pair, grad, bias_weight, step=16):
    rows, cols, chans = pair.shape
    heads, parts = grad.shape[:2]
    return pl.pallas_call(
        back_kernel, grid=(rows // step,),
        in_specs=[pl.BlockSpec((step, cols, chans), lambda i: (i, 0, 0)),
                  pl.BlockSpec((heads, parts, step, cols), lambda i: (0, 0, i, 0)),
                  pl.BlockSpec((chans, heads), lambda i: (0, 0))],
        out_specs=pl.BlockSpec((step, cols, chans), lambda i: (i, 0, 0)),
        out_shape=jax.ShapeDtypeStruct((rows, cols, chans), F32),
        compiler_params=pltpu.CompilerParams(dimension_semantics=("arbitrary",), vmem_limit_bytes=60 << 20),
    )(pair, grad, bias_weight)

def project_kernel(core_ref, single_ref, got_ref, cot_ref, gotc_ref, w_ref, packed_ref, tokens_ref, normed, cotan):
    half, block, width = tokens_ref.shape
    heads, _, lanes = packed_ref.shape
    size = width // heads
    rows = block // 2
    step = pl.program_id(0)
    core = core_ref[0]

    @pl.when(step == 0)
    def _():
        mine = pl.ds(pl.multiple_of(core * rows, rows), rows)
        other = pl.ds(pl.multiple_of((1 - core) * rows, rows), rows)
        for u in range(half):
            for src, far, dst in ((single_ref, got_ref, tokens_ref), (cot_ref, gotc_ref, cotan)):
                dst[u, mine, :] = src[core * half + u]
                dst[u, other, :] = far[core * half + u]
        normed[...] = unit(tokens_ref[...].reshape(lanes, width).astype(F32))[0].astype(BF)
        turned = cotan[...].reshape(lanes, width).astype(F32).T.astype(BF)
        for h in range(heads):
            packed_ref[h, 3 * size : 4 * size, :] = turned[h * size : (h + 1) * size]

    cols = w_ref.shape[1]
    out = jnp.dot(normed[...], w_ref[...], preferred_element_type=F32).T.astype(BF)
    for p in range(3):
        @pl.when(step // 2 == p)
        def _():
            base = (step % 2) * (cols // size)
            for h in range(cols // size):
                packed_ref[base + h, p * size : (p + 1) * size, :] = out[h * size : (h + 1) * size]

def project(core, single, got, cot, gotc, w_qkv, heads):
    samp, rows, width = single.shape
    half, block = samp // 2, 2 * rows
    lanes = half * block
    size = width // heads
    whole = pl.BlockSpec((samp, rows, width), lambda i, c: (0, 0, 0))
    return pl.pallas_call(
        project_kernel,
        grid_spec=pltpu.PrefetchScalarGridSpec(
            num_scalar_prefetch=1, grid=(6,),
            in_specs=[whole] * 4 + [pl.BlockSpec((width, width // 2), lambda i, c: (0, i))],
            out_specs=[pl.BlockSpec((heads, 4 * size, lanes), lambda i, c: (0, 0, 0)),
                       pl.BlockSpec((half, block, width), lambda i, c: (0, 0, 0))],
            scratch_shapes=[pltpu.VMEM((lanes, width), BF), pltpu.VMEM((half, block, width), BF)],
        ),
        out_shape=[jax.ShapeDtypeStruct((heads, 4 * size, lanes), BF), jax.ShapeDtypeStruct((half, block, width), BF)],
        compiler_params=pltpu.CompilerParams(dimension_semantics=("arbitrary",), vmem_limit_bytes=60 << 20),
    )(core, single, got, cot, gotc, w_qkv)


def attend_kernel(n_col, n_chip, n_samp, size, span, unroll, c_ref, blk_ref, *refs):
    bias_refs = refs[: n_col // 2]
    att_ref = refs[n_col // 2]
    out_refs = refs[n_col // 2 + 1 : n_col + 1]
    bias2, acc, kt, vt = refs[n_col + 1 :]
    half_rows = bias_refs[0].shape[1] // 2
    samp = pl.program_id(0)
    me = c_ref[0]
    block = blk_ref.shape[2]
    wide = block * n_col

    @pl.when(samp == 0)
    def _():
        for k in range(n_col):
            far = k // (n_col // 2)
            part = bias_refs[k % (n_col // 2)][:, far * half_rows : (far + 1) * half_rows, :]
            part = part.astype(F32).reshape(bias2.shape[0], block)
            bias2[:, k * block : (k + 1) * block] = part * LOG2E
        acc[...] = jnp.zeros_like(acc)
        rest = block - 2 * size
        kt[2 * size :, :] = jnp.zeros((rest, wide), BF)
        row = lax.broadcasted_iota(jnp.int32, (rest, wide), 0)
        vt[2 * size :, :] = jnp.where(row < 3, 1.0, 0.0).astype(BF)

    for k in range(n_col):
        owner = jnp.bitwise_xor(me, k)
        cols = slice(k * block, (k + 1) * block)
        keys = blk_ref[owner, size : 2 * size, :]
        kt[:size, cols] = keys
        kt[size : 2 * size, cols] = keys
        vals = blk_ref[owner, 2 * size : 3 * size, :]
        vt[:size, cols] = vals
        vt[size : 2 * size, cols] = vals

    scale = LOG2E / math.sqrt(size)
    rest = block - 2 * size
    row = lax.broadcasted_iota(jnp.int32, (rest, block), 0)

    def split(v):
        high = v.astype(BF).astype(F32)
        return high, v - high

    def one_block(b, carry):
        rows = pl.ds(pl.multiple_of(b * (block * span), block * span), block * span)
        lhs = []
        for i in range(span):
            high, low = split(blk_ref[b * span + i, :size, :].astype(F32) * scale)
            lhs.append(jnp.concatenate([high, low, jnp.zeros((rest, block), F32)], axis=0).T.astype(BF))
        lhs = jnp.concatenate(lhs, axis=0) if span > 1 else lhs[0]
        scores = jnp.dot(lhs, kt[...], preferred_element_type=F32) + bias2[rows, :]
        top = jnp.max(scores, axis=1, keepdims=True)
        probs = jnp.exp2(scores - top)
        mixed = lax.dot_general(
            probs.astype(BF), vt[...], (((1,), (1,)), ((), ())), preferred_element_type=F32
        )
        lhs2 = []
        for i in range(span):
            mixed_t = mixed[i * block : (i + 1) * block].T
            inv = 1.0 / mixed_t[2 * size : 2 * size + 1]
            att = mixed_t[:size] * inv
            att_ref[b * span + i, :, :] = att.astype(BF)
            cotan = blk_ref[b * span + i, 3 * size :, :].astype(F32)
            delta = -jnp.sum(cotan * att, axis=0, keepdims=True) * inv
            high, low = split(cotan * inv)
            d0, rem = split(delta)
            d1, d2 = split(rem)
            tail = jnp.where(row == 0, d0, jnp.where(row == 1, d1, jnp.where(row == 2, d2, 0.0)))
            lhs2.append(jnp.concatenate([high, low, tail], axis=0).T.astype(BF))
        lhs2 = jnp.concatenate(lhs2, axis=0) if span > 1 else lhs2[0]
        acc[rows, :] += probs * jnp.dot(lhs2, vt[...], preferred_element_type=F32)
        return carry

    lax.fori_loop(0, n_chip // span, one_block, 0, unroll=unroll)

    @pl.when(samp == n_samp - 1)
    def _():
        for k in range(n_col):
            part = acc[:, k * block : (k + 1) * block].astype(BF)
            out_ref = out_refs[k % (n_col // 2)]
            far = jnp.bitwise_xor(me // (n_col // 2), k // (n_col // 2))
            out_ref[:, far] = part.reshape(out_ref.shape[0], half_rows, block)


def attend(me, qkvc, biases, n_samp, size, span=1, unroll=1):
    n_chip, _, _, lanes = qkvc.shape
    per = n_samp // 2
    block = lanes // per
    n_col = 2 * len(biases)
    n_row, both_rows, _ = biases[0].shape
    tokens = n_chip * block
    wide = n_col * block
    whole = pl.BlockSpec((n_row, both_rows, block), lambda s, c: (0, 0, 0))
    parts = (n_row, 2, both_rows // 2, block)
    spec = lambda feats: pl.BlockSpec((n_chip, None, feats, block), lambda s, c: (0, s // per, 0, s % per))
    return pl.pallas_call(
        functools.partial(attend_kernel, n_col, n_chip, n_samp, size, span, unroll),
        grid_spec=pltpu.PrefetchScalarGridSpec(
            num_scalar_prefetch=1,
            grid=(n_samp,),
            in_specs=[spec(4 * size)] + [whole] * len(biases),
            out_specs=[spec(size)] + [pl.BlockSpec(parts, lambda s, c: (0, 0, 0, 0))] * len(biases),
            scratch_shapes=[
                pltpu.VMEM((tokens, wide), F32),
                pltpu.VMEM((tokens, wide), F32),
                pltpu.VMEM((block, wide), BF),
                pltpu.VMEM((block, wide), BF),
            ],
        ),
        out_shape=[jax.ShapeDtypeStruct((n_chip, 2, size, lanes), BF)]
        + [jax.ShapeDtypeStruct(parts, BF)] * len(biases),
        compiler_params=pltpu.CompilerParams(
            dimension_semantics=("arbitrary",), vmem_limit_bytes=56 * 1024 * 1024
        ),
    )(me, qkvc, *biases)


def transition(flat_in, attended_t, w_out, w_gate_up, w_down):
    mid = flat_in.astype(F32) + lax.dot_general(
        attended_t, w_out, (((0,), (0,)), ((), ())), preferred_element_type=F32
    )
    normed_mid = unit(mid)[0].astype(BF)
    gate_up = jnp.dot(normed_mid, w_gate_up, preferred_element_type=F32)
    half = gate_up.shape[1] // 2
    hidden = (jax.nn.silu(gate_up[:, :half]) * gate_up[:, half:]).astype(BF)
    result = mid + jnp.dot(hidden, w_down, preferred_element_type=F32)
    return result.astype(BF)


def shards(n_row, n_col, pair, bias_weight, single, w_qkv, w_out, w_gate_up, w_down, cotangent):
    samp, rows, width = single.shape
    heads = bias_weight.shape[1]
    size = width // heads
    half = samp // 2
    block = 2 * rows
    n_chip = n_row // 2
    core = lax.rem(lax.axis_index("row"), 2).astype(jnp.int32)
    me = lax.axis_index("col").astype(jnp.int32).reshape(1)
    cores = [(i, i ^ 1) for i in range(n_row)]
    flip = lambda k: [(i, i ^ k) for i in range(n_col)]

    got = lax.ppermute(single, "row", cores)
    got_cot = lax.ppermute(cotangent, "row", cores)
    bias = pair_bias(pair, bias_weight, 16)
    bias, got, got_cot = lax.optimization_barrier((bias, got, got_cot))
    far = lax.ppermute(bias, "col", flip(n_col // 2))
    packed, tokens = project(core.reshape(1), single, got, cotangent, got_cot, w_qkv, heads)
    bias = lax.all_to_all(jnp.concatenate([bias, far], axis=1), "row", 0, 0, tiled=True)
    biases = [bias] + [lax.ppermute(bias, "col", flip(k)) for k in range(1, n_col // 2)]

    packed = lax.all_to_all(packed, "row", 0, 0, tiled=True)
    packed = packed.reshape(n_chip, 2, 4 * size, half * block)
    attended, *grads = attend(me, packed, biases, samp, size, n_chip)
    grads = [grads[0]] + [lax.ppermute(grads[k], "col", flip(k)) for k in range(1, n_col // 2)]
    attended = attended.reshape(n_row, size, half * block)
    attended = lax.all_to_all(attended, "row", 0, 0, tiled=True)
    total = grads[0].astype(F32)
    for part in grads[1:]:
        total = total + part.astype(F32)
    attended, total = lax.optimization_barrier((attended, total.astype(BF)))
    total = total.reshape(2 * n_row, rows, pair.shape[1])
    groups = [[r * n_col + z * (n_col // 2) + y for r in range(n_row) for z in range(2)] for y in range(n_col // 2)]
    total = lax.all_to_all(total, ("row", "col"), 0, 0, tiled=True, axis_index_groups=groups)
    total = total.reshape(n_row, 2, rows, pair.shape[1])

    updated = transition(
        tokens.reshape(half * block, width), attended.reshape(width, half * block), w_out, w_gate_up, w_down
    )
    updated, total = lax.optimization_barrier((updated, total))
    updated = updated.reshape(half, block, width)
    mine = lax.dynamic_slice_in_dim(updated, core * rows, rows, 1)
    theirs = lax.dynamic_slice_in_dim(updated, (1 - core) * rows, rows, 1)
    got = lax.ppermute(theirs, "row", cores)
    updated = jnp.concatenate([jnp.where(core == 0, mine, got), jnp.where(core == 0, got, mine)], axis=0)
    pair_grad = pair_back(pair, total, bias_weight, 16)
    return (updated, pair_grad)


def solution(mesh):
    sizes = dict(mesh.shape)
    return jax.shard_map(
        functools.partial(shards, sizes["row"], sizes["col"]),
        mesh=mesh,
        in_specs=(
            P("row", "col", None),
            P(),
            P("col", "row", None),
            P(),
            P(),
            P(),
            P(),
            P("col", "row", None),
        ),
        out_specs=(P("col", "row", None), P("row", "col", None)),
        check_vma=False,
    )
```

```python
import functools
import math

import jax
import jax.numpy as jnp
from jax import lax
from jax.experimental import pallas as pl
from jax.experimental.pallas import tpu as pltpu
from jax.sharding import PartitionSpec as P

BF = jnp.bfloat16
F32 = jnp.float32
LOG2E = 1.4426950408889634


def unit(values):
    mean_val = jnp.mean(values, axis=-1, keepdims=True)
    centred = values - mean_val
    variance = jnp.mean(centred * centred, axis=-1, keepdims=True)
    scaled = lax.rsqrt(variance + 1e-05)
    return centred * scaled, scaled

def pair_kernel(pair_ref, w_ref, out_ref):
    rows, cols, chans = pair_ref.shape
    heads = w_ref.shape[0]
    normed, _ = unit(pair_ref[...].astype(F32).reshape(rows * cols, chans))
    high = normed.astype(BF)
    low = (normed - high.astype(F32)).astype(BF)
    weight = w_ref[...]
    both = jnp.concatenate([high, low], axis=1)
    weight = jnp.concatenate([weight, weight], axis=1)
    flat = lax.dot_general(weight, both, (((1,), (1,)), ((), ())), preferred_element_type=F32)
    flat = flat.reshape(heads, rows, cols).astype(BF)
    out_ref[:, 0] = flat
    out_ref[:, 1] = flat

def pair_bias(pair, bias_weight, step=16):
    rows, cols, chans = pair.shape
    heads = bias_weight.shape[1]
    return pl.pallas_call(
        pair_kernel, grid=(rows // step,),
        in_specs=[pl.BlockSpec((step, cols, chans), lambda i: (i, 0, 0)),
                  pl.BlockSpec((heads, chans), lambda i: (0, 0))],
        out_specs=pl.BlockSpec((heads, 2, step, cols), lambda i: (0, 0, i, 0)),
        out_shape=jax.ShapeDtypeStruct((heads, 2, rows, cols), BF),
        compiler_params=pltpu.CompilerParams(dimension_semantics=("arbitrary",), vmem_limit_bytes=60 << 20),
    )(pair, bias_weight.T)

def back_kernel(pair_ref, grad_ref, w_ref, out_ref):
    rows, cols, chans = pair_ref.shape
    heads, parts = grad_ref.shape[:2]
    normed, scaled = unit(pair_ref[...].astype(F32).reshape(rows * cols, chans))
    grad = grad_ref[:, 0].astype(F32)
    for g in range(1, parts):
        grad = grad + grad_ref[:, g].astype(F32)
    grad = grad.reshape(heads, rows * cols)
    high = grad.astype(BF)
    low = (grad - high.astype(F32)).astype(BF)
    weight = w_ref[...]
    both = jnp.concatenate([high, low], axis=0)
    weight = jnp.concatenate([weight, weight], axis=0)
    normed_grad = lax.dot_general(both, weight, (((0,), (0,)), ((), ())), preferred_element_type=F32)
    centred = normed_grad - jnp.mean(normed_grad, axis=-1, keepdims=True)
    along = jnp.mean(normed_grad * normed, axis=-1, keepdims=True)
    out_ref[...] = ((centred - normed * along) * scaled).reshape(rows, cols, chans)

def pair_back(pair, grad, bias_weight, step=16):
    rows, cols, chans = pair.shape
    heads, parts = grad.shape[:2]
    return pl.pallas_call(
        back_kernel, grid=(rows // step,),
        in_specs=[pl.BlockSpec((step, cols, chans), lambda i: (i, 0, 0)),
                  pl.BlockSpec((heads, parts, step, cols), lambda i: (0, 0, i, 0)),
                  pl.BlockSpec((heads, chans), lambda i: (0, 0))],
        out_specs=pl.BlockSpec((step, cols, chans), lambda i: (i, 0, 0)),
        out_shape=jax.ShapeDtypeStruct((rows, cols, chans), F32),
        compiler_params=pltpu.CompilerParams(dimension_semantics=("arbitrary",), vmem_limit_bytes=60 << 20),
    )(pair, grad, bias_weight.T)

def project_kernel(core_ref, single_ref, got_ref, cot_ref, gotc_ref, w_ref, packed_ref, tokens_ref, normed, cotan):
    half, block, width = tokens_ref.shape
    heads, _, lanes = packed_ref.shape
    size = width // heads
    rows = block // 2
    step = pl.program_id(0)
    core = core_ref[0]

    @pl.when(step == 0)
    def _():
        mine = pl.ds(pl.multiple_of(core * rows, rows), rows)
        other = pl.ds(pl.multiple_of((1 - core) * rows, rows), rows)
        for u in range(half):
            for src, far, dst in ((single_ref, got_ref, tokens_ref), (cot_ref, gotc_ref, cotan)):
                dst[u, mine, :] = src[core * half + u]
                dst[u, other, :] = far[core * half + u]
        normed[...] = unit(tokens_ref[...].reshape(lanes, width).astype(F32))[0].astype(BF)
        turned = cotan[...].reshape(lanes, width).astype(F32).T.astype(BF)
        for h in range(heads):
            packed_ref[h, 3 * size : 4 * size, :] = turned[h * size : (h + 1) * size]

    cols = w_ref.shape[1]
    out = jnp.dot(normed[...], w_ref[...], preferred_element_type=F32).T.astype(BF)
    for p in range(3):
        @pl.when(step // 2 == p)
        def _():
            base = (step % 2) * (cols // size)
            for h in range(cols // size):
                packed_ref[base + h, p * size : (p + 1) * size, :] = out[h * size : (h + 1) * size]

def project(core, single, got, cot, gotc, w_qkv, heads):
    samp, rows, width = single.shape
    half, block = samp // 2, 2 * rows
    lanes = half * block
    size = width // heads
    whole = pl.BlockSpec((samp, rows, width), lambda i, c: (0, 0, 0))
    return pl.pallas_call(
        project_kernel,
        grid_spec=pltpu.PrefetchScalarGridSpec(
            num_scalar_prefetch=1, grid=(6,),
            in_specs=[whole] * 4 + [pl.BlockSpec((width, width // 2), lambda i, c: (0, i))],
            out_specs=[pl.BlockSpec((heads, 4 * size, lanes), lambda i, c: (0, 0, 0)),
                       pl.BlockSpec((half, block, width), lambda i, c: (0, 0, 0))],
            scratch_shapes=[pltpu.VMEM((lanes, width), BF), pltpu.VMEM((half, block, width), BF)],
        ),
        out_shape=[jax.ShapeDtypeStruct((heads, 4 * size, lanes), BF), jax.ShapeDtypeStruct((half, block, width), BF)],
        compiler_params=pltpu.CompilerParams(dimension_semantics=("arbitrary",), vmem_limit_bytes=60 << 20),
    )(core, single, got, cot, gotc, w_qkv)

def transition_kernel(core_ref, tokens_ref, att_ref, wo_ref, wg_ref, wu_ref, wd_ref, mine_ref, theirs_ref, mid, normed, done):
    half, block, width = tokens_ref.shape
    rows = block // 2
    step = pl.program_id(0)

    @pl.when(step == 0)
    def _():
        attended = att_ref[...].astype(F32).T.astype(BF)
        flat = tokens_ref[...].reshape(half * block, width).astype(F32)
        flat = flat + jnp.dot(attended, wo_ref[...], preferred_element_type=F32)
        mid[...] = flat
        normed[...] = unit(flat)[0].astype(BF)

    gate = jnp.dot(normed[...], wg_ref[...], preferred_element_type=F32)
    up = jnp.dot(normed[...], wu_ref[...], preferred_element_type=F32)
    hidden = (jax.nn.silu(gate) * up).astype(BF)
    mid[...] += jnp.dot(hidden, wd_ref[...], preferred_element_type=F32)

    @pl.when(step == pl.num_programs(0) - 1)
    def _():
        done[...] = mid[...].astype(BF).reshape(half, block, width)
        core = core_ref[0]
        mine = pl.ds(pl.multiple_of(core * rows, rows), rows)
        other = pl.ds(pl.multiple_of((1 - core) * rows, rows), rows)
        for u in range(half):
            mine_ref[u] = done[u, mine, :]
            theirs_ref[u] = done[u, other, :]

def transition(core, tokens, attended_t, w_out, w_gate_up, w_down, steps=4):
    half, block, width = tokens.shape
    lanes = half * block
    inner = w_down.shape[0]
    part = inner // steps
    out = pl.BlockSpec((half, block // 2, width), lambda i, c: (0, 0, 0))
    return pl.pallas_call(
        transition_kernel,
        grid_spec=pltpu.PrefetchScalarGridSpec(
            num_scalar_prefetch=1, grid=(steps,),
            in_specs=[pl.BlockSpec((half, block, width), lambda i, c: (0, 0, 0)),
                      pl.BlockSpec((width, lanes), lambda i, c: (0, 0)),
                      pl.BlockSpec((width, width), lambda i, c: (0, 0)),
                      pl.BlockSpec((width, part), lambda i, c: (0, i)),
                      pl.BlockSpec((width, part), lambda i, c: (0, i + steps)),
                      pl.BlockSpec((part, width), lambda i, c: (i, 0))],
            out_specs=[out, out],
            scratch_shapes=[pltpu.VMEM((lanes, width), F32), pltpu.VMEM((lanes, width), BF),
                            pltpu.VMEM((half, block, width), BF)],
        ),
        out_shape=[jax.ShapeDtypeStruct((half, block // 2, width), BF)] * 2,
        compiler_params=pltpu.CompilerParams(dimension_semantics=("arbitrary",), vmem_limit_bytes=60 << 20),
    )(core, tokens, attended_t, w_out, w_gate_up, w_gate_up, w_down)


def attend_kernel(n_col, n_chip, n_samp, size, span, unroll, c_ref, blk_ref, *refs):
    bias_refs = refs[: n_col // 2]
    att_ref = refs[n_col // 2]
    out_refs = refs[n_col // 2 + 1 : n_col + 1]
    bias2, acc, kt, vt = refs[n_col + 1 :]
    side = c_ref[0] // (n_col // 2)
    samp = pl.program_id(0)
    me = c_ref[0]
    block = blk_ref.shape[2]
    wide = block * n_col

    @pl.when(samp == 0)
    def _():
        for k in range(n_col):
            far = jnp.bitwise_xor(side, k // (n_col // 2))
            part = bias_refs[k % (n_col // 2)][:, far]
            part = part.astype(F32).reshape(bias2.shape[0], block)
            bias2[:, k * block : (k + 1) * block] = part * LOG2E
        acc[...] = jnp.zeros_like(acc)
        rest = block - 2 * size
        kt[2 * size :, :] = jnp.zeros((rest, wide), BF)
        row = lax.broadcasted_iota(jnp.int32, (rest, wide), 0)
        vt[2 * size :, :] = jnp.where(row < 3, 1.0, 0.0).astype(BF)

    for k in range(n_col):
        owner = jnp.bitwise_xor(me, k)
        cols = slice(k * block, (k + 1) * block)
        keys = blk_ref[owner, size : 2 * size, :]
        kt[:size, cols] = keys
        kt[size : 2 * size, cols] = keys
        vals = blk_ref[owner, 2 * size : 3 * size, :]
        vt[:size, cols] = vals
        vt[size : 2 * size, cols] = vals

    scale = LOG2E / math.sqrt(size)
    rest = block - 2 * size
    row = lax.broadcasted_iota(jnp.int32, (rest, block), 0)

    def split(v):
        high = v.astype(BF).astype(F32)
        return high, v - high

    def one_block(b, carry):
        rows = pl.ds(pl.multiple_of(b * (block * span), block * span), block * span)
        lhs = []
        for i in range(span):
            high, low = split(blk_ref[b * span + i, :size, :].astype(F32) * scale)
            lhs.append(jnp.concatenate([high, low, jnp.zeros((rest, block), F32)], axis=0).T.astype(BF))
        lhs = jnp.concatenate(lhs, axis=0) if span > 1 else lhs[0]
        scores = jnp.dot(lhs, kt[...], preferred_element_type=F32) + bias2[rows, :]
        top = jnp.max(scores, axis=1, keepdims=True)
        probs = jnp.exp2(scores - top)
        mixed = lax.dot_general(
            probs.astype(BF), vt[...], (((1,), (1,)), ((), ())), preferred_element_type=F32
        )
        lhs2 = []
        for i in range(span):
            mixed_t = mixed[i * block : (i + 1) * block].T
            inv = 1.0 / mixed_t[2 * size : 2 * size + 1]
            att = mixed_t[:size] * inv
            att_ref[b * span + i, :, :] = att.astype(BF)
            cotan = blk_ref[b * span + i, 3 * size :, :].astype(F32)
            delta = -jnp.sum(cotan * att, axis=0, keepdims=True) * inv
            high, low = split(cotan * inv)
            d0, rem = split(delta)
            d1, d2 = split(rem)
            tail = jnp.where(row == 0, d0, jnp.where(row == 1, d1, jnp.where(row == 2, d2, 0.0)))
            lhs2.append(jnp.concatenate([high, low, tail], axis=0).T.astype(BF))
        lhs2 = jnp.concatenate(lhs2, axis=0) if span > 1 else lhs2[0]
        acc[rows, :] += probs * jnp.dot(lhs2, vt[...], preferred_element_type=F32)
        return carry

    lax.fori_loop(0, n_chip // span, one_block, 0, unroll=unroll)

    @pl.when(samp == n_samp - 1)
    def _():
        for k in range(n_col):
            part = acc[:, k * block : (k + 1) * block].astype(BF)
            out_ref = out_refs[k % (n_col // 2)]
            far = jnp.bitwise_xor(side, k // (n_col // 2))
            out_ref[:, far] = part.reshape(out_ref.shape[0], out_ref.shape[2], block)


def attend(me, qkvc, biases, n_samp, size, span=1, unroll=1):
    n_chip, _, _, lanes = qkvc.shape
    per = n_samp // 2
    block = lanes // per
    n_col = 2 * len(biases)
    tokens = n_chip * block
    wide = n_col * block
    parts = biases[0].shape
    whole = pl.BlockSpec(parts, lambda s, c: (0, 0, 0, 0))
    spec = lambda feats: pl.BlockSpec((n_chip, None, feats, block), lambda s, c: (0, s // per, 0, s % per))
    return pl.pallas_call(
        functools.partial(attend_kernel, n_col, n_chip, n_samp, size, span, unroll),
        grid_spec=pltpu.PrefetchScalarGridSpec(
            num_scalar_prefetch=1,
            grid=(n_samp,),
            in_specs=[spec(4 * size)] + [whole] * len(biases),
            out_specs=[spec(size)] + [whole] * len(biases),
            scratch_shapes=[
                pltpu.VMEM((tokens, wide), F32),
                pltpu.VMEM((tokens, wide), F32),
                pltpu.VMEM((block, wide), BF),
                pltpu.VMEM((block, wide), BF),
            ],
        ),
        out_shape=[jax.ShapeDtypeStruct((n_chip, 2, size, lanes), BF)]
        + [jax.ShapeDtypeStruct(parts, BF)] * len(biases),
        compiler_params=pltpu.CompilerParams(
            dimension_semantics=("arbitrary",), vmem_limit_bytes=56 * 1024 * 1024
        ),
    )(me, qkvc, *biases)


def shards(n_row, n_col, pair, bias_weight, single, w_qkv, w_out, w_gate_up, w_down, cotangent):
    samp, rows, width = single.shape
    heads = bias_weight.shape[1]
    size = width // heads
    half = samp // 2
    block = 2 * rows
    n_chip = n_row // 2
    core = lax.rem(lax.axis_index("row"), 2).astype(jnp.int32)
    me = lax.axis_index("col").astype(jnp.int32).reshape(1)
    cores = [(i, i ^ 1) for i in range(n_row)]
    flip = lambda k: [(i, i ^ k) for i in range(n_col)]

    got = lax.ppermute(single, "row", cores)
    got_cot = lax.ppermute(cotangent, "row", cores)
    groups = [[r * n_col + z * (n_col // 2) + y for r in range(n_row) for z in range(2)] for y in range(n_col // 2)]
    share = lambda v: lax.all_to_all(
        v.reshape(2 * n_row, rows, pair.shape[1]), ("row", "col"), 0, 0, tiled=True, axis_index_groups=groups
    ).reshape(n_row, 2, rows, pair.shape[1])
    bias = share(pair_bias(pair, bias_weight, 16))
    packed, tokens = project(core.reshape(1), single, got, cotangent, got_cot, w_qkv, heads)
    biases = [bias] + [lax.ppermute(bias, "col", flip(k)) for k in range(1, n_col // 2)]

    packed = lax.all_to_all(packed, "row", 0, 0, tiled=True)
    packed = packed.reshape(n_chip, 2, 4 * size, half * block)
    attended, *grads = attend(me, packed, biases, samp, size, n_chip)
    grads = [grads[0]] + [lax.ppermute(grads[k], "col", flip(k)) for k in range(1, n_col // 2)]
    attended = attended.reshape(n_row, size, half * block)
    attended = lax.all_to_all(attended, "row", 0, 0, tiled=True)
    total = grads[0].astype(F32)
    for part in grads[1:]:
        total = total + part.astype(F32)
    attended, total = lax.optimization_barrier((attended, total.astype(BF)))
    total = share(total)
    mine, theirs = transition(
        core.reshape(1), tokens, attended.reshape(width, half * block), w_out, w_gate_up, w_down
    )
    mine, theirs, total = lax.optimization_barrier((mine, theirs, total))
    got = lax.ppermute(theirs, "row", cores)
    updated = jnp.concatenate([jnp.where(core == 0, mine, got), jnp.where(core == 0, got, mine)], axis=0)
    pair_grad = pair_back(pair, total, bias_weight, 16)
    return (updated, pair_grad)


def solution(mesh):
    sizes = dict(mesh.shape)
    return jax.shard_map(
        functools.partial(shards, sizes["row"], sizes["col"]),
        mesh=mesh,
        in_specs=(
            P("row", "col", None),
            P(),
            P("col", "row", None),
            P(),
            P(),
            P(),
            P(),
            P("col", "row", None),
        ),
        out_specs=(P("col", "row", None), P("row", "col", None)),
        check_vma=False,
    )
```

```python
import functools
import math

import jax
import jax.numpy as jnp
from jax import lax
from jax.experimental import pallas as pl
from jax.experimental.pallas import tpu as pltpu
from jax.sharding import PartitionSpec as P

BF = jnp.bfloat16
F32 = jnp.float32
LOG2E = 1.4426950408889634

def unit(values):
    mean_val = jnp.mean(values, axis=-1, keepdims=True)
    centred = values - mean_val
    variance = jnp.mean(centred * centred, axis=-1, keepdims=True)
    scaled = lax.rsqrt(variance + 1e-05)
    return centred * scaled, scaled

def halves(v):
    high = v.astype(BF)
    return high, (v - high.astype(F32)).astype(BF)

def across(lhs, rhs):
    return lax.dot_general(lhs, rhs, (((1,), (1,)), ((), ())), preferred_element_type=F32)

def pair_kernel(pair_ref, w_ref, out_ref):
    rows, cols, chans = pair_ref.shape
    heads = w_ref.shape[0]
    values = pair_ref[...].astype(F32).reshape(rows * cols, chans)
    centred = values - jnp.mean(values, axis=-1, keepdims=True)
    weight = w_ref[...]
    flat = across(jnp.concatenate([weight, weight], axis=1), jnp.concatenate(halves(centred), axis=1))
    ones = jnp.full((8, 2 * chans), 1.0 / chans, BF)
    variance = across(ones, jnp.concatenate(halves(centred * centred), axis=1))[:1]
    flat = (flat * lax.rsqrt(variance + 1e-05)).reshape(heads, rows, cols).astype(BF)
    out_ref[:, 0] = flat
    out_ref[:, 1] = flat

def pair_bias(pair, bias_weight, step=16):
    rows, cols, chans = pair.shape
    heads = bias_weight.shape[1]
    return pl.pallas_call(
        pair_kernel, grid=(rows // step,),
        in_specs=[pl.BlockSpec((step, cols, chans), lambda i: (i, 0, 0)),
                  pl.BlockSpec((heads, chans), lambda i: (0, 0))],
        out_specs=pl.BlockSpec((heads, 2, step, cols), lambda i: (0, 0, i, 0)),
        out_shape=jax.ShapeDtypeStruct((heads, 2, rows, cols), BF),
        compiler_params=pltpu.CompilerParams(dimension_semantics=("arbitrary",), vmem_limit_bytes=60 << 20),
    )(pair, bias_weight.T)

def stats_kernel(pair_ref, normed_ref, scaled_ref):
    rows, cols, chans = pair_ref.shape
    normed, scaled = unit(pair_ref[...].astype(F32).reshape(rows * cols, chans))
    normed_ref[...] = normed.reshape(rows, cols, chans)
    lanes = jnp.broadcast_to(scaled, (rows * cols, chans)).reshape(rows, cols, chans)
    for i in range(rows):
        scaled_ref[i : i + 1] = lanes[i].T[:1]

def pair_stats(pair, step=16):
    rows, cols, chans = pair.shape
    return pl.pallas_call(
        stats_kernel, grid=(rows // step,),
        in_specs=[pl.BlockSpec((step, cols, chans), lambda i: (i, 0, 0))],
        out_specs=[pl.BlockSpec((step, cols, chans), lambda i: (i, 0, 0)), pl.BlockSpec((step, cols), lambda i: (i, 0))],
        out_shape=[jax.ShapeDtypeStruct((rows, cols, chans), F32), jax.ShapeDtypeStruct((rows, cols), F32)],
        compiler_params=pltpu.CompilerParams(dimension_semantics=("arbitrary",), vmem_limit_bytes=60 << 20),
    )(pair)

def back_kernel(normed_ref, scaled_ref, grad_ref, w_ref, out_ref):
    rows, cols, chans = normed_ref.shape
    heads, parts = grad_ref.shape[:2]
    grad = grad_ref[:, 0].astype(F32)
    for g in range(1, parts):
        grad = grad + grad_ref[:, g].astype(F32)
    grad = (grad * scaled_ref[...][None]).reshape(heads, rows * cols)
    high, low = halves(grad)
    weight = w_ref[...].astype(F32)
    w_high, w_low = halves(weight - jnp.mean(weight, axis=1, keepdims=True))
    both = jnp.concatenate([high, low, high, low], axis=0)
    weight = jnp.concatenate([w_high, w_high, w_low, w_low], axis=0)
    centred = lax.dot_general(both, weight, (((0,), (0,)), ((), ())), preferred_element_type=F32)
    normed = normed_ref[...].reshape(rows * cols, chans)
    along = jnp.mean(centred * normed, axis=-1, keepdims=True)
    out_ref[...] = (centred - normed * along).reshape(rows, cols, chans)

def pair_back(stats, grad, bias_weight, step=16):
    normed, scaled = stats
    rows, cols, chans = normed.shape
    heads, parts = grad.shape[:2]
    return pl.pallas_call(
        back_kernel, grid=(rows // step,),
        in_specs=[pl.BlockSpec((step, cols, chans), lambda i: (i, 0, 0)),
                  pl.BlockSpec((step, cols), lambda i: (i, 0)),
                  pl.BlockSpec((heads, parts, step, cols), lambda i: (0, 0, i, 0)),
                  pl.BlockSpec((heads, chans), lambda i: (0, 0))],
        out_specs=pl.BlockSpec((step, cols, chans), lambda i: (i, 0, 0)),
        out_shape=jax.ShapeDtypeStruct((rows, cols, chans), F32),
        compiler_params=pltpu.CompilerParams(dimension_semantics=("arbitrary",), vmem_limit_bytes=60 << 20),
    )(normed, scaled, grad, bias_weight.T)

def project_kernel(core_ref, single_ref, got_ref, cot_ref, gotc_ref, w_ref, packed_ref, tokens_ref, normed, cotan):
    half, block, width = tokens_ref.shape
    heads, _, lanes = packed_ref.shape
    size = width // heads
    rows = block // 2
    step = pl.program_id(0)
    core = core_ref[0]

    @pl.when(step == 0)
    def _():
        mine = pl.ds(pl.multiple_of(core * rows, rows), rows)
        other = pl.ds(pl.multiple_of((1 - core) * rows, rows), rows)
        for u in range(half):
            for src, far, dst in ((single_ref, got_ref, tokens_ref), (cot_ref, gotc_ref, cotan)):
                dst[u, mine, :] = src[core * half + u]
                dst[u, other, :] = far[core * half + u]
        normed[...] = unit(tokens_ref[...].reshape(lanes, width).astype(F32))[0].astype(BF)
        turned = cotan[...].reshape(lanes, width).astype(F32).T.astype(BF)
        for h in range(heads):
            packed_ref[h, 3 * size : 4 * size, :] = turned[h * size : (h + 1) * size]

    cols = w_ref.shape[1]
    out = jnp.dot(normed[...], w_ref[...], preferred_element_type=F32).T.astype(BF)
    for p in range(3):
        @pl.when(step // 2 == p)
        def _():
            base = (step % 2) * (cols // size)
            for h in range(cols // size):
                packed_ref[base + h, p * size : (p + 1) * size, :] = out[h * size : (h + 1) * size]

def project(core, single, got, cot, gotc, w_qkv, heads):
    samp, rows, width = single.shape
    half, block = samp // 2, 2 * rows
    lanes = half * block
    size = width // heads
    whole = pl.BlockSpec((samp, rows, width), lambda i, c: (0, 0, 0))
    return pl.pallas_call(
        project_kernel,
        grid_spec=pltpu.PrefetchScalarGridSpec(
            num_scalar_prefetch=1, grid=(6,),
            in_specs=[whole] * 4 + [pl.BlockSpec((width, width // 2), lambda i, c: (0, i))],
            out_specs=[pl.BlockSpec((heads, 4 * size, lanes), lambda i, c: (0, 0, 0)),
                       pl.BlockSpec((half, block, width), lambda i, c: (0, 0, 0))],
            scratch_shapes=[pltpu.VMEM((lanes, width), BF), pltpu.VMEM((half, block, width), BF)],
        ),
        out_shape=[jax.ShapeDtypeStruct((heads, 4 * size, lanes), BF), jax.ShapeDtypeStruct((half, block, width), BF)],
        compiler_params=pltpu.CompilerParams(dimension_semantics=("arbitrary",), vmem_limit_bytes=60 << 20),
    )(core, single, got, cot, gotc, w_qkv)

def transition_kernel(core_ref, tokens_ref, att_ref, wo_ref, wg_ref, wu_ref, wd_ref, mine_ref, theirs_ref, mid, normed, done):
    half, block, width = tokens_ref.shape
    rows = block // 2
    step = pl.program_id(0)

    @pl.when(step == 0)
    def _():
        attended = att_ref[...].astype(F32).T.astype(BF)
        flat = tokens_ref[...].reshape(half * block, width).astype(F32)
        flat = flat + jnp.dot(attended, wo_ref[...], preferred_element_type=F32)
        mid[...] = flat
        normed[...] = unit(flat)[0].astype(BF)

    gate = jnp.dot(normed[...], wg_ref[...], preferred_element_type=F32)
    up = jnp.dot(normed[...], wu_ref[...], preferred_element_type=F32)
    hidden = (jax.nn.silu(gate) * up).astype(BF)
    mid[...] += jnp.dot(hidden, wd_ref[...], preferred_element_type=F32)

    @pl.when(step == pl.num_programs(0) - 1)
    def _():
        done[...] = mid[...].astype(BF).reshape(half, block, width)
        core = core_ref[0]
        mine = pl.ds(pl.multiple_of(core * rows, rows), rows)
        other = pl.ds(pl.multiple_of((1 - core) * rows, rows), rows)
        for u in range(half):
            mine_ref[u] = done[u, mine, :]
            theirs_ref[u] = done[u, other, :]

def transition(core, tokens, attended_t, w_out, w_gate_up, w_down, steps=4):
    half, block, width = tokens.shape
    lanes = half * block
    inner = w_down.shape[0]
    part = inner // steps
    out = pl.BlockSpec((half, block // 2, width), lambda i, c: (0, 0, 0))
    return pl.pallas_call(
        transition_kernel,
        grid_spec=pltpu.PrefetchScalarGridSpec(
            num_scalar_prefetch=1, grid=(steps,),
            in_specs=[pl.BlockSpec((half, block, width), lambda i, c: (0, 0, 0)),
                      pl.BlockSpec((width, lanes), lambda i, c: (0, 0)),
                      pl.BlockSpec((width, width), lambda i, c: (0, 0)),
                      pl.BlockSpec((width, part), lambda i, c: (0, i)),
                      pl.BlockSpec((width, part), lambda i, c: (0, i + steps)),
                      pl.BlockSpec((part, width), lambda i, c: (i, 0))],
            out_specs=[out, out],
            scratch_shapes=[pltpu.VMEM((lanes, width), F32), pltpu.VMEM((lanes, width), BF),
                            pltpu.VMEM((half, block, width), BF)],
        ),
        out_shape=[jax.ShapeDtypeStruct((half, block // 2, width), BF)] * 2,
        compiler_params=pltpu.CompilerParams(dimension_semantics=("arbitrary",), vmem_limit_bytes=60 << 20),
    )(core, tokens, attended_t, w_out, w_gate_up, w_gate_up, w_down)

def split(v):
    high = v.astype(BF).astype(F32)
    return high, v - high

def attend_kernel(n_col, n_chip, per, size, c_ref, blk_ref, *refs):
    bias_refs = refs[: n_col // 2]
    att_ref = refs[n_col // 2]
    out_refs = refs[n_col // 2 + 1 : n_col + 1]
    bias2, acc, kt, vt = refs[n_col + 1 :]
    step = pl.program_id(0)
    me = c_ref[0]
    side = me // (n_col // 2)
    block = blk_ref.shape[3]
    wide = block * n_col
    rest = block - 2 * size

    @pl.when(step == 0)
    def _():
        for k in range(n_col):
            far = jnp.bitwise_xor(side, k // (n_col // 2))
            part = bias_refs[k % (n_col // 2)][:, far]
            part = part.astype(F32).reshape(bias2.shape[0], block)
            bias2[:, k * block : (k + 1) * block] = part * LOG2E
        row = lax.broadcasted_iota(jnp.int32, (rest, wide), 0)
        for h in range(2):
            kt[h, 2 * size :, :] = jnp.zeros((rest, wide), BF)
            vt[h, 2 * size :, :] = jnp.where(row < 3, 1.0, 0.0).astype(BF)

    scale = LOG2E / math.sqrt(size)
    row = lax.broadcasted_iota(jnp.int32, (rest, block), 0)

    def prepare(h):
        for k in range(n_col):
            owner = jnp.bitwise_xor(me, k)
            cols = slice(k * block, (k + 1) * block)
            keys = blk_ref[owner, h, size : 2 * size, :]
            kt[h, :size, cols] = keys
            kt[h, size : 2 * size, cols] = keys
            vals = blk_ref[owner, h, 2 * size : 3 * size, :]
            vt[h, :size, cols] = vals
            vt[h, size : 2 * size, cols] = vals
        lhs = []
        for b in range(n_chip):
            high, low = split(blk_ref[b, h, :size, :].astype(F32) * scale)
            lhs.append(jnp.concatenate([high, low, jnp.zeros((rest, block), F32)], axis=0).T.astype(BF))
        return jnp.concatenate(lhs, axis=0)

    def softmax(h, lhs):
        scores = jnp.dot(lhs, kt[h], preferred_element_type=F32) + bias2[...]
        top = jnp.max(scores, axis=1, keepdims=True)
        return jnp.exp2(scores - top)

    def mix(h, probs):
        mixed = lax.dot_general(
            probs.astype(BF), vt[h], (((1,), (1,)), ((), ())), preferred_element_type=F32
        )
        lhs = []
        for b in range(n_chip):
            mixed_t = mixed[b * block : (b + 1) * block].T
            inv = 1.0 / mixed_t[2 * size : 2 * size + 1]
            att = mixed_t[:size] * inv
            att_ref[b, h, :, :] = att.astype(BF)
            cotan = blk_ref[b, h, 3 * size :, :].astype(F32)
            delta = -jnp.sum(cotan * att, axis=0, keepdims=True) * inv
            high, low = split(cotan * inv)
            d0, rem = split(delta)
            d1, d2 = split(rem)
            tail = jnp.where(row == 0, d0, jnp.where(row == 1, d1, jnp.where(row == 2, d2, 0.0)))
            lhs.append(jnp.concatenate([high, low, tail], axis=0).T.astype(BF))
        return jnp.concatenate(lhs, axis=0)

    def grad(h, probs, lhs):
        return probs * jnp.dot(lhs, vt[h], preferred_element_type=F32)

    lhs = [prepare(h) for h in range(2)]
    probs = [softmax(h, lhs[h]) for h in range(2)]
    lhs = [mix(h, probs[h]) for h in range(2)]
    term = grad(0, probs[0], lhs[0]) + grad(1, probs[1], lhs[1])

    @pl.when(step == 0)
    def _():
        acc[...] = term

    @pl.when(step > 0)
    def _():
        acc[...] += term

    @pl.when(step == per - 1)
    def _():
        for k in range(n_col):
            part = acc[:, k * block : (k + 1) * block].astype(BF)
            out_ref = out_refs[k % (n_col // 2)]
            far = jnp.bitwise_xor(side, k // (n_col // 2))
            out_ref[:, far] = part.reshape(out_ref.shape[0], out_ref.shape[2], block)


def attend(me, qkvc, biases, n_samp, size, limit=56):
    n_chip, _, _, lanes = qkvc.shape
    per = n_samp // 2
    block = lanes // per
    n_col = 2 * len(biases)
    tokens = n_chip * block
    wide = n_col * block
    parts = biases[0].shape
    whole = pl.BlockSpec(parts, lambda s, c: (0, 0, 0, 0))
    spec = lambda feats: pl.BlockSpec((n_chip, 2, feats, block), lambda s, c: (0, 0, 0, s))
    return pl.pallas_call(
        functools.partial(attend_kernel, n_col, n_chip, per, size),
        grid_spec=pltpu.PrefetchScalarGridSpec(
            num_scalar_prefetch=1,
            grid=(per,),
            in_specs=[spec(4 * size)] + [whole] * len(biases),
            out_specs=[spec(size)] + [whole] * len(biases),
            scratch_shapes=[
                pltpu.VMEM((tokens, wide), F32),
                pltpu.VMEM((tokens, wide), F32),
                pltpu.VMEM((2, block, wide), BF),
                pltpu.VMEM((2, block, wide), BF),
            ],
        ),
        out_shape=[jax.ShapeDtypeStruct((n_chip, 2, size, lanes), BF)]
        + [jax.ShapeDtypeStruct(parts, BF)] * len(biases),
        compiler_params=pltpu.CompilerParams(
            dimension_semantics=("arbitrary",), vmem_limit_bytes=limit * 1024 * 1024
        ),
    )(me, qkvc, *biases)


def shards(n_row, n_col, pair, bias_weight, single, w_qkv, w_out, w_gate_up, w_down, cotangent):
    samp, rows, width = single.shape
    heads = bias_weight.shape[1]
    size = width // heads
    half = samp // 2
    block = 2 * rows
    n_chip = n_row // 2
    core = lax.rem(lax.axis_index("row"), 2).astype(jnp.int32)
    me = lax.axis_index("col").astype(jnp.int32).reshape(1)
    cores = [(i, i ^ 1) for i in range(n_row)]
    flip = lambda k: [(i, i ^ k) for i in range(n_col)]

    got = lax.ppermute(single, "row", cores)
    got_cot = lax.ppermute(cotangent, "row", cores)
    groups = [[r * n_col + z * (n_col // 2) + y for r in range(n_row) for z in range(2)] for y in range(n_col // 2)]
    share = lambda v: lax.all_to_all(
        v.reshape(2 * n_row, rows, pair.shape[1]), ("row", "col"), 0, 0, tiled=True, axis_index_groups=groups
    ).reshape(n_row, 2, rows, pair.shape[1])
    bias = share(pair_bias(pair, bias_weight, 32))
    packed, tokens = project(core.reshape(1), single, got, cotangent, got_cot, w_qkv, heads)
    biases = [bias] + [lax.ppermute(bias, "col", flip(k)) for k in range(1, n_col // 2)]

    later, _ = lax.optimization_barrier((pair, bias))
    stats = pair_stats(later, 16)
    packed = lax.all_to_all(packed, "row", 0, 0, tiled=True)
    packed, stats = lax.optimization_barrier((packed, stats))
    packed = packed.reshape(n_chip, 2, 4 * size, half * block)
    attended, *grads = attend(me, packed, biases, samp, size)
    grads = [grads[0]] + [lax.ppermute(grads[k], "col", flip(k)) for k in range(1, n_col // 2)]
    attended = attended.reshape(n_row, size, half * block)
    attended = lax.all_to_all(attended, "row", 0, 0, tiled=True)
    total = grads[0].astype(F32)
    for part in grads[1:]:
        total = total + part.astype(F32)
    attended, total = lax.optimization_barrier((attended, total.astype(BF)))
    total = share(total)
    mine, theirs = transition(
        core.reshape(1), tokens, attended.reshape(width, half * block), w_out, w_gate_up, w_down
    )
    mine, theirs, total = lax.optimization_barrier((mine, theirs, total))
    got = lax.ppermute(theirs, "row", cores)
    updated = jnp.concatenate([jnp.where(core == 0, mine, got), jnp.where(core == 0, got, mine)], axis=0)
    pair_grad = pair_back(stats, total, bias_weight, 32)
    return (updated, pair_grad)


def solution(mesh):
    sizes = dict(mesh.shape)
    return jax.shard_map(
        functools.partial(shards, sizes["row"], sizes["col"]),
        mesh=mesh,
        in_specs=(
            P("row", "col", None),
            P(),
            P("col", "row", None),
            P(),
            P(),
            P(),
            P(),
            P("col", "row", None),
        ),
        out_specs=(P("col", "row", None), P("row", "col", None)),
        check_vma=False,
    )
```

```python
import functools
import math

import jax
import jax.numpy as jnp
from jax import lax
from jax.experimental import pallas as pl
from jax.experimental.pallas import tpu as pltpu
from jax.sharding import PartitionSpec as P

BF = jnp.bfloat16
F32 = jnp.float32
LOG2E = 1.4426950408889634

def unit(values):
    mean_val = jnp.mean(values, axis=-1, keepdims=True)
    centred = values - mean_val
    variance = jnp.mean(centred * centred, axis=-1, keepdims=True)
    scaled = lax.rsqrt(variance + 1e-05)
    return centred * scaled, scaled

def halves(v):
    high = v.astype(BF)
    return high, (v - high.astype(F32)).astype(BF)

def across(lhs, rhs):
    return lax.dot_general(lhs, rhs, (((1,), (1,)), ((), ())), preferred_element_type=F32)

def pair_kernel(pair_ref, w_ref, out_ref):
    rows, cols, chans = pair_ref.shape
    heads = w_ref.shape[0]
    values = pair_ref[...].astype(F32).reshape(rows * cols, chans)
    centred = values - jnp.mean(values, axis=-1, keepdims=True)
    weight = w_ref[...]
    flat = across(jnp.concatenate([weight, weight], axis=1), jnp.concatenate(halves(centred), axis=1))
    ones = jnp.full((8, chans), 1.0 / chans, BF)
    variance = across(ones, (centred * centred).astype(BF))[:1]
    flat = (flat * lax.rsqrt(variance + 1e-05)).reshape(heads, rows, cols).astype(BF)
    out_ref[:, 0] = flat
    out_ref[:, 1] = flat

def pair_bias(pair, bias_weight, step=16):
    rows, cols, chans = pair.shape
    heads = bias_weight.shape[1]
    return pl.pallas_call(
        pair_kernel, grid=(rows // step,),
        in_specs=[pl.BlockSpec((step, cols, chans), lambda i: (i, 0, 0)),
                  pl.BlockSpec((heads, chans), lambda i: (0, 0))],
        out_specs=pl.BlockSpec((heads, 2, step, cols), lambda i: (0, 0, i, 0)),
        out_shape=jax.ShapeDtypeStruct((heads, 2, rows, cols), BF),
        compiler_params=pltpu.CompilerParams(dimension_semantics=("arbitrary",), vmem_limit_bytes=60 << 20),
    )(pair, bias_weight.T)

def stats_kernel(pair_ref, normed_ref, scaled_ref):
    rows, cols, chans = pair_ref.shape
    normed, scaled = unit(pair_ref[...].astype(F32).reshape(rows * cols, chans))
    normed_ref[...] = normed.reshape(rows, cols, chans)
    lanes = jnp.broadcast_to(scaled, (rows * cols, chans)).reshape(rows, cols, chans)
    for i in range(rows):
        scaled_ref[i : i + 1] = lanes[i].T[:1]

def pair_stats(pair, step=16):
    rows, cols, chans = pair.shape
    return pl.pallas_call(
        stats_kernel, grid=(rows // step,),
        in_specs=[pl.BlockSpec((step, cols, chans), lambda i: (i, 0, 0))],
        out_specs=[pl.BlockSpec((step, cols, chans), lambda i: (i, 0, 0)), pl.BlockSpec((step, cols), lambda i: (i, 0))],
        out_shape=[jax.ShapeDtypeStruct((rows, cols, chans), F32), jax.ShapeDtypeStruct((rows, cols), F32)],
        compiler_params=pltpu.CompilerParams(dimension_semantics=("arbitrary",), vmem_limit_bytes=60 << 20),
    )(pair)

def back_kernel(normed_ref, scaled_ref, grad_ref, w_ref, out_ref):
    rows, cols, chans = normed_ref.shape
    heads, parts = grad_ref.shape[:2]
    grad = grad_ref[:, 0].astype(F32)
    for g in range(1, parts):
        grad = grad + grad_ref[:, g].astype(F32)
    grad = (grad * scaled_ref[...][None]).reshape(heads, rows * cols)
    high, low = halves(grad)
    weight = w_ref[...].astype(F32)
    w_high, w_low = halves(weight - jnp.mean(weight, axis=1, keepdims=True))
    both = jnp.concatenate([high, low, high, low], axis=0)
    weight = jnp.concatenate([w_high, w_high, w_low, w_low], axis=0)
    centred = lax.dot_general(both, weight, (((0,), (0,)), ((), ())), preferred_element_type=F32)
    normed = normed_ref[...].reshape(rows * cols, chans)
    along = jnp.mean(centred * normed, axis=-1, keepdims=True)
    out_ref[...] = (centred - normed * along).reshape(rows, cols, chans)

def pair_back(stats, grad, bias_weight, step=16):
    normed, scaled = stats
    rows, cols, chans = normed.shape
    heads, parts = grad.shape[:2]
    return pl.pallas_call(
        back_kernel, grid=(rows // step,),
        in_specs=[pl.BlockSpec((step, cols, chans), lambda i: (i, 0, 0)),
                  pl.BlockSpec((step, cols), lambda i: (i, 0)),
                  pl.BlockSpec((heads, parts, step, cols), lambda i: (0, 0, i, 0)),
                  pl.BlockSpec((heads, chans), lambda i: (0, 0))],
        out_specs=pl.BlockSpec((step, cols, chans), lambda i: (i, 0, 0)),
        out_shape=jax.ShapeDtypeStruct((rows, cols, chans), F32),
        compiler_params=pltpu.CompilerParams(dimension_semantics=("arbitrary",), vmem_limit_bytes=60 << 20),
    )(normed, scaled, grad, bias_weight.T)

def project_kernel(core_ref, single_ref, got_ref, cot_ref, gotc_ref, w_ref, packed_ref, tokens_ref, normed, cotan):
    half, block, width = tokens_ref.shape
    heads, _, lanes = packed_ref.shape
    size = width // heads
    rows = block // 2
    step = pl.program_id(0)
    core = core_ref[0]

    @pl.when(step == 0)
    def _():
        mine = pl.ds(pl.multiple_of(core * rows, rows), rows)
        other = pl.ds(pl.multiple_of((1 - core) * rows, rows), rows)
        for u in range(half):
            for src, far, dst in ((single_ref, got_ref, tokens_ref), (cot_ref, gotc_ref, cotan)):
                dst[u, mine, :] = src[core * half + u]
                dst[u, other, :] = far[core * half + u]
        normed[...] = unit(tokens_ref[...].reshape(lanes, width).astype(F32))[0].astype(BF)
        turned = cotan[...].reshape(lanes, width).astype(F32).T.astype(BF)
        for h in range(heads):
            packed_ref[h, 3 * size : 4 * size, :] = turned[h * size : (h + 1) * size]

    cols = w_ref.shape[1]
    out = jnp.dot(normed[...], w_ref[...], preferred_element_type=F32).T.astype(BF)
    for p in range(3):
        @pl.when(step // 2 == p)
        def _():
            base = (step % 2) * (cols // size)
            for h in range(cols // size):
                packed_ref[base + h, p * size : (p + 1) * size, :] = out[h * size : (h + 1) * size]

def project(core, single, got, cot, gotc, w_qkv, heads):
    samp, rows, width = single.shape
    half, block = samp // 2, 2 * rows
    lanes = half * block
    size = width // heads
    whole = pl.BlockSpec((samp, rows, width), lambda i, c: (0, 0, 0))
    return pl.pallas_call(
        project_kernel,
        grid_spec=pltpu.PrefetchScalarGridSpec(
            num_scalar_prefetch=1, grid=(6,),
            in_specs=[whole] * 4 + [pl.BlockSpec((width, width // 2), lambda i, c: (0, i))],
            out_specs=[pl.BlockSpec((heads, 4 * size, lanes), lambda i, c: (0, 0, 0)),
                       pl.BlockSpec((half, block, width), lambda i, c: (0, 0, 0))],
            scratch_shapes=[pltpu.VMEM((lanes, width), BF), pltpu.VMEM((half, block, width), BF)],
        ),
        out_shape=[jax.ShapeDtypeStruct((heads, 4 * size, lanes), BF), jax.ShapeDtypeStruct((half, block, width), BF)],
        compiler_params=pltpu.CompilerParams(dimension_semantics=("arbitrary",), vmem_limit_bytes=60 << 20),
    )(core, single, got, cot, gotc, w_qkv)

def transition_kernel(core_ref, tokens_ref, att_ref, wo_ref, wg_ref, wu_ref, wd_ref, mine_ref, theirs_ref, mid, normed, done):
    half, block, width = tokens_ref.shape
    rows = block // 2
    step = pl.program_id(0)

    @pl.when(step == 0)
    def _():
        attended = att_ref[...].astype(F32).T.astype(BF)
        flat = tokens_ref[...].reshape(half * block, width).astype(F32)
        flat = flat + jnp.dot(attended, wo_ref[...], preferred_element_type=F32)
        mid[...] = flat
        normed[...] = unit(flat)[0].astype(BF)

    gate = jnp.dot(normed[...], wg_ref[...], preferred_element_type=F32)
    up = jnp.dot(normed[...], wu_ref[...], preferred_element_type=F32)
    hidden = (jax.nn.silu(gate) * up).astype(BF)
    mid[...] += jnp.dot(hidden, wd_ref[...], preferred_element_type=F32)

    @pl.when(step == pl.num_programs(0) - 1)
    def _():
        done[...] = mid[...].astype(BF).reshape(half, block, width)
        core = core_ref[0]
        mine = pl.ds(pl.multiple_of(core * rows, rows), rows)
        other = pl.ds(pl.multiple_of((1 - core) * rows, rows), rows)
        for u in range(half):
            mine_ref[u] = done[u, mine, :]
            theirs_ref[u] = done[u, other, :]

def transition(core, tokens, attended_t, w_out, w_gate_up, w_down, steps=4):
    half, block, width = tokens.shape
    lanes = half * block
    inner = w_down.shape[0]
    part = inner // steps
    out = pl.BlockSpec((half, block // 2, width), lambda i, c: (0, 0, 0))
    return pl.pallas_call(
        transition_kernel,
        grid_spec=pltpu.PrefetchScalarGridSpec(
            num_scalar_prefetch=1, grid=(steps,),
            in_specs=[pl.BlockSpec((half, block, width), lambda i, c: (0, 0, 0)),
                      pl.BlockSpec((width, lanes), lambda i, c: (0, 0)),
                      pl.BlockSpec((width, width), lambda i, c: (0, 0)),
                      pl.BlockSpec((width, part), lambda i, c: (0, i)),
                      pl.BlockSpec((width, part), lambda i, c: (0, i + steps)),
                      pl.BlockSpec((part, width), lambda i, c: (i, 0))],
            out_specs=[out, out],
            scratch_shapes=[pltpu.VMEM((lanes, width), F32), pltpu.VMEM((lanes, width), BF),
                            pltpu.VMEM((half, block, width), BF)],
        ),
        out_shape=[jax.ShapeDtypeStruct((half, block // 2, width), BF)] * 2,
        compiler_params=pltpu.CompilerParams(dimension_semantics=("arbitrary",), vmem_limit_bytes=60 << 20),
    )(core, tokens, attended_t, w_out, w_gate_up, w_gate_up, w_down)

def split(v):
    high = v.astype(BF).astype(F32)
    return high, v - high

def attend_kernel(n_col, n_chip, per, size, c_ref, blk_ref, *refs):
    bias_refs = refs[: n_col // 2]
    att_ref = refs[n_col // 2]
    out_refs = refs[n_col // 2 + 1 : n_col + 1]
    bias2, acc, kt, vt = refs[n_col + 1 :]
    step = pl.program_id(0)
    me = c_ref[0]
    side = me // (n_col // 2)
    block = blk_ref.shape[3]
    wide = block * n_col
    rest = block - 2 * size

    @pl.when(step == 0)
    def _():
        for k in range(n_col):
            far = jnp.bitwise_xor(side, k // (n_col // 2))
            part = bias_refs[k % (n_col // 2)][:, far]
            part = part.astype(F32).reshape(bias2.shape[0], block)
            bias2[:, k * block : (k + 1) * block] = part * LOG2E
        row = lax.broadcasted_iota(jnp.int32, (rest, wide), 0)
        for h in range(2):
            kt[h, 2 * size :, :] = jnp.zeros((rest, wide), BF)
            vt[h, 2 * size :, :] = jnp.where(row < 3, 1.0, 0.0).astype(BF)

    scale = LOG2E / math.sqrt(size)
    row = lax.broadcasted_iota(jnp.int32, (rest, block), 0)

    def prepare(h):
        for k in range(n_col):
            owner = jnp.bitwise_xor(me, k)
            cols = slice(k * block, (k + 1) * block)
            keys = blk_ref[owner, h, size : 2 * size, :]
            kt[h, :size, cols] = keys
            kt[h, size : 2 * size, cols] = keys
            vals = blk_ref[owner, h, 2 * size : 3 * size, :]
            vt[h, :size, cols] = vals
            vt[h, size : 2 * size, cols] = vals
        lhs = []
        for b in range(n_chip):
            high, low = split(blk_ref[b, h, :size, :].astype(F32) * scale)
            lhs.append(jnp.concatenate([high, low, jnp.zeros((rest, block), F32)], axis=0).T.astype(BF))
        return jnp.concatenate(lhs, axis=0)

    def softmax(h, lhs):
        scores = jnp.dot(lhs, kt[h], preferred_element_type=F32) + bias2[...]
        top = jnp.max(scores, axis=1, keepdims=True)
        return jnp.exp2(scores - top)

    def mix(h, probs):
        mixed = lax.dot_general(
            probs.astype(BF), vt[h], (((1,), (1,)), ((), ())), preferred_element_type=F32
        )
        lhs = []
        for b in range(n_chip):
            mixed_t = mixed[b * block : (b + 1) * block].T
            inv = 1.0 / mixed_t[2 * size : 2 * size + 1]
            att = mixed_t[:size] * inv
            att_ref[b, h, :, :] = att.astype(BF)
            cotan = blk_ref[b, h, 3 * size :, :].astype(F32)
            delta = -jnp.sum(cotan * att, axis=0, keepdims=True) * inv
            high, low = split(cotan * inv)
            d0, rem = split(delta)
            d1, d2 = split(rem)
            tail = jnp.where(row == 0, d0, jnp.where(row == 1, d1, jnp.where(row == 2, d2, 0.0)))
            lhs.append(jnp.concatenate([high, low, tail], axis=0).T.astype(BF))
        return jnp.concatenate(lhs, axis=0)

    def grad(h, probs, lhs):
        return probs * jnp.dot(lhs, vt[h], preferred_element_type=F32)

    lhs = [prepare(h) for h in range(2)]
    probs = [softmax(h, lhs[h]) for h in range(2)]
    lhs = [mix(h, probs[h]) for h in range(2)]
    term = grad(0, probs[0], lhs[0]) + grad(1, probs[1], lhs[1])

    @pl.when(step == 0)
    def _():
        acc[...] = term

    @pl.when(step > 0)
    def _():
        acc[...] += term

    @pl.when(step == per - 1)
    def _():
        for k in range(n_col):
            part = acc[:, k * block : (k + 1) * block].astype(BF)
            out_ref = out_refs[k % (n_col // 2)]
            far = jnp.bitwise_xor(side, k // (n_col // 2))
            out_ref[:, far] = part.reshape(out_ref.shape[0], out_ref.shape[2], block)


def attend(me, qkvc, biases, n_samp, size, limit=48):
    n_chip, _, _, lanes = qkvc.shape
    per = n_samp // 2
    block = lanes // per
    n_col = 2 * len(biases)
    tokens = n_chip * block
    wide = n_col * block
    parts = biases[0].shape
    whole = pl.BlockSpec(parts, lambda s, c: (0, 0, 0, 0))
    spec = lambda feats: pl.BlockSpec((n_chip, 2, feats, block), lambda s, c: (0, 0, 0, s))
    return pl.pallas_call(
        functools.partial(attend_kernel, n_col, n_chip, per, size),
        grid_spec=pltpu.PrefetchScalarGridSpec(
            num_scalar_prefetch=1,
            grid=(per,),
            in_specs=[spec(4 * size)] + [whole] * len(biases),
            out_specs=[spec(size)] + [whole] * len(biases),
            scratch_shapes=[
                pltpu.VMEM((tokens, wide), F32),
                pltpu.VMEM((tokens, wide), F32),
                pltpu.VMEM((2, block, wide), BF),
                pltpu.VMEM((2, block, wide), BF),
            ],
        ),
        out_shape=[jax.ShapeDtypeStruct((n_chip, 2, size, lanes), BF)]
        + [jax.ShapeDtypeStruct(parts, BF)] * len(biases),
        compiler_params=pltpu.CompilerParams(
            dimension_semantics=("arbitrary",), vmem_limit_bytes=limit * 1024 * 1024
        ),
    )(me, qkvc, *biases)


def shards(n_row, n_col, pair, bias_weight, single, w_qkv, w_out, w_gate_up, w_down, cotangent):
    samp, rows, width = single.shape
    heads = bias_weight.shape[1]
    size = width // heads
    half = samp // 2
    block = 2 * rows
    n_chip = n_row // 2
    core = lax.rem(lax.axis_index("row"), 2).astype(jnp.int32)
    me = lax.axis_index("col").astype(jnp.int32).reshape(1)
    cores = [(i, i ^ 1) for i in range(n_row)]
    flip = lambda k: [(i, i ^ k) for i in range(n_col)]

    got = lax.ppermute(single, "row", cores)
    got_cot = lax.ppermute(cotangent, "row", cores)
    groups = [[r * n_col + z * (n_col // 2) + y for r in range(n_row) for z in range(2)] for y in range(n_col // 2)]
    share = lambda v: lax.all_to_all(
        v.reshape(2 * n_row, rows, pair.shape[1]), ("row", "col"), 0, 0, tiled=True, axis_index_groups=groups
    ).reshape(n_row, 2, rows, pair.shape[1])
    bias = share(pair_bias(pair, bias_weight, 32))
    packed, tokens = project(core.reshape(1), single, got, cotangent, got_cot, w_qkv, heads)
    biases = [bias] + [lax.ppermute(bias, "col", flip(k)) for k in range(1, n_col // 2)]

    later, _ = lax.optimization_barrier((pair, bias))
    stats = pair_stats(later, 16)
    packed = lax.all_to_all(packed, "row", 0, 0, tiled=True)
    packed, stats = lax.optimization_barrier((packed, stats))
    packed = packed.reshape(n_chip, 2, 4 * size, half * block)
    attended, *grads = attend(me, packed, biases, samp, size)
    grads = [grads[0]] + [lax.ppermute(grads[k], "col", flip(k)) for k in range(1, n_col // 2)]
    attended = attended.reshape(n_row, size, half * block)
    attended = lax.all_to_all(attended, "row", 0, 0, tiled=True)
    total = grads[0].astype(F32)
    for part in grads[1:]:
        total = total + part.astype(F32)
    attended, total = lax.optimization_barrier((attended, total.astype(BF)))
    total = share(total)
    mine, theirs = transition(
        core.reshape(1), tokens, attended.reshape(width, half * block), w_out, w_gate_up, w_down
    )
    mine, theirs, total = lax.optimization_barrier((mine, theirs, total))
    got = lax.ppermute(theirs, "row", cores)
    updated = jnp.concatenate([jnp.where(core == 0, mine, got), jnp.where(core == 0, got, mine)], axis=0)
    pair_grad = pair_back(stats, total, bias_weight, 32)
    return (updated, pair_grad)


def solution(mesh):
    sizes = dict(mesh.shape)
    return jax.shard_map(
        functools.partial(shards, sizes["row"], sizes["col"]),
        mesh=mesh,
        in_specs=(
            P("row", "col", None),
            P(),
            P("col", "row", None),
            P(),
            P(),
            P(),
            P(),
            P("col", "row", None),
        ),
        out_specs=(P("col", "row", None), P("row", "col", None)),
        check_vma=False,
    )
```

```python
import functools
import math

import jax
import jax.numpy as jnp
from jax import lax
from jax.experimental import pallas as pl
from jax.experimental.pallas import tpu as pltpu
from jax.sharding import PartitionSpec as P

BF = jnp.bfloat16
F32 = jnp.float32
LOG2E = 1.4426950408889634

def unit(values):
    mean_val = jnp.mean(values, axis=-1, keepdims=True)
    centred = values - mean_val
    variance = jnp.mean(centred * centred, axis=-1, keepdims=True)
    scaled = lax.rsqrt(variance + 1e-05)
    return centred * scaled, scaled

def halves(v):
    high = v.astype(BF)
    return high, (v - high.astype(F32)).astype(BF)

def across(lhs, rhs):
    return lax.dot_general(lhs, rhs, (((1,), (1,)), ((), ())), preferred_element_type=F32)

def pair_kernel(pair_ref, w_ref, out_ref):
    rows, cols, chans = pair_ref.shape
    heads = w_ref.shape[0]
    values = pair_ref[...].astype(F32).reshape(rows * cols, chans)
    centred = values - jnp.mean(values, axis=-1, keepdims=True)
    weight = w_ref[...]
    flat = across(jnp.concatenate([weight, weight], axis=1), jnp.concatenate(halves(centred), axis=1))
    ones = jnp.full((8, chans), 1.0 / chans, BF)
    variance = across(ones, (centred * centred).astype(BF))[:1]
    flat = (flat * lax.rsqrt(variance + 1e-05)).reshape(heads, rows, cols).astype(BF)
    out_ref[:, 0] = flat
    out_ref[:, 1] = flat

def pair_bias(pair, bias_weight, step=16):
    rows, cols, chans = pair.shape
    heads = bias_weight.shape[1]
    return pl.pallas_call(
        pair_kernel, grid=(rows // step,),
        in_specs=[pl.BlockSpec((step, cols, chans), lambda i: (i, 0, 0)),
                  pl.BlockSpec((heads, chans), lambda i: (0, 0))],
        out_specs=pl.BlockSpec((heads, 2, step, cols), lambda i: (0, 0, i, 0)),
        out_shape=jax.ShapeDtypeStruct((heads, 2, rows, cols), BF),
        compiler_params=pltpu.CompilerParams(dimension_semantics=("arbitrary",), vmem_limit_bytes=60 << 20),
    )(pair, bias_weight.T)

def stats_kernel(pair_ref, normed_ref, scaled_ref):
    rows, cols, chans = pair_ref.shape
    normed, scaled = unit(pair_ref[...].astype(F32).reshape(rows * cols, chans))
    normed_ref[...] = normed.reshape(rows, cols, chans)
    lanes = jnp.broadcast_to(scaled, (rows * cols, chans)).reshape(rows, cols, chans)
    for i in range(rows):
        scaled_ref[i : i + 1] = lanes[i].T[:1]

def pair_stats(pair, step=16):
    rows, cols, chans = pair.shape
    return pl.pallas_call(
        stats_kernel, grid=(rows // step,),
        in_specs=[pl.BlockSpec((step, cols, chans), lambda i: (i, 0, 0))],
        out_specs=[pl.BlockSpec((step, cols, chans), lambda i: (i, 0, 0)), pl.BlockSpec((step, cols), lambda i: (i, 0))],
        out_shape=[jax.ShapeDtypeStruct((rows, cols, chans), F32), jax.ShapeDtypeStruct((rows, cols), F32)],
        compiler_params=pltpu.CompilerParams(dimension_semantics=("arbitrary",), vmem_limit_bytes=60 << 20),
    )(pair)

def back_kernel(normed_ref, scaled_ref, grad_ref, w_ref, out_ref):
    rows, cols, chans = normed_ref.shape
    heads, parts = grad_ref.shape[:2]
    grad = grad_ref[:, 0].astype(F32)
    for g in range(1, parts):
        grad = grad + grad_ref[:, g].astype(F32)
    grad = (grad * scaled_ref[...][None]).reshape(heads, rows * cols)
    high, low = halves(grad)
    weight = w_ref[...].astype(F32)
    w_high, w_low = halves(weight - jnp.mean(weight, axis=1, keepdims=True))
    both = jnp.concatenate([high, low, high, low], axis=0)
    weight = jnp.concatenate([w_high, w_high, w_low, w_low], axis=0)
    centred = lax.dot_general(both, weight, (((0,), (0,)), ((), ())), preferred_element_type=F32)
    normed = normed_ref[...].reshape(rows * cols, chans)
    along = jnp.mean(centred * normed, axis=-1, keepdims=True)
    out_ref[...] = (centred - normed * along).reshape(rows, cols, chans)

def pair_back(stats, grad, bias_weight, step=16):
    normed, scaled = stats
    rows, cols, chans = normed.shape
    heads, parts = grad.shape[:2]
    return pl.pallas_call(
        back_kernel, grid=(rows // step,),
        in_specs=[pl.BlockSpec((step, cols, chans), lambda i: (i, 0, 0)),
                  pl.BlockSpec((step, cols), lambda i: (i, 0)),
                  pl.BlockSpec((heads, parts, step, cols), lambda i: (0, 0, i, 0)),
                  pl.BlockSpec((heads, chans), lambda i: (0, 0))],
        out_specs=pl.BlockSpec((step, cols, chans), lambda i: (i, 0, 0)),
        out_shape=jax.ShapeDtypeStruct((rows, cols, chans), F32),
        compiler_params=pltpu.CompilerParams(dimension_semantics=("arbitrary",), vmem_limit_bytes=60 << 20),
    )(normed, scaled, grad, bias_weight.T)

def project_kernel(core_ref, single_ref, got_ref, cot_ref, gotc_ref, w_ref, packed_ref, tokens_ref, normed, cotan):
    half, block, width = tokens_ref.shape
    heads, _, lanes = packed_ref.shape
    size = width // heads
    rows = block // 2
    step = pl.program_id(0)
    core = core_ref[0]

    @pl.when(step == 0)
    def _():
        mine = pl.ds(pl.multiple_of(core * rows, rows), rows)
        other = pl.ds(pl.multiple_of((1 - core) * rows, rows), rows)
        for u in range(half):
            for src, far, dst in ((single_ref, got_ref, tokens_ref), (cot_ref, gotc_ref, cotan)):
                dst[u, mine, :] = src[core * half + u]
                dst[u, other, :] = far[core * half + u]
        normed[...] = unit(tokens_ref[...].reshape(lanes, width).astype(F32))[0].astype(BF)
        turned = cotan[...].reshape(lanes, width).astype(F32).T.astype(BF)
        for h in range(heads):
            packed_ref[h, 3 * size : 4 * size, :] = turned[h * size : (h + 1) * size]

    cols = w_ref.shape[1]
    out = jnp.dot(normed[...], w_ref[...], preferred_element_type=F32).T.astype(BF)
    for p in range(3):
        @pl.when(step // 2 == p)
        def _():
            base = (step % 2) * (cols // size)
            for h in range(cols // size):
                packed_ref[base + h, p * size : (p + 1) * size, :] = out[h * size : (h + 1) * size]

def project(core, single, got, cot, gotc, w_qkv, heads):
    samp, rows, width = single.shape
    half, block = samp // 2, 2 * rows
    lanes = half * block
    size = width // heads
    whole = pl.BlockSpec((samp, rows, width), lambda i, c: (0, 0, 0))
    return pl.pallas_call(
        project_kernel,
        grid_spec=pltpu.PrefetchScalarGridSpec(
            num_scalar_prefetch=1, grid=(6,),
            in_specs=[whole] * 4 + [pl.BlockSpec((width, width // 2), lambda i, c: (0, i))],
            out_specs=[pl.BlockSpec((heads, 4 * size, lanes), lambda i, c: (0, 0, 0)),
                       pl.BlockSpec((half, block, width), lambda i, c: (0, 0, 0))],
            scratch_shapes=[pltpu.VMEM((lanes, width), BF), pltpu.VMEM((half, block, width), BF)],
        ),
        out_shape=[jax.ShapeDtypeStruct((heads, 4 * size, lanes), BF), jax.ShapeDtypeStruct((half, block, width), BF)],
        compiler_params=pltpu.CompilerParams(dimension_semantics=("arbitrary",), vmem_limit_bytes=60 << 20),
    )(core, single, got, cot, gotc, w_qkv)

def transition_kernel(core_ref, tokens_ref, att_ref, wo_ref, wg_ref, wu_ref, wd_ref, mine_ref, theirs_ref, mid, normed, done):
    half, block, width = tokens_ref.shape
    rows = block // 2
    step = pl.program_id(0)

    @pl.when(step == 0)
    def _():
        attended = att_ref[...].astype(F32).T.astype(BF)
        flat = tokens_ref[...].reshape(half * block, width).astype(F32)
        flat = flat + jnp.dot(attended, wo_ref[...], preferred_element_type=F32)
        mid[...] = flat
        normed[...] = unit(flat)[0].astype(BF)

    gate = jnp.dot(normed[...], wg_ref[...], preferred_element_type=F32)
    up = jnp.dot(normed[...], wu_ref[...], preferred_element_type=F32)
    hidden = (jax.nn.silu(gate) * up).astype(BF)
    mid[...] += jnp.dot(hidden, wd_ref[...], preferred_element_type=F32)

    @pl.when(step == pl.num_programs(0) - 1)
    def _():
        done[...] = mid[...].astype(BF).reshape(half, block, width)
        core = core_ref[0]
        mine = pl.ds(pl.multiple_of(core * rows, rows), rows)
        other = pl.ds(pl.multiple_of((1 - core) * rows, rows), rows)
        for u in range(half):
            mine_ref[u] = done[u, mine, :]
            theirs_ref[u] = done[u, other, :]

def transition(core, tokens, attended_t, w_out, w_gate_up, w_down, steps=4):
    half, block, width = tokens.shape
    lanes = half * block
    inner = w_down.shape[0]
    part = inner // steps
    out = pl.BlockSpec((half, block // 2, width), lambda i, c: (0, 0, 0))
    return pl.pallas_call(
        transition_kernel,
        grid_spec=pltpu.PrefetchScalarGridSpec(
            num_scalar_prefetch=1, grid=(steps,),
            in_specs=[pl.BlockSpec((half, block, width), lambda i, c: (0, 0, 0)),
                      pl.BlockSpec((width, lanes), lambda i, c: (0, 0)),
                      pl.BlockSpec((width, width), lambda i, c: (0, 0)),
                      pl.BlockSpec((width, part), lambda i, c: (0, i)),
                      pl.BlockSpec((width, part), lambda i, c: (0, i + steps)),
                      pl.BlockSpec((part, width), lambda i, c: (i, 0))],
            out_specs=[out, out],
            scratch_shapes=[pltpu.VMEM((lanes, width), F32), pltpu.VMEM((lanes, width), BF),
                            pltpu.VMEM((half, block, width), BF)],
        ),
        out_shape=[jax.ShapeDtypeStruct((half, block // 2, width), BF)] * 2,
        compiler_params=pltpu.CompilerParams(dimension_semantics=("arbitrary",), vmem_limit_bytes=60 << 20),
    )(core, tokens, attended_t, w_out, w_gate_up, w_gate_up, w_down)

def split(v):
    high = v.astype(BF).astype(F32)
    return high, v - high

def attend_kernel(n_col, n_chip, per, size, c_ref, blk_ref, *refs):
    bias_refs = refs[: n_col // 2]
    att_ref = refs[n_col // 2]
    out_refs = refs[n_col // 2 + 1 : n_col + 1]
    bias2, acc, kt, vt = refs[n_col + 1 :]
    me = c_ref[0]
    side = me // (n_col // 2)
    block = blk_ref.shape[3] // per
    wide = block * n_col
    rest = block - 2 * size

    for k in range(n_col):
        far = jnp.bitwise_xor(side, k // (n_col // 2))
        part = bias_refs[k % (n_col // 2)][:, far]
        part = part.astype(F32).reshape(bias2.shape[0], block)
        bias2[:, k * block : (k + 1) * block] = part * LOG2E
    row = lax.broadcasted_iota(jnp.int32, (rest, wide), 0)
    for h in range(2 * per):
        kt[h, 2 * size :, :] = jnp.zeros((rest, wide), BF)
        vt[h, 2 * size :, :] = jnp.where(row < 3, 1.0, 0.0).astype(BF)

    scale = LOG2E / math.sqrt(size)
    row = lax.broadcasted_iota(jnp.int32, (rest, block), 0)

    def prepare(u, h):
        for k in range(n_col):
            owner = jnp.bitwise_xor(me, k)
            cols = slice(k * block, (k + 1) * block)
            keys = blk_ref[owner, h, size : 2 * size, u * block : (u + 1) * block]
            kt[2 * u + h, :size, cols] = keys
            kt[2 * u + h, size : 2 * size, cols] = keys
            vals = blk_ref[owner, h, 2 * size : 3 * size, u * block : (u + 1) * block]
            vt[2 * u + h, :size, cols] = vals
            vt[2 * u + h, size : 2 * size, cols] = vals
        lhs = []
        for b in range(n_chip):
            high, low = split(blk_ref[b, h, :size, u * block : (u + 1) * block].astype(F32) * scale)
            lhs.append(jnp.concatenate([high, low, jnp.zeros((rest, block), F32)], axis=0).T.astype(BF))
        return jnp.concatenate(lhs, axis=0)

    def softmax(u, h, lhs):
        scores = jnp.dot(lhs, kt[2 * u + h], preferred_element_type=F32) + bias2[...]
        top = jnp.max(scores, axis=1, keepdims=True)
        return jnp.exp2(scores - top)

    def mix(u, h, probs):
        mixed = lax.dot_general(
            probs.astype(BF), vt[2 * u + h], (((1,), (1,)), ((), ())), preferred_element_type=F32
        )
        lhs = []
        for b in range(n_chip):
            mixed_t = mixed[b * block : (b + 1) * block].T
            inv = 1.0 / mixed_t[2 * size : 2 * size + 1]
            att = mixed_t[:size] * inv
            att_ref[b, h, :, u * block : (u + 1) * block] = att.astype(BF)
            cotan = blk_ref[b, h, 3 * size :, u * block : (u + 1) * block].astype(F32)
            delta = -jnp.sum(cotan * att, axis=0, keepdims=True) * inv
            high, low = split(cotan * inv)
            d0, rem = split(delta)
            d1, d2 = split(rem)
            tail = jnp.where(row == 0, d0, jnp.where(row == 1, d1, jnp.where(row == 2, d2, 0.0)))
            lhs.append(jnp.concatenate([high, low, tail], axis=0).T.astype(BF))
        return jnp.concatenate(lhs, axis=0)

    def grad(u, h, probs, lhs):
        return probs * jnp.dot(lhs, vt[2 * u + h], preferred_element_type=F32)

    for u in range(per):
        lhs = [prepare(u, h) for h in range(2)]
        probs = [softmax(u, h, lhs[h]) for h in range(2)]
        lhs = [mix(u, h, probs[h]) for h in range(2)]
        term = grad(u, 0, probs[0], lhs[0]) + grad(u, 1, probs[1], lhs[1])
        if u == 0:
            acc[...] = term
        elif u < per - 1:
            acc[...] += term
        else:
            term = (acc[...] + term).astype(BF)
            for k in range(n_col):
                part = term[:, k * block : (k + 1) * block]
                out_ref = out_refs[k % (n_col // 2)]
                far = jnp.bitwise_xor(side, k // (n_col // 2))
                out_ref[:, far] = part.reshape(out_ref.shape[0], out_ref.shape[2], block)


def attend(me, qkvc, biases, n_samp, size, limit=48):
    n_chip, _, _, lanes = qkvc.shape
    per = n_samp // 2
    block = lanes // per
    n_col = 2 * len(biases)
    tokens = n_chip * block
    wide = n_col * block
    parts = biases[0].shape
    whole = pl.BlockSpec(parts, lambda s, c: (0, 0, 0, 0))
    spec = lambda feats: pl.BlockSpec((n_chip, 2, feats, lanes), lambda s, c: (0, 0, 0, 0))
    return pl.pallas_call(
        functools.partial(attend_kernel, n_col, n_chip, per, size),
        grid_spec=pltpu.PrefetchScalarGridSpec(
            num_scalar_prefetch=1,
            grid=(1,),
            in_specs=[spec(4 * size)] + [whole] * len(biases),
            out_specs=[spec(size)] + [whole] * len(biases),
            scratch_shapes=[
                pltpu.VMEM((tokens, wide), F32),
                pltpu.VMEM((tokens, wide), F32),
                pltpu.VMEM((n_samp, block, wide), BF),
                pltpu.VMEM((n_samp, block, wide), BF),
            ],
        ),
        out_shape=[jax.ShapeDtypeStruct((n_chip, 2, size, lanes), BF)]
        + [jax.ShapeDtypeStruct(parts, BF)] * len(biases),
        compiler_params=pltpu.CompilerParams(
            dimension_semantics=("arbitrary",), vmem_limit_bytes=limit * 1024 * 1024
        ),
    )(me, qkvc, *biases)


def shards(n_row, n_col, pair, bias_weight, single, w_qkv, w_out, w_gate_up, w_down, cotangent):
    samp, rows, width = single.shape
    heads = bias_weight.shape[1]
    size = width // heads
    half = samp // 2
    block = 2 * rows
    n_chip = n_row // 2
    core = lax.rem(lax.axis_index("row"), 2).astype(jnp.int32)
    me = lax.axis_index("col").astype(jnp.int32).reshape(1)
    cores = [(i, i ^ 1) for i in range(n_row)]
    flip = lambda k: [(i, i ^ k) for i in range(n_col)]

    got = lax.ppermute(single, "row", cores)
    got_cot = lax.ppermute(cotangent, "row", cores)
    groups = [[r * n_col + z * (n_col // 2) + y for r in range(n_row) for z in range(2)] for y in range(n_col // 2)]
    share = lambda v: lax.all_to_all(
        v.reshape(2 * n_row, rows, pair.shape[1]), ("row", "col"), 0, 0, tiled=True, axis_index_groups=groups
    ).reshape(n_row, 2, rows, pair.shape[1])
    bias = share(pair_bias(pair, bias_weight, 32))
    packed, tokens = project(core.reshape(1), single, got, cotangent, got_cot, w_qkv, heads)
    biases = [bias] + [lax.ppermute(bias, "col", flip(k)) for k in range(1, n_col // 2)]

    later, _ = lax.optimization_barrier((pair, bias))
    stats = pair_stats(later, 16)
    packed = lax.all_to_all(packed, "row", 0, 0, tiled=True)
    packed, stats = lax.optimization_barrier((packed, stats))
    packed = packed.reshape(n_chip, 2, 4 * size, half * block)
    attended, *grads = attend(me, packed, biases, samp, size)
    grads = [grads[0]] + [lax.ppermute(grads[k], "col", flip(k)) for k in range(1, n_col // 2)]
    attended = attended.reshape(n_row, size, half * block)
    attended = lax.all_to_all(attended, "row", 0, 0, tiled=True)
    total = grads[0].astype(F32)
    for part in grads[1:]:
        total = total + part.astype(F32)
    attended, total = lax.optimization_barrier((attended, total.astype(BF)))
    total = share(total)
    mine, theirs = transition(
        core.reshape(1), tokens, attended.reshape(width, half * block), w_out, w_gate_up, w_down
    )
    mine, theirs, total = lax.optimization_barrier((mine, theirs, total))
    got = lax.ppermute(theirs, "row", cores)
    updated = jnp.concatenate([jnp.where(core == 0, mine, got), jnp.where(core == 0, got, mine)], axis=0)
    pair_grad = pair_back(stats, total, bias_weight, 32)
    return (updated, pair_grad)


def solution(mesh):
    sizes = dict(mesh.shape)
    return jax.shard_map(
        functools.partial(shards, sizes["row"], sizes["col"]),
        mesh=mesh,
        in_specs=(
            P("row", "col", None),
            P(),
            P("col", "row", None),
            P(),
            P(),
            P(),
            P(),
            P("col", "row", None),
        ),
        out_specs=(P("col", "row", None), P("row", "col", None)),
        check_vma=False,
    )
```

```python
import functools
import math

import jax
import jax.numpy as jnp
from jax import lax
from jax.experimental import pallas as pl
from jax.experimental.pallas import tpu as pltpu
from jax.sharding import PartitionSpec as P

BF = jnp.bfloat16
F32 = jnp.float32
LOG2E = 1.4426950408889634

def unit(values):
    mean_val = jnp.mean(values, axis=-1, keepdims=True)
    centred = values - mean_val
    variance = jnp.mean(centred * centred, axis=-1, keepdims=True)
    scaled = lax.rsqrt(variance + 1e-05)
    return centred * scaled, scaled

def halves(v):
    high = v.astype(BF)
    return high, (v - high.astype(F32)).astype(BF)

def across(lhs, rhs):
    return lax.dot_general(lhs, rhs, (((1,), (1,)), ((), ())), preferred_element_type=F32)

def pair_kernel(pair_ref, w_ref, out_ref):
    rows, cols, chans = pair_ref.shape
    heads = w_ref.shape[0]
    raw = pair_ref[...].reshape(rows * cols, chans)
    values = raw.astype(F32)
    centred = values - jnp.mean(values, axis=-1, keepdims=True)
    weight = w_ref[...].astype(F32)
    weight = weight - jnp.mean(weight, axis=1, keepdims=True)
    w0 = weight.astype(BF)
    w1, w2 = halves(weight - w0.astype(F32))
    flat = across(jnp.concatenate([w0, w1, w2], axis=0), raw)
    flat = flat[:heads] + flat[heads : 2 * heads] + flat[2 * heads :]
    ones = jnp.full((8, chans), 1.0 / chans, BF)
    variance = across(ones, (centred * centred).astype(BF))[:1]
    flat = (flat * lax.rsqrt(variance + 1e-05)).reshape(heads, rows, cols).astype(BF)
    out_ref[:, 0] = flat
    out_ref[:, 1] = flat

def pair_bias(pair, bias_weight, step=16):
    rows, cols, chans = pair.shape
    heads = bias_weight.shape[1]
    return pl.pallas_call(
        pair_kernel, grid=(rows // step,),
        in_specs=[pl.BlockSpec((step, cols, chans), lambda i: (i, 0, 0)),
                  pl.BlockSpec((heads, chans), lambda i: (0, 0))],
        out_specs=pl.BlockSpec((heads, 2, step, cols), lambda i: (0, 0, i, 0)),
        out_shape=jax.ShapeDtypeStruct((heads, 2, rows, cols), BF),
        compiler_params=pltpu.CompilerParams(dimension_semantics=("arbitrary",), vmem_limit_bytes=60 << 20),
    )(pair, bias_weight.T)

def stats_kernel(pair_ref, normed_ref, scaled_ref):
    rows, cols, chans = pair_ref.shape
    normed, scaled = unit(pair_ref[...].astype(F32).reshape(rows * cols, chans))
    normed_ref[...] = normed.reshape(rows, cols, chans)
    lanes = jnp.broadcast_to(scaled, (rows * cols, chans)).reshape(rows, cols, chans)
    for i in range(rows):
        scaled_ref[i : i + 1] = lanes[i].T[:1]

def pair_stats(pair, step=16):
    rows, cols, chans = pair.shape
    return pl.pallas_call(
        stats_kernel, grid=(rows // step,),
        in_specs=[pl.BlockSpec((step, cols, chans), lambda i: (i, 0, 0))],
        out_specs=[pl.BlockSpec((step, cols, chans), lambda i: (i, 0, 0)), pl.BlockSpec((step, cols), lambda i: (i, 0))],
        out_shape=[jax.ShapeDtypeStruct((rows, cols, chans), F32), jax.ShapeDtypeStruct((rows, cols), F32)],
        compiler_params=pltpu.CompilerParams(dimension_semantics=("arbitrary",), vmem_limit_bytes=60 << 20),
    )(pair)

def back_kernel(normed_ref, scaled_ref, grad_ref, w_ref, out_ref):
    rows, cols, chans = normed_ref.shape
    heads, parts = grad_ref.shape[:2]
    grad = grad_ref[:, 0].astype(F32)
    for g in range(1, parts):
        grad = grad + grad_ref[:, g].astype(F32)
    grad = (grad * scaled_ref[...][None]).reshape(heads, rows * cols)
    high, low = halves(grad)
    weight = w_ref[...].astype(F32)
    w_high, w_low = halves(weight - jnp.mean(weight, axis=1, keepdims=True))
    both = jnp.concatenate([high, low, high, low], axis=0)
    weight = jnp.concatenate([w_high, w_high, w_low, w_low], axis=0)
    centred = lax.dot_general(both, weight, (((0,), (0,)), ((), ())), preferred_element_type=F32)
    normed = normed_ref[...].reshape(rows * cols, chans)
    along = jnp.mean(centred * normed, axis=-1, keepdims=True)
    out_ref[...] = (centred - normed * along).reshape(rows, cols, chans)

def pair_back(stats, grad, bias_weight, step=16):
    normed, scaled = stats
    rows, cols, chans = normed.shape
    heads, parts = grad.shape[:2]
    return pl.pallas_call(
        back_kernel, grid=(rows // step,),
        in_specs=[pl.BlockSpec((step, cols, chans), lambda i: (i, 0, 0)),
                  pl.BlockSpec((step, cols), lambda i: (i, 0)),
                  pl.BlockSpec((heads, parts, step, cols), lambda i: (0, 0, i, 0)),
                  pl.BlockSpec((heads, chans), lambda i: (0, 0))],
        out_specs=pl.BlockSpec((step, cols, chans), lambda i: (i, 0, 0)),
        out_shape=jax.ShapeDtypeStruct((rows, cols, chans), F32),
        compiler_params=pltpu.CompilerParams(dimension_semantics=("arbitrary",), vmem_limit_bytes=50 << 20),
    )(normed, scaled, grad, bias_weight.T)

def project_kernel(core_ref, single_ref, got_ref, cot_ref, gotc_ref, w_ref, packed_ref, tokens_ref, normed, cotan):
    half, block, width = tokens_ref.shape
    heads, _, lanes = packed_ref.shape
    size = width // heads
    rows = block // 2
    step = pl.program_id(0)
    core = core_ref[0]

    @pl.when(step == 0)
    def _():
        mine = pl.ds(pl.multiple_of(core * rows, rows), rows)
        other = pl.ds(pl.multiple_of((1 - core) * rows, rows), rows)
        for u in range(half):
            for src, far, dst in ((single_ref, got_ref, tokens_ref), (cot_ref, gotc_ref, cotan)):
                dst[u, mine, :] = src[core * half + u]
                dst[u, other, :] = far[core * half + u]
        normed[...] = unit(tokens_ref[...].reshape(lanes, width).astype(F32))[0].astype(BF)
        turned = cotan[...].reshape(lanes, width).astype(F32).T.astype(BF)
        for h in range(heads):
            packed_ref[h, 3 * size : 4 * size, :] = turned[h * size : (h + 1) * size]

    cols = w_ref.shape[1]
    out = jnp.dot(normed[...], w_ref[...], preferred_element_type=F32).T.astype(BF)
    for p in range(3):
        @pl.when(step // 2 == p)
        def _():
            base = (step % 2) * (cols // size)
            for h in range(cols // size):
                packed_ref[base + h, p * size : (p + 1) * size, :] = out[h * size : (h + 1) * size]

def project(core, single, got, cot, gotc, w_qkv, heads):
    samp, rows, width = single.shape
    half, block = samp // 2, 2 * rows
    lanes = half * block
    size = width // heads
    whole = pl.BlockSpec((samp, rows, width), lambda i, c: (0, 0, 0))
    return pl.pallas_call(
        project_kernel,
        grid_spec=pltpu.PrefetchScalarGridSpec(
            num_scalar_prefetch=1, grid=(6,),
            in_specs=[whole] * 4 + [pl.BlockSpec((width, width // 2), lambda i, c: (0, i))],
            out_specs=[pl.BlockSpec((heads, 4 * size, lanes), lambda i, c: (0, 0, 0)),
                       pl.BlockSpec((half, block, width), lambda i, c: (0, 0, 0))],
            scratch_shapes=[pltpu.VMEM((lanes, width), BF), pltpu.VMEM((half, block, width), BF)],
        ),
        out_shape=[jax.ShapeDtypeStruct((heads, 4 * size, lanes), BF), jax.ShapeDtypeStruct((half, block, width), BF)],
        compiler_params=pltpu.CompilerParams(dimension_semantics=("arbitrary",), vmem_limit_bytes=50 << 20),
    )(core, single, got, cot, gotc, w_qkv)

def transition_kernel(core_ref, tokens_ref, att_ref, wo_ref, wg_ref, wu_ref, wd_ref, mine_ref, theirs_ref, mid, normed, done):
    half, block, width = tokens_ref.shape
    rows = block // 2
    step = pl.program_id(0)

    @pl.when(step == 0)
    def _():
        attended = att_ref[...].astype(F32).T.astype(BF)
        flat = tokens_ref[...].reshape(half * block, width).astype(F32)
        flat = flat + jnp.dot(attended, wo_ref[...], preferred_element_type=F32)
        mid[...] = flat
        normed[...] = unit(flat)[0].astype(BF)

    gate = jnp.dot(normed[...], wg_ref[...], preferred_element_type=F32)
    up = jnp.dot(normed[...], wu_ref[...], preferred_element_type=F32)
    hidden = (jax.nn.silu(gate) * up).astype(BF)
    mid[...] += jnp.dot(hidden, wd_ref[...], preferred_element_type=F32)

    @pl.when(step == pl.num_programs(0) - 1)
    def _():
        done[...] = mid[...].astype(BF).reshape(half, block, width)
        core = core_ref[0]
        mine = pl.ds(pl.multiple_of(core * rows, rows), rows)
        other = pl.ds(pl.multiple_of((1 - core) * rows, rows), rows)
        for u in range(half):
            mine_ref[core * half + u] = done[u, mine, :]
            mine_ref[(1 - core) * half + u] = jnp.zeros((rows, width), BF)
            theirs_ref[u] = done[u, other, :]

def transition(core, tokens, attended_t, w_out, w_gate_up, w_down, steps=4):
    half, block, width = tokens.shape
    lanes = half * block
    inner = w_down.shape[0]
    part = inner // steps
    out = lambda n: pl.BlockSpec((n, block // 2, width), lambda i, c: (0, 0, 0))
    return pl.pallas_call(
        transition_kernel,
        grid_spec=pltpu.PrefetchScalarGridSpec(
            num_scalar_prefetch=1, grid=(steps,),
            in_specs=[pl.BlockSpec((half, block, width), lambda i, c: (0, 0, 0)),
                      pl.BlockSpec((width, lanes), lambda i, c: (0, 0)),
                      pl.BlockSpec((width, width), lambda i, c: (0, 0)),
                      pl.BlockSpec((width, part), lambda i, c: (0, i)),
                      pl.BlockSpec((width, part), lambda i, c: (0, i + steps)),
                      pl.BlockSpec((part, width), lambda i, c: (i, 0))],
            out_specs=[out(2 * half), out(half)],
            scratch_shapes=[pltpu.VMEM((lanes, width), F32), pltpu.VMEM((lanes, width), BF),
                            pltpu.VMEM((half, block, width), BF)],
        ),
        out_shape=[jax.ShapeDtypeStruct((n * half, block // 2, width), BF) for n in (2, 1)],
        compiler_params=pltpu.CompilerParams(dimension_semantics=("arbitrary",), vmem_limit_bytes=60 << 20),
    )(core, tokens, attended_t, w_out, w_gate_up, w_gate_up, w_down)

def split(v):
    high = v.astype(BF).astype(F32)
    return high, v - high

def attend_kernel(n_col, n_chip, per, size, c_ref, blk_ref, *refs):
    bias_refs = refs[: n_col // 2]
    att_ref = refs[n_col // 2]
    out_refs = refs[n_col // 2 + 1 : n_col + 1]
    bias2, acc, kt, vt = refs[n_col + 1 :]
    me = c_ref[0]
    side = me // (n_col // 2)
    block = blk_ref.shape[3] // per
    wide = block * n_col
    rest = block - 2 * size

    for k in range(n_col):
        far = jnp.bitwise_xor(side, k // (n_col // 2))
        part = bias_refs[k % (n_col // 2)][:, far]
        part = part.astype(F32).reshape(bias2.shape[0], block)
        bias2[:, k * block : (k + 1) * block] = part * LOG2E
    row = lax.broadcasted_iota(jnp.int32, (rest, wide), 0)
    for h in range(2 * per):
        kt[h, 2 * size :, :] = jnp.zeros((rest, wide), BF)
        vt[h, 2 * size :, :] = jnp.where(row < 3, 1.0, 0.0).astype(BF)

    scale = LOG2E / math.sqrt(size)
    row = lax.broadcasted_iota(jnp.int32, (rest, block), 0)

    def prepare(u, h):
        for k in range(n_col):
            owner = jnp.bitwise_xor(me, k)
            cols = slice(k * block, (k + 1) * block)
            keys = blk_ref[owner, h, size : 2 * size, u * block : (u + 1) * block]
            kt[2 * u + h, :size, cols] = keys
            kt[2 * u + h, size : 2 * size, cols] = keys
            vals = blk_ref[owner, h, 2 * size : 3 * size, u * block : (u + 1) * block]
            vt[2 * u + h, :size, cols] = vals
            vt[2 * u + h, size : 2 * size, cols] = vals
        lhs = []
        for b in range(n_chip):
            high, low = split(blk_ref[b, h, :size, u * block : (u + 1) * block].astype(F32) * scale)
            lhs.append(jnp.concatenate([high, low, jnp.zeros((rest, block), F32)], axis=0).T.astype(BF))
        return jnp.concatenate(lhs, axis=0)

    def softmax(u, h, lhs):
        scores = jnp.dot(lhs, kt[2 * u + h], preferred_element_type=F32) + bias2[...]
        top = jnp.max(scores, axis=1, keepdims=True)
        return jnp.exp2(scores - top)

    def mix(u, h, probs):
        mixed = lax.dot_general(
            probs.astype(BF), vt[2 * u + h], (((1,), (1,)), ((), ())), preferred_element_type=F32
        )
        lhs = []
        for b in range(n_chip):
            mixed_t = mixed[b * block : (b + 1) * block].T
            inv = 1.0 / mixed_t[2 * size : 2 * size + 1]
            att = mixed_t[:size] * inv
            att_ref[b, h, :, u * block : (u + 1) * block] = att.astype(BF)
            cotan = blk_ref[b, h, 3 * size :, u * block : (u + 1) * block].astype(F32)
            delta = -jnp.sum(cotan * att, axis=0, keepdims=True) * inv
            high, low = split(cotan * inv)
            d0, rem = split(delta)
            d1, d2 = split(rem)
            tail = jnp.where(row == 0, d0, jnp.where(row == 1, d1, jnp.where(row == 2, d2, 0.0)))
            lhs.append(jnp.concatenate([high, low, tail], axis=0).T.astype(BF))
        return jnp.concatenate(lhs, axis=0)

    def grad(u, h, probs, lhs):
        return probs * jnp.dot(lhs, vt[2 * u + h], preferred_element_type=F32)

    for u in range(per):
        lhs = [prepare(u, h) for h in range(2)]
        probs = [softmax(u, h, lhs[h]) for h in range(2)]
        lhs = [mix(u, h, probs[h]) for h in range(2)]
        term = grad(u, 0, probs[0], lhs[0]) + grad(u, 1, probs[1], lhs[1])
        if u == 0:
            acc[...] = term
        elif u < per - 1:
            acc[...] += term
        else:
            term = (acc[...] + term).astype(BF)
            for k in range(n_col):
                part = term[:, k * block : (k + 1) * block]
                out_ref = out_refs[k % (n_col // 2)]
                far = jnp.bitwise_xor(side, k // (n_col // 2))
                out_ref[:, far] = part.reshape(out_ref.shape[0], out_ref.shape[2], block)


def attend(me, qkvc, biases, n_samp, size, limit=48):
    n_chip, _, _, lanes = qkvc.shape
    per = n_samp // 2
    block = lanes // per
    n_col = 2 * len(biases)
    tokens = n_chip * block
    wide = n_col * block
    parts = biases[0].shape
    whole = pl.BlockSpec(parts, lambda s, c: (0, 0, 0, 0))
    spec = lambda feats: pl.BlockSpec((n_chip, 2, feats, lanes), lambda s, c: (0, 0, 0, 0))
    return pl.pallas_call(
        functools.partial(attend_kernel, n_col, n_chip, per, size),
        grid_spec=pltpu.PrefetchScalarGridSpec(
            num_scalar_prefetch=1,
            grid=(1,),
            in_specs=[spec(4 * size)] + [whole] * len(biases),
            out_specs=[spec(size)] + [whole] * len(biases),
            scratch_shapes=[
                pltpu.VMEM((tokens, wide), F32),
                pltpu.VMEM((tokens, wide), F32),
                pltpu.VMEM((n_samp, block, wide), BF),
                pltpu.VMEM((n_samp, block, wide), BF),
            ],
        ),
        out_shape=[jax.ShapeDtypeStruct((n_chip, 2, size, lanes), BF)]
        + [jax.ShapeDtypeStruct(parts, BF)] * len(biases),
        compiler_params=pltpu.CompilerParams(
            dimension_semantics=("arbitrary",), vmem_limit_bytes=limit * 1024 * 1024
        ),
    )(me, qkvc, *biases)


def shards(n_row, n_col, pair, bias_weight, single, w_qkv, w_out, w_gate_up, w_down, cotangent):
    samp, rows, width = single.shape
    heads = bias_weight.shape[1]
    size = width // heads
    half = samp // 2
    block = 2 * rows
    n_chip = n_row // 2
    core = lax.rem(lax.axis_index("row"), 2).astype(jnp.int32)
    me = lax.axis_index("col").astype(jnp.int32).reshape(1)
    cores = [(i, i ^ 1) for i in range(n_row)]
    flip = lambda k: [(i, i ^ k) for i in range(n_col)]

    got = lax.ppermute(single, "row", cores)
    got_cot = lax.ppermute(cotangent, "row", cores)
    groups = [[r * n_col + z * (n_col // 2) + y for r in range(n_row) for z in range(2)] for y in range(n_col // 2)]
    share = lambda v: lax.all_to_all(
        v.reshape(2 * n_row, rows, pair.shape[1]), ("row", "col"), 0, 0, tiled=True, axis_index_groups=groups
    ).reshape(n_row, 2, rows, pair.shape[1])
    bias = share(pair_bias(pair, bias_weight, 32))
    packed, tokens = project(core.reshape(1), single, got, cotangent, got_cot, w_qkv, heads)
    biases = [bias] + [lax.ppermute(bias, "col", flip(k)) for k in range(1, n_col // 2)]

    later, _ = lax.optimization_barrier((pair, bias))
    stats = pair_stats(later, 16)
    packed = lax.all_to_all(packed, "row", 0, 0, tiled=True)
    packed, stats = lax.optimization_barrier((packed, stats))
    packed = packed.reshape(n_chip, 2, 4 * size, half * block)
    attended, *grads = attend(me, packed, biases, samp, size)
    grads = [grads[0]] + [lax.ppermute(grads[k], "col", flip(k)) for k in range(1, n_col // 2)]
    attended = attended.reshape(n_row, size, half * block)
    attended = lax.all_to_all(attended, "row", 0, 0, tiled=True)
    total = grads[0].astype(F32)
    for part in grads[1:]:
        total = total + part.astype(F32)
    attended, total = lax.optimization_barrier((attended, total.astype(BF)))
    total = share(total)
    mine, theirs = transition(
        core.reshape(1), tokens, attended.reshape(width, half * block), w_out, w_gate_up, w_down
    )
    mine, theirs, total = lax.optimization_barrier((mine, theirs, total))
    got = lax.ppermute(theirs, "row", cores)
    updated = lax.dynamic_update_slice_in_dim(mine, got, (1 - core) * half, 0)
    pair_grad = pair_back(stats, total, bias_weight, 32)
    return (updated, pair_grad)


def solution(mesh):
    sizes = dict(mesh.shape)
    return jax.shard_map(
        functools.partial(shards, sizes["row"], sizes["col"]),
        mesh=mesh,
        in_specs=(
            P("row", "col", None),
            P(),
            P("col", "row", None),
            P(),
            P(),
            P(),
            P(),
            P("col", "row", None),
        ),
        out_specs=(P("col", "row", None), P("row", "col", None)),
        check_vma=False,
    )
```

```python
import functools
import math

import jax
import jax.numpy as jnp
from jax import lax
from jax.experimental import pallas as pl
from jax.experimental.pallas import tpu as pltpu
from jax.sharding import PartitionSpec as P

BF = jnp.bfloat16
F32 = jnp.float32
LOG2E = 1.4426950408889634

def unit(values):
    mean_val = jnp.mean(values, axis=-1, keepdims=True)
    centred = values - mean_val
    variance = jnp.mean(centred * centred, axis=-1, keepdims=True)
    scaled = lax.rsqrt(variance + 1e-05)
    return centred * scaled, scaled

def halves(v):
    high = v.astype(BF)
    return high, (v - high.astype(F32)).astype(BF)

def across(lhs, rhs):
    return lax.dot_general(lhs, rhs, (((1,), (1,)), ((), ())), preferred_element_type=F32)

def pair_kernel(pair_ref, w_ref, out_ref):
    rows, cols, chans = pair_ref.shape
    heads = w_ref.shape[0]
    raw = pair_ref[...].reshape(rows * cols, chans)
    values = raw.astype(F32)
    centred = values - jnp.mean(values, axis=-1, keepdims=True)
    weight = w_ref[...].astype(F32)
    weight = weight - jnp.mean(weight, axis=1, keepdims=True)
    w0 = weight.astype(BF)
    w1, w2 = halves(weight - w0.astype(F32))
    flat = across(jnp.concatenate([w0, w1, w2], axis=0), raw)
    flat = flat[:heads] + flat[heads : 2 * heads] + flat[2 * heads :]
    ones = jnp.full((8, chans), 1.0 / chans, BF)
    variance = across(ones, (centred * centred).astype(BF))[:1]
    flat = (flat * lax.rsqrt(variance + 1e-05)).reshape(heads, rows, cols).astype(BF)
    out_ref[:, 0] = flat
    out_ref[:, 1] = flat

def pair_bias(pair, bias_weight, step=16):
    rows, cols, chans = pair.shape
    heads = bias_weight.shape[1]
    return pl.pallas_call(
        pair_kernel, grid=(rows // step,),
        in_specs=[pl.BlockSpec((step, cols, chans), lambda i: (i, 0, 0)),
                  pl.BlockSpec((heads, chans), lambda i: (0, 0))],
        out_specs=pl.BlockSpec((heads, 2, step, cols), lambda i: (0, 0, i, 0)),
        out_shape=jax.ShapeDtypeStruct((heads, 2, rows, cols), BF),
        compiler_params=pltpu.CompilerParams(dimension_semantics=("arbitrary",), vmem_limit_bytes=60 << 20),
    )(pair, bias_weight.T)

def stats_kernel(pair_ref, normed_ref, scaled_ref):
    rows, cols, chans = pair_ref.shape
    normed, scaled = unit(pair_ref[...].astype(F32).reshape(rows * cols, chans))
    normed_ref[...] = normed.reshape(rows, cols, chans)
    lanes = jnp.broadcast_to(scaled, (rows * cols, chans)).reshape(rows, cols, chans)
    for i in range(rows):
        scaled_ref[i : i + 1] = lanes[i].T[:1]

def pair_stats(pair, step=16):
    rows, cols, chans = pair.shape
    return pl.pallas_call(
        stats_kernel, grid=(rows // step,),
        in_specs=[pl.BlockSpec((step, cols, chans), lambda i: (i, 0, 0))],
        out_specs=[pl.BlockSpec((step, cols, chans), lambda i: (i, 0, 0)), pl.BlockSpec((step, cols), lambda i: (i, 0))],
        out_shape=[jax.ShapeDtypeStruct((rows, cols, chans), F32), jax.ShapeDtypeStruct((rows, cols), F32)],
        compiler_params=pltpu.CompilerParams(dimension_semantics=("arbitrary",), vmem_limit_bytes=60 << 20),
    )(pair)

def back_kernel(normed_ref, scaled_ref, grad_ref, w_ref, out_ref):
    rows, cols, chans = normed_ref.shape
    heads, parts = grad_ref.shape[:2]
    grad = grad_ref[:, 0].astype(F32)
    for g in range(1, parts):
        grad = grad + grad_ref[:, g].astype(F32)
    grad = (grad * scaled_ref[...][None]).reshape(heads, rows * cols)
    high, low = halves(grad)
    weight = w_ref[...].astype(F32)
    w_high, w_low = halves(weight - jnp.mean(weight, axis=1, keepdims=True))
    both = jnp.concatenate([high, low, high, low], axis=0)
    weight = jnp.concatenate([w_high, w_high, w_low, w_low], axis=0)
    centred = lax.dot_general(both, weight, (((0,), (0,)), ((), ())), preferred_element_type=F32)
    normed = normed_ref[...].reshape(rows * cols, chans)
    along = jnp.mean(centred * normed, axis=-1, keepdims=True)
    out_ref[...] = (centred - normed * along).reshape(rows, cols, chans)

def pair_back(stats, grad, bias_weight, step=16):
    normed, scaled = stats
    rows, cols, chans = normed.shape
    heads, parts = grad.shape[:2]
    return pl.pallas_call(
        back_kernel, grid=(rows // step,),
        in_specs=[pl.BlockSpec((step, cols, chans), lambda i: (i, 0, 0)),
                  pl.BlockSpec((step, cols), lambda i: (i, 0)),
                  pl.BlockSpec((heads, parts, step, cols), lambda i: (0, 0, i, 0)),
                  pl.BlockSpec((heads, chans), lambda i: (0, 0))],
        out_specs=pl.BlockSpec((step, cols, chans), lambda i: (i, 0, 0)),
        out_shape=jax.ShapeDtypeStruct((rows, cols, chans), F32),
        compiler_params=pltpu.CompilerParams(dimension_semantics=("arbitrary",), vmem_limit_bytes=50 << 20),
    )(normed, scaled, grad, bias_weight.T)

def project_kernel(core_ref, single_ref, got_ref, cot_ref, gotc_ref, w_ref, packed_ref, tokens_ref, normed, cotan):
    half, block, width = tokens_ref.shape
    heads, _, lanes = packed_ref.shape
    size = width // heads
    rows = block // 2
    step = pl.program_id(0)
    core = core_ref[0]

    @pl.when(step == 0)
    def _():
        mine = pl.ds(pl.multiple_of(core * rows, rows), rows)
        other = pl.ds(pl.multiple_of((1 - core) * rows, rows), rows)
        for u in range(half):
            for src, far, dst in ((single_ref, got_ref, tokens_ref), (cot_ref, gotc_ref, cotan)):
                dst[u, mine, :] = src[core * half + u]
                dst[u, other, :] = far[core * half + u]
        normed[...] = unit(tokens_ref[...].reshape(lanes, width).astype(F32))[0].astype(BF)
        turned = cotan[...].reshape(lanes, width).astype(F32).T.astype(BF)
        for h in range(heads):
            packed_ref[h, 3 * size : 4 * size, :] = turned[h * size : (h + 1) * size]

    cols = w_ref.shape[1]
    out = jnp.dot(normed[...], w_ref[...], preferred_element_type=F32).T.astype(BF)
    for p in range(3):
        @pl.when(step // 2 == p)
        def _():
            base = (step % 2) * (cols // size)
            for h in range(cols // size):
                packed_ref[base + h, p * size : (p + 1) * size, :] = out[h * size : (h + 1) * size]

def project(core, single, got, cot, gotc, w_qkv, heads):
    samp, rows, width = single.shape
    half, block = samp // 2, 2 * rows
    lanes = half * block
    size = width // heads
    whole = pl.BlockSpec((samp, rows, width), lambda i, c: (0, 0, 0))
    return pl.pallas_call(
        project_kernel,
        grid_spec=pltpu.PrefetchScalarGridSpec(
            num_scalar_prefetch=1, grid=(6,),
            in_specs=[whole] * 4 + [pl.BlockSpec((width, width // 2), lambda i, c: (0, i))],
            out_specs=[pl.BlockSpec((heads, 4 * size, lanes), lambda i, c: (0, 0, 0)),
                       pl.BlockSpec((half, block, width), lambda i, c: (0, 0, 0))],
            scratch_shapes=[pltpu.VMEM((lanes, width), BF), pltpu.VMEM((half, block, width), BF)],
        ),
        out_shape=[jax.ShapeDtypeStruct((heads, 4 * size, lanes), BF), jax.ShapeDtypeStruct((half, block, width), BF)],
        compiler_params=pltpu.CompilerParams(dimension_semantics=("arbitrary",), vmem_limit_bytes=50 << 20),
    )(core, single, got, cot, gotc, w_qkv)

def transition_kernel(core_ref, tokens_ref, att_ref, wo_ref, wg_ref, wu_ref, wd_ref, mine_ref, theirs_ref, mid, normed, done):
    half, block, width = tokens_ref.shape
    rows = block // 2
    step = pl.program_id(0)

    @pl.when(step == 0)
    def _():
        attended = att_ref[...].astype(F32).T.astype(BF)
        flat = tokens_ref[...].reshape(half * block, width).astype(F32)
        flat = flat + jnp.dot(attended, wo_ref[...], preferred_element_type=F32)
        mid[...] = flat
        normed[...] = unit(flat)[0].astype(BF)

    gate = jnp.dot(normed[...], wg_ref[...], preferred_element_type=F32)
    up = jnp.dot(normed[...], wu_ref[...], preferred_element_type=F32)
    hidden = (jax.nn.silu(gate) * up).astype(BF)
    mid[...] += jnp.dot(hidden, wd_ref[...], preferred_element_type=F32)

    @pl.when(step == pl.num_programs(0) - 1)
    def _():
        done[...] = mid[...].astype(BF).reshape(half, block, width)
        core = core_ref[0]
        mine = pl.ds(pl.multiple_of(core * rows, rows), rows)
        other = pl.ds(pl.multiple_of((1 - core) * rows, rows), rows)
        for u in range(half):
            mine_ref[core * half + u] = done[u, mine, :]
            mine_ref[(1 - core) * half + u] = jnp.zeros((rows, width), BF)
            theirs_ref[u] = done[u, other, :]

def transition(core, tokens, attended_t, w_out, w_gate_up, w_down, steps=4):
    half, block, width = tokens.shape
    lanes = half * block
    inner = w_down.shape[0]
    part = inner // steps
    out = lambda n: pl.BlockSpec((n, block // 2, width), lambda i, c: (0, 0, 0))
    return pl.pallas_call(
        transition_kernel,
        grid_spec=pltpu.PrefetchScalarGridSpec(
            num_scalar_prefetch=1, grid=(steps,),
            in_specs=[pl.BlockSpec((half, block, width), lambda i, c: (0, 0, 0)),
                      pl.BlockSpec((width, lanes), lambda i, c: (0, 0)),
                      pl.BlockSpec((width, width), lambda i, c: (0, 0)),
                      pl.BlockSpec((width, part), lambda i, c: (0, i)),
                      pl.BlockSpec((width, part), lambda i, c: (0, i + steps)),
                      pl.BlockSpec((part, width), lambda i, c: (i, 0))],
            out_specs=[out(2 * half), out(half)],
            scratch_shapes=[pltpu.VMEM((lanes, width), F32), pltpu.VMEM((lanes, width), BF),
                            pltpu.VMEM((half, block, width), BF)],
        ),
        out_shape=[jax.ShapeDtypeStruct((n * half, block // 2, width), BF) for n in (2, 1)],
        compiler_params=pltpu.CompilerParams(dimension_semantics=("arbitrary",), vmem_limit_bytes=60 << 20),
    )(core, tokens, attended_t, w_out, w_gate_up, w_gate_up, w_down)

def split(v):
    high = v.astype(BF).astype(F32)
    return high, v - high

def attend_kernel(n_col, n_chip, per, size, c_ref, blk_ref, *refs):
    bias_refs = refs[: n_col // 2]
    att_ref = refs[n_col // 2]
    out_refs = refs[n_col // 2 + 1 : n_col]
    pair_refs = refs[n_col : n_col + 2]
    bias2, acc, kt, vt = refs[n_col + 2 :]
    me = c_ref[0]
    side = me // (n_col // 2)
    block = blk_ref.shape[3] // per
    wide = block * n_col
    rest = block - 2 * size

    for k in range(n_col):
        far = jnp.bitwise_xor(side, k // (n_col // 2))
        part = bias_refs[k % (n_col // 2)][:, far]
        part = part.astype(F32).reshape(bias2.shape[0], block)
        bias2[:, k * block : (k + 1) * block] = part * LOG2E
    row = lax.broadcasted_iota(jnp.int32, (rest, wide), 0)
    for h in range(2 * per):
        kt[h, 2 * size :, :] = jnp.zeros((rest, wide), BF)
        vt[h, 2 * size :, :] = jnp.where(row < 3, 1.0, 0.0).astype(BF)

    scale = LOG2E / math.sqrt(size)
    row = lax.broadcasted_iota(jnp.int32, (rest, block), 0)

    def prepare(u, h):
        for k in range(n_col):
            owner = jnp.bitwise_xor(me, k)
            cols = slice(k * block, (k + 1) * block)
            keys = blk_ref[owner, h, size : 2 * size, u * block : (u + 1) * block]
            kt[2 * u + h, :size, cols] = keys
            kt[2 * u + h, size : 2 * size, cols] = keys
            vals = blk_ref[owner, h, 2 * size : 3 * size, u * block : (u + 1) * block]
            vt[2 * u + h, :size, cols] = vals
            vt[2 * u + h, size : 2 * size, cols] = vals
        lhs = []
        for b in range(n_chip):
            high, low = split(blk_ref[b, h, :size, u * block : (u + 1) * block].astype(F32) * scale)
            lhs.append(jnp.concatenate([high, low, jnp.zeros((rest, block), F32)], axis=0).T.astype(BF))
        return jnp.concatenate(lhs, axis=0)

    def softmax(u, h, lhs):
        scores = jnp.dot(lhs, kt[2 * u + h], preferred_element_type=F32) + bias2[...]
        top = jnp.max(scores, axis=1, keepdims=True)
        return jnp.exp2(scores - top)

    def mix(u, h, probs):
        mixed = lax.dot_general(
            probs.astype(BF), vt[2 * u + h], (((1,), (1,)), ((), ())), preferred_element_type=F32
        )
        lhs = []
        for b in range(n_chip):
            mixed_t = mixed[b * block : (b + 1) * block].T
            inv = 1.0 / mixed_t[2 * size : 2 * size + 1]
            att = mixed_t[:size] * inv
            att_ref[b, h, :, u * block : (u + 1) * block] = att.astype(BF)
            cotan = blk_ref[b, h, 3 * size :, u * block : (u + 1) * block].astype(F32)
            delta = -jnp.sum(cotan * att, axis=0, keepdims=True) * inv
            high, low = split(cotan * inv)
            d0, rem = split(delta)
            d1, d2 = split(rem)
            tail = jnp.where(row == 0, d0, jnp.where(row == 1, d1, jnp.where(row == 2, d2, 0.0)))
            lhs.append(jnp.concatenate([high, low, tail], axis=0).T.astype(BF))
        return jnp.concatenate(lhs, axis=0)

    def grad(u, h, probs, lhs):
        return probs * jnp.dot(lhs, vt[2 * u + h], preferred_element_type=F32)

    for u in range(per):
        lhs = [prepare(u, h) for h in range(2)]
        probs = [softmax(u, h, lhs[h]) for h in range(2)]
        lhs = [mix(u, h, probs[h]) for h in range(2)]
        term = grad(u, 0, probs[0], lhs[0]) + grad(u, 1, probs[1], lhs[1])
        if u == 0:
            acc[...] = term
        elif u < per - 1:
            acc[...] += term
        else:
            term = (acc[...] + term).astype(BF)
            for k in range(n_col):
                part = term[:, k * block : (k + 1) * block]
                part = part.reshape(out_refs[0].shape[0], out_refs[0].shape[2], block)
                ring = k % (n_col // 2)
                if ring == 2:
                    pair_refs[k // (n_col // 2)][...] = part
                else:
                    out_ref = out_refs[min(ring, 2)]
                    out_ref[:, jnp.bitwise_xor(side, k // (n_col // 2))] = part


def attend(me, qkvc, biases, n_samp, size, limit=48):
    n_chip, _, _, lanes = qkvc.shape
    per = n_samp // 2
    block = lanes // per
    n_col = 2 * len(biases)
    tokens = n_chip * block
    wide = n_col * block
    parts = biases[0].shape
    whole = pl.BlockSpec(parts, lambda s, c: (0, 0, 0, 0))
    single = (parts[0],) + parts[2:]
    made = [whole] * 3 + [pl.BlockSpec(single, lambda s, c: (0, 0, 0))] * 2
    shapes = [parts] * 3 + [single] * 2
    spec = lambda feats: pl.BlockSpec((n_chip, 2, feats, lanes), lambda s, c: (0, 0, 0, 0))
    return pl.pallas_call(
        functools.partial(attend_kernel, n_col, n_chip, per, size),
        grid_spec=pltpu.PrefetchScalarGridSpec(
            num_scalar_prefetch=1,
            grid=(1,),
            in_specs=[spec(4 * size)] + [whole] * len(biases),
            out_specs=[spec(size)] + made,
            scratch_shapes=[
                pltpu.VMEM((tokens, wide), F32),
                pltpu.VMEM((tokens, wide), F32),
                pltpu.VMEM((n_samp, block, wide), BF),
                pltpu.VMEM((n_samp, block, wide), BF),
            ],
        ),
        out_shape=[jax.ShapeDtypeStruct((n_chip, 2, size, lanes), BF)]
        + [jax.ShapeDtypeStruct(shape, BF) for shape in shapes],
        compiler_params=pltpu.CompilerParams(
            dimension_semantics=("arbitrary",), vmem_limit_bytes=limit * 1024 * 1024
        ),
    )(me, qkvc, *biases)


def shards(n_row, n_col, pair, bias_weight, single, w_qkv, w_out, w_gate_up, w_down, cotangent):
    samp, rows, width = single.shape
    heads = bias_weight.shape[1]
    size = width // heads
    half = samp // 2
    block = 2 * rows
    n_chip = n_row // 2
    core = lax.rem(lax.axis_index("row"), 2).astype(jnp.int32)
    me = lax.axis_index("col").astype(jnp.int32).reshape(1)
    cores = [(i, i ^ 1) for i in range(n_row)]
    flip = lambda k: [(i, i ^ k) for i in range(n_col)]

    got = lax.ppermute(single, "row", cores)
    got_cot = lax.ppermute(cotangent, "row", cores)
    groups = [[r * n_col + z * (n_col // 2) + y for r in range(n_row) for z in range(2)] for y in range(n_col // 2)]
    share = lambda v: lax.all_to_all(
        v.reshape(2 * n_row, rows, pair.shape[1]), ("row", "col"), 0, 0, tiled=True, axis_index_groups=groups
    ).reshape(n_row, 2, rows, pair.shape[1])
    bias = share(pair_bias(pair, bias_weight, 32))
    packed, tokens = project(core.reshape(1), single, got, cotangent, got_cot, w_qkv, heads)
    biases = [bias] + [lax.ppermute(bias, "col", flip(k)) for k in range(1, n_col // 2)]

    later, _ = lax.optimization_barrier((pair, bias))
    stats = pair_stats(later, 16)
    packed = lax.all_to_all(packed, "row", 0, 0, tiled=True)
    packed, stats = lax.optimization_barrier((packed, stats))
    packed = packed.reshape(n_chip, 2, 4 * size, half * block)
    attended, *grads = attend(me, packed, biases, samp, size)
    mine, one, three, two, far = grads
    far = lax.ppermute(far, "col", flip(n_col // 2))
    one = lax.ppermute(one, "col", flip(1))
    three = lax.ppermute(three, "col", flip(3))
    attended = attended.reshape(n_row, size, half * block)
    attended = lax.all_to_all(attended, "row", 0, 0, tiled=True)
    two = lax.ppermute((two.astype(F32) + far.astype(F32)).astype(BF), "col", flip(2))
    side = lax.broadcasted_iota(jnp.int32, mine.shape, 1) == me[0] // (n_col // 2)
    total = mine.astype(F32) + one.astype(F32) + three.astype(F32)
    total = total + jnp.where(side, two.astype(F32)[:, None], 0.0)
    attended, total = lax.optimization_barrier((attended, total.astype(BF)))
    total = share(total)
    mine, theirs = transition(
        core.reshape(1), tokens, attended.reshape(width, half * block), w_out, w_gate_up, w_down
    )
    mine, theirs, total = lax.optimization_barrier((mine, theirs, total))
    got = lax.ppermute(theirs, "row", cores)
    updated = lax.dynamic_update_slice_in_dim(mine, got, (1 - core) * half, 0)
    pair_grad = pair_back(stats, total, bias_weight, 32)
    return (updated, pair_grad)


def solution(mesh):
    sizes = dict(mesh.shape)
    return jax.shard_map(
        functools.partial(shards, sizes["row"], sizes["col"]),
        mesh=mesh,
        in_specs=(
            P("row", "col", None),
            P(),
            P("col", "row", None),
            P(),
            P(),
            P(),
            P(),
            P("col", "row", None),
        ),
        out_specs=(P("col", "row", None), P("row", "col", None)),
        check_vma=False,
    )
```

```python
import functools
import math

import jax
import jax.numpy as jnp
from jax import lax
from jax.experimental import pallas as pl
from jax.experimental.pallas import tpu as pltpu
from jax.sharding import PartitionSpec as P

BF = jnp.bfloat16
F32 = jnp.float32
LOG2E = 1.4426950408889634

def unit(values):
    mean_val = jnp.mean(values, axis=-1, keepdims=True)
    centred = values - mean_val
    variance = jnp.mean(centred * centred, axis=-1, keepdims=True)
    scaled = lax.rsqrt(variance + 1e-05)
    return centred * scaled, scaled

def halves(v):
    high = v.astype(BF)
    return high, (v - high.astype(F32)).astype(BF)

def across(lhs, rhs):
    return lax.dot_general(lhs, rhs, (((1,), (1,)), ((), ())), preferred_element_type=F32)

def pair_kernel(pair_ref, w_ref, out_ref):
    rows, cols, chans = pair_ref.shape
    heads = w_ref.shape[0]
    raw = pair_ref[...].reshape(rows * cols, chans)
    values = raw.astype(F32)
    centred = values - jnp.mean(values, axis=-1, keepdims=True)
    weight = w_ref[...].astype(F32)
    weight = weight - jnp.mean(weight, axis=1, keepdims=True)
    w0 = weight.astype(BF)
    w1, w2 = halves(weight - w0.astype(F32))
    flat = across(jnp.concatenate([w0, w1, w2], axis=0), raw)
    flat = flat[:heads] + flat[heads : 2 * heads] + flat[2 * heads :]
    ones = jnp.full((8, chans), 1.0 / chans, BF)
    variance = across(ones, (centred * centred).astype(BF))[:1]
    flat = (flat * lax.rsqrt(variance + 1e-05)).reshape(heads, rows, cols).astype(BF)
    out_ref[:, 0] = flat
    out_ref[:, 1] = flat

def pair_bias(pair, bias_weight, step=16):
    rows, cols, chans = pair.shape
    heads = bias_weight.shape[1]
    return pl.pallas_call(
        pair_kernel, grid=(rows // step,),
        in_specs=[pl.BlockSpec((step, cols, chans), lambda i: (i, 0, 0)),
                  pl.BlockSpec((heads, chans), lambda i: (0, 0))],
        out_specs=pl.BlockSpec((heads, 2, step, cols), lambda i: (0, 0, i, 0)),
        out_shape=jax.ShapeDtypeStruct((heads, 2, rows, cols), BF),
        compiler_params=pltpu.CompilerParams(dimension_semantics=("arbitrary",), vmem_limit_bytes=60 << 20),
    )(pair, bias_weight.T)

def stats_kernel(pair_ref, normed_ref, scaled_ref):
    rows, cols, chans = pair_ref.shape
    normed, scaled = unit(pair_ref[...].astype(F32).reshape(rows * cols, chans))
    normed_ref[...] = normed.reshape(rows, cols, chans).astype(BF)
    lanes = jnp.broadcast_to(scaled, (rows * cols, chans)).reshape(rows, cols, chans)
    for i in range(rows):
        scaled_ref[i : i + 1] = lanes[i].T[:1]

def pair_stats(pair, step=16):
    rows, cols, chans = pair.shape
    return pl.pallas_call(
        stats_kernel, grid=(rows // step,),
        in_specs=[pl.BlockSpec((step, cols, chans), lambda i: (i, 0, 0))],
        out_specs=[pl.BlockSpec((step, cols, chans), lambda i: (i, 0, 0)), pl.BlockSpec((step, cols), lambda i: (i, 0))],
        out_shape=[jax.ShapeDtypeStruct((rows, cols, chans), BF), jax.ShapeDtypeStruct((rows, cols), F32)],
        compiler_params=pltpu.CompilerParams(dimension_semantics=("arbitrary",), vmem_limit_bytes=60 << 20),
    )(pair)

def back_kernel(normed_ref, scaled_ref, grad_ref, w_ref, out_ref):
    rows, cols, chans = normed_ref.shape
    heads, parts = grad_ref.shape[:2]
    grad = grad_ref[:, 0].astype(F32)
    for g in range(1, parts):
        grad = grad + grad_ref[:, g].astype(F32)
    grad = (grad * scaled_ref[...][None]).reshape(heads, rows * cols)
    high, low = halves(grad)
    weight = w_ref[...].astype(F32)
    w_high, w_low = halves(weight - jnp.mean(weight, axis=1, keepdims=True))
    both = jnp.concatenate([high, low, high, low], axis=0)
    weight = jnp.concatenate([w_high, w_high, w_low, w_low], axis=0)
    centred = lax.dot_general(both, weight, (((0,), (0,)), ((), ())), preferred_element_type=F32)
    normed = normed_ref[...].astype(F32).reshape(rows * cols, chans)
    along = jnp.mean(centred * normed, axis=-1, keepdims=True)
    out_ref[...] = (centred - normed * along).reshape(rows, cols, chans)

def pair_back(stats, grad, bias_weight, step=16):
    normed, scaled = stats
    rows, cols, chans = normed.shape
    heads, parts = grad.shape[:2]
    return pl.pallas_call(
        back_kernel, grid=(rows // step,),
        in_specs=[pl.BlockSpec((step, cols, chans), lambda i: (i, 0, 0)),
                  pl.BlockSpec((step, cols), lambda i: (i, 0)),
                  pl.BlockSpec((heads, parts, step, cols), lambda i: (0, 0, i, 0)),
                  pl.BlockSpec((heads, chans), lambda i: (0, 0))],
        out_specs=pl.BlockSpec((step, cols, chans), lambda i: (i, 0, 0)),
        out_shape=jax.ShapeDtypeStruct((rows, cols, chans), F32),
        compiler_params=pltpu.CompilerParams(dimension_semantics=("arbitrary",), vmem_limit_bytes=50 << 20),
    )(normed, scaled, grad, bias_weight.T)

def project_kernel(core_ref, single_ref, got_ref, cot_ref, gotc_ref, w_ref, packed_ref, tokens_ref, normed, cotan):
    half, block, width = tokens_ref.shape
    heads, _, lanes = packed_ref.shape
    size = width // heads
    rows = block // 2
    step = pl.program_id(0)
    core = core_ref[0]

    @pl.when(step == 0)
    def _():
        mine = pl.ds(pl.multiple_of(core * rows, rows), rows)
        other = pl.ds(pl.multiple_of((1 - core) * rows, rows), rows)
        for u in range(half):
            for src, far, dst in ((single_ref, got_ref, tokens_ref), (cot_ref, gotc_ref, cotan)):
                dst[u, mine, :] = src[core * half + u]
                dst[u, other, :] = far[core * half + u]
        normed[...] = unit(tokens_ref[...].reshape(lanes, width).astype(F32))[0].astype(BF)
        turned = cotan[...].reshape(lanes, width).astype(F32).T.astype(BF)
        for h in range(heads):
            packed_ref[h, 3 * size : 4 * size, :] = turned[h * size : (h + 1) * size]

    cols = w_ref.shape[1]
    out = jnp.dot(normed[...], w_ref[...], preferred_element_type=F32).T.astype(BF)
    for p in range(3):
        @pl.when(step // 2 == p)
        def _():
            base = (step % 2) * (cols // size)
            for h in range(cols // size):
                packed_ref[base + h, p * size : (p + 1) * size, :] = out[h * size : (h + 1) * size]

def project(core, single, got, cot, gotc, w_qkv, heads):
    samp, rows, width = single.shape
    half, block = samp // 2, 2 * rows
    lanes = half * block
    size = width // heads
    whole = pl.BlockSpec((samp, rows, width), lambda i, c: (0, 0, 0))
    return pl.pallas_call(
        project_kernel,
        grid_spec=pltpu.PrefetchScalarGridSpec(
            num_scalar_prefetch=1, grid=(6,),
            in_specs=[whole] * 4 + [pl.BlockSpec((width, width // 2), lambda i, c: (0, i))],
            out_specs=[pl.BlockSpec((heads, 4 * size, lanes), lambda i, c: (0, 0, 0)),
                       pl.BlockSpec((half, block, width), lambda i, c: (0, 0, 0))],
            scratch_shapes=[pltpu.VMEM((lanes, width), BF), pltpu.VMEM((half, block, width), BF)],
        ),
        out_shape=[jax.ShapeDtypeStruct((heads, 4 * size, lanes), BF), jax.ShapeDtypeStruct((half, block, width), BF)],
        compiler_params=pltpu.CompilerParams(dimension_semantics=("arbitrary",), vmem_limit_bytes=50 << 20),
    )(core, single, got, cot, gotc, w_qkv)

def transition_kernel(core_ref, tokens_ref, att_ref, wo_ref, wg_ref, wu_ref, wd_ref, mine_ref, theirs_ref, mid, normed, done):
    half, block, width = tokens_ref.shape
    rows = block // 2
    step = pl.program_id(0)

    @pl.when(step == 0)
    def _():
        attended = att_ref[...].astype(F32).T.astype(BF)
        flat = tokens_ref[...].reshape(half * block, width).astype(F32)
        flat = flat + jnp.dot(attended, wo_ref[...], preferred_element_type=F32)
        mid[...] = flat
        normed[...] = unit(flat)[0].astype(BF)

    gate = jnp.dot(normed[...], wg_ref[...], preferred_element_type=F32)
    up = jnp.dot(normed[...], wu_ref[...], preferred_element_type=F32)
    hidden = (jax.nn.silu(gate) * up).astype(BF)
    mid[...] += jnp.dot(hidden, wd_ref[...], preferred_element_type=F32)

    @pl.when(step == pl.num_programs(0) - 1)
    def _():
        done[...] = mid[...].astype(BF).reshape(half, block, width)
        core = core_ref[0]
        mine = pl.ds(pl.multiple_of(core * rows, rows), rows)
        other = pl.ds(pl.multiple_of((1 - core) * rows, rows), rows)
        for u in range(half):
            mine_ref[core * half + u] = done[u, mine, :]
            mine_ref[(1 - core) * half + u] = jnp.zeros((rows, width), BF)
            theirs_ref[u] = done[u, other, :]

def transition(core, tokens, attended_t, w_out, w_gate_up, w_down, steps=4):
    half, block, width = tokens.shape
    lanes = half * block
    inner = w_down.shape[0]
    part = inner // steps
    out = lambda n: pl.BlockSpec((n, block // 2, width), lambda i, c: (0, 0, 0))
    return pl.pallas_call(
        transition_kernel,
        grid_spec=pltpu.PrefetchScalarGridSpec(
            num_scalar_prefetch=1, grid=(steps,),
            in_specs=[pl.BlockSpec((half, block, width), lambda i, c: (0, 0, 0)),
                      pl.BlockSpec((width, lanes), lambda i, c: (0, 0)),
                      pl.BlockSpec((width, width), lambda i, c: (0, 0)),
                      pl.BlockSpec((width, part), lambda i, c: (0, i)),
                      pl.BlockSpec((width, part), lambda i, c: (0, i + steps)),
                      pl.BlockSpec((part, width), lambda i, c: (i, 0))],
            out_specs=[out(2 * half), out(half)],
            scratch_shapes=[pltpu.VMEM((lanes, width), F32), pltpu.VMEM((lanes, width), BF),
                            pltpu.VMEM((half, block, width), BF)],
        ),
        out_shape=[jax.ShapeDtypeStruct((n * half, block // 2, width), BF) for n in (2, 1)],
        compiler_params=pltpu.CompilerParams(dimension_semantics=("arbitrary",), vmem_limit_bytes=60 << 20),
    )(core, tokens, attended_t, w_out, w_gate_up, w_gate_up, w_down)

def split(v):
    high = v.astype(BF).astype(F32)
    return high, v - high

def attend_kernel(n_col, n_chip, per, size, c_ref, blk_ref, *refs):
    bias_refs = refs[: n_col // 2]
    att_ref = refs[n_col // 2]
    out_refs = refs[n_col // 2 + 1 : n_col]
    pair_refs = refs[n_col : n_col + 2]
    bias2, acc, kt, vt = refs[n_col + 2 :]
    me = c_ref[0]
    side = me // (n_col // 2)
    block = blk_ref.shape[3] // per
    wide = block * n_col
    rest = block - 2 * size

    for k in range(n_col):
        far = jnp.bitwise_xor(side, k // (n_col // 2))
        part = bias_refs[k % (n_col // 2)][:, far]
        part = part.astype(F32).reshape(bias2.shape[0], block)
        bias2[:, k * block : (k + 1) * block] = part * LOG2E
    row = lax.broadcasted_iota(jnp.int32, (rest, wide), 0)
    for h in range(2 * per):
        kt[h, 2 * size :, :] = jnp.zeros((rest, wide), BF)
        vt[h, 2 * size :, :] = jnp.where(row < 3, 1.0, 0.0).astype(BF)

    scale = LOG2E / math.sqrt(size)
    row = lax.broadcasted_iota(jnp.int32, (rest, block), 0)

    def prepare(u, h):
        for k in range(n_col):
            owner = jnp.bitwise_xor(me, k)
            cols = slice(k * block, (k + 1) * block)
            keys = blk_ref[owner, h, size : 2 * size, u * block : (u + 1) * block]
            kt[2 * u + h, :size, cols] = keys
            kt[2 * u + h, size : 2 * size, cols] = keys
            vals = blk_ref[owner, h, 2 * size : 3 * size, u * block : (u + 1) * block]
            vt[2 * u + h, :size, cols] = vals
            vt[2 * u + h, size : 2 * size, cols] = vals
        lhs = []
        for b in range(n_chip):
            high, low = split(blk_ref[b, h, :size, u * block : (u + 1) * block].astype(F32) * scale)
            lhs.append(jnp.concatenate([high, low, jnp.zeros((rest, block), F32)], axis=0).T.astype(BF))
        return jnp.concatenate(lhs, axis=0)

    def softmax(u, h, lhs):
        scores = jnp.dot(lhs, kt[2 * u + h], preferred_element_type=F32) + bias2[...]
        top = jnp.max(scores, axis=1, keepdims=True)
        return jnp.exp2(scores - top)

    def mix(u, h, probs):
        mixed = lax.dot_general(
            probs.astype(BF), vt[2 * u + h], (((1,), (1,)), ((), ())), preferred_element_type=F32
        )
        lhs = []
        for b in range(n_chip):
            mixed_t = mixed[b * block : (b + 1) * block].T
            inv = 1.0 / mixed_t[2 * size : 2 * size + 1]
            att = mixed_t[:size] * inv
            att_ref[b, h, :, u * block : (u + 1) * block] = att.astype(BF)
            cotan = blk_ref[b, h, 3 * size :, u * block : (u + 1) * block].astype(F32)
            delta = -jnp.sum(cotan * att, axis=0, keepdims=True) * inv
            high, low = split(cotan * inv)
            d0, rem = split(delta)
            d1, d2 = split(rem)
            tail = jnp.where(row == 0, d0, jnp.where(row == 1, d1, jnp.where(row == 2, d2, 0.0)))
            lhs.append(jnp.concatenate([high, low, tail], axis=0).T.astype(BF))
        return jnp.concatenate(lhs, axis=0)

    def grad(u, h, probs, lhs):
        return probs * jnp.dot(lhs, vt[2 * u + h], preferred_element_type=F32)

    for u in range(per):
        lhs = [prepare(u, h) for h in range(2)]
        probs = [softmax(u, h, lhs[h]) for h in range(2)]
        lhs = [mix(u, h, probs[h]) for h in range(2)]
        term = grad(u, 0, probs[0], lhs[0]) + grad(u, 1, probs[1], lhs[1])
        if u == 0:
            acc[...] = term
        elif u < per - 1:
            acc[...] += term
        else:
            term = (acc[...] + term).astype(BF)
            for k in range(n_col):
                part = term[:, k * block : (k + 1) * block]
                part = part.reshape(out_refs[0].shape[0], out_refs[0].shape[2], block)
                ring = k % (n_col // 2)
                if ring == 2:
                    pair_refs[k // (n_col // 2)][...] = part
                else:
                    out_ref = out_refs[min(ring, 2)]
                    out_ref[:, jnp.bitwise_xor(side, k // (n_col // 2))] = part


def attend(me, qkvc, biases, n_samp, size, limit=48):
    n_chip, _, _, lanes = qkvc.shape
    per = n_samp // 2
    block = lanes // per
    n_col = 2 * len(biases)
    tokens = n_chip * block
    wide = n_col * block
    parts = biases[0].shape
    whole = pl.BlockSpec(parts, lambda s, c: (0, 0, 0, 0))
    single = (parts[0],) + parts[2:]
    made = [whole] * 3 + [pl.BlockSpec(single, lambda s, c: (0, 0, 0))] * 2
    shapes = [parts] * 3 + [single] * 2
    spec = lambda feats: pl.BlockSpec((n_chip, 2, feats, lanes), lambda s, c: (0, 0, 0, 0))
    return pl.pallas_call(
        functools.partial(attend_kernel, n_col, n_chip, per, size),
        grid_spec=pltpu.PrefetchScalarGridSpec(
            num_scalar_prefetch=1,
            grid=(1,),
            in_specs=[spec(4 * size)] + [whole] * len(biases),
            out_specs=[spec(size)] + made,
            scratch_shapes=[
                pltpu.VMEM((tokens, wide), F32),
                pltpu.VMEM((tokens, wide), F32),
                pltpu.VMEM((n_samp, block, wide), BF),
                pltpu.VMEM((n_samp, block, wide), BF),
            ],
        ),
        out_shape=[jax.ShapeDtypeStruct((n_chip, 2, size, lanes), BF)]
        + [jax.ShapeDtypeStruct(shape, BF) for shape in shapes],
        compiler_params=pltpu.CompilerParams(
            dimension_semantics=("arbitrary",), vmem_limit_bytes=limit * 1024 * 1024
        ),
    )(me, qkvc, *biases)


def shards(n_row, n_col, pair, bias_weight, single, w_qkv, w_out, w_gate_up, w_down, cotangent):
    samp, rows, width = single.shape
    heads = bias_weight.shape[1]
    size = width // heads
    half = samp // 2
    block = 2 * rows
    n_chip = n_row // 2
    core = lax.rem(lax.axis_index("row"), 2).astype(jnp.int32)
    me = lax.axis_index("col").astype(jnp.int32).reshape(1)
    cores = [(i, i ^ 1) for i in range(n_row)]
    flip = lambda k: [(i, i ^ k) for i in range(n_col)]

    got = lax.ppermute(single, "row", cores)
    got_cot = lax.ppermute(cotangent, "row", cores)
    groups = [[r * n_col + z * (n_col // 2) + y for r in range(n_row) for z in range(2)] for y in range(n_col // 2)]
    share = lambda v: lax.all_to_all(
        v.reshape(2 * n_row, rows, pair.shape[1]), ("row", "col"), 0, 0, tiled=True, axis_index_groups=groups
    ).reshape(n_row, 2, rows, pair.shape[1])
    bias = share(pair_bias(pair, bias_weight, 32))
    packed, tokens = project(core.reshape(1), single, got, cotangent, got_cot, w_qkv, heads)
    biases = [bias] + [lax.ppermute(bias, "col", flip(k)) for k in range(1, n_col // 2)]

    later, _ = lax.optimization_barrier((pair, bias))
    stats = pair_stats(later, 16)
    packed = lax.all_to_all(packed, "row", 0, 0, tiled=True)
    packed, stats = lax.optimization_barrier((packed, stats))
    packed = packed.reshape(n_chip, 2, 4 * size, half * block)
    attended, *grads = attend(me, packed, biases, samp, size)
    mine, one, three, two, far = grads
    far = lax.ppermute(far, "col", flip(n_col // 2))
    one = lax.ppermute(one, "col", flip(1))
    three = lax.ppermute(three, "col", flip(3))
    attended = attended.reshape(n_row, size, half * block)
    attended = lax.all_to_all(attended, "row", 0, 0, tiled=True)
    two = lax.ppermute((two.astype(F32) + far.astype(F32)).astype(BF), "col", flip(2))
    side = lax.broadcasted_iota(jnp.int32, mine.shape, 1) == me[0] // (n_col // 2)
    total = mine.astype(F32) + one.astype(F32) + three.astype(F32)
    total = total + jnp.where(side, two.astype(F32)[:, None], 0.0)
    attended, total = lax.optimization_barrier((attended, total.astype(BF)))
    total = share(total)
    mine, theirs = transition(
        core.reshape(1), tokens, attended.reshape(width, half * block), w_out, w_gate_up, w_down
    )
    mine, theirs, total = lax.optimization_barrier((mine, theirs, total))
    got = lax.ppermute(theirs, "row", cores)
    updated = lax.dynamic_update_slice_in_dim(mine, got, (1 - core) * half, 0)
    pair_grad = pair_back(stats, total, bias_weight, 32)
    return (updated, pair_grad)


def solution(mesh):
    sizes = dict(mesh.shape)
    return jax.shard_map(
        functools.partial(shards, sizes["row"], sizes["col"]),
        mesh=mesh,
        in_specs=(
            P("row", "col", None),
            P(),
            P("col", "row", None),
            P(),
            P(),
            P(),
            P(),
            P("col", "row", None),
        ),
        out_specs=(P("col", "row", None), P("row", "col", None)),
        check_vma=False,
    )
```

```python
import functools
import math

import jax
import jax.numpy as jnp
from jax import lax
from jax.experimental import pallas as pl
from jax.experimental.pallas import tpu as pltpu
from jax.sharding import PartitionSpec as P

BF = jnp.bfloat16
F32 = jnp.float32
LOG2E = 1.4426950408889634

def unit(values):
    mean_val = jnp.mean(values, axis=-1, keepdims=True)
    centred = values - mean_val
    variance = jnp.mean(centred * centred, axis=-1, keepdims=True)
    scaled = lax.rsqrt(variance + 1e-05)
    return centred * scaled, scaled

def halves(v):
    high = v.astype(BF)
    return high, (v - high.astype(F32)).astype(BF)

def across(lhs, rhs):
    return lax.dot_general(lhs, rhs, (((1,), (1,)), ((), ())), preferred_element_type=F32)

def pair_kernel(pair_ref, w_ref, out_ref):
    rows, cols, chans = pair_ref.shape
    heads = w_ref.shape[0]
    raw = pair_ref[...].reshape(rows * cols, chans)
    values = raw.astype(F32)
    centred = values - jnp.mean(values, axis=-1, keepdims=True)
    weight = w_ref[...].astype(F32)
    weight = weight - jnp.mean(weight, axis=1, keepdims=True)
    w0 = weight.astype(BF)
    w1, w2 = halves(weight - w0.astype(F32))
    flat = across(jnp.concatenate([w0, w1, w2], axis=0), raw)
    flat = flat[:heads] + flat[heads : 2 * heads] + flat[2 * heads :]
    ones = jnp.full((8, chans), 1.0 / chans, BF)
    variance = across(ones, (centred * centred).astype(BF))[:1]
    flat = (flat * lax.rsqrt(variance + 1e-05)).reshape(heads, rows, cols).astype(BF)
    out_ref[:, 0] = flat
    out_ref[:, 1] = flat

def pair_bias(pair, bias_weight, step=16):
    rows, cols, chans = pair.shape
    heads = bias_weight.shape[1]
    return pl.pallas_call(
        pair_kernel, grid=(rows // step,),
        in_specs=[pl.BlockSpec((step, cols, chans), lambda i: (i, 0, 0)),
                  pl.BlockSpec((heads, chans), lambda i: (0, 0))],
        out_specs=pl.BlockSpec((heads, 2, step, cols), lambda i: (0, 0, i, 0)),
        out_shape=jax.ShapeDtypeStruct((heads, 2, rows, cols), BF),
        compiler_params=pltpu.CompilerParams(dimension_semantics=("arbitrary",), vmem_limit_bytes=60 << 20),
    )(pair, bias_weight.T)

def stats_kernel(pair_ref, normed_ref, scaled_ref):
    rows, cols, chans = pair_ref.shape
    normed, scaled = unit(pair_ref[...].astype(F32).reshape(rows * cols, chans))
    normed_ref[...] = normed.reshape(rows, cols, chans).astype(BF)
    lanes = jnp.broadcast_to(scaled, (rows * cols, chans)).reshape(rows, cols, chans)
    for i in range(rows):
        scaled_ref[i : i + 1] = lanes[i].T[:1]

def pair_stats(pair, step=16):
    rows, cols, chans = pair.shape
    return pl.pallas_call(
        stats_kernel, grid=(rows // step,),
        in_specs=[pl.BlockSpec((step, cols, chans), lambda i: (i, 0, 0))],
        out_specs=[pl.BlockSpec((step, cols, chans), lambda i: (i, 0, 0)), pl.BlockSpec((step, cols), lambda i: (i, 0))],
        out_shape=[jax.ShapeDtypeStruct((rows, cols, chans), BF), jax.ShapeDtypeStruct((rows, cols), F32)],
        compiler_params=pltpu.CompilerParams(dimension_semantics=("arbitrary",), vmem_limit_bytes=60 << 20),
    )(pair)

def back_kernel(normed_ref, scaled_ref, grad_ref, w_ref, out_ref):
    rows, cols, chans = normed_ref.shape
    heads, parts = grad_ref.shape[:2]
    grad = grad_ref[:, 0].astype(F32)
    for g in range(1, parts):
        grad = grad + grad_ref[:, g].astype(F32)
    grad = (grad * scaled_ref[...][None]).reshape(heads, rows * cols)
    high, low = halves(grad)
    weight = w_ref[...].astype(F32)
    w_high, w_low = halves(weight - jnp.mean(weight, axis=1, keepdims=True))
    both = jnp.concatenate([high, low, high, low], axis=0)
    weight = jnp.concatenate([w_high, w_high, w_low, w_low], axis=0)
    centred = lax.dot_general(both, weight, (((0,), (0,)), ((), ())), preferred_element_type=F32)
    normed = normed_ref[...].astype(F32).reshape(rows * cols, chans)
    along = jnp.mean(centred * normed, axis=-1, keepdims=True)
    out_ref[...] = (centred - normed * along).reshape(rows, cols, chans)

def pair_back(stats, grad, bias_weight, step=16):
    normed, scaled = stats
    rows, cols, chans = normed.shape
    heads, parts = grad.shape[:2]
    return pl.pallas_call(
        back_kernel, grid=(rows // step,),
        in_specs=[pl.BlockSpec((step, cols, chans), lambda i: (i, 0, 0)),
                  pl.BlockSpec((step, cols), lambda i: (i, 0)),
                  pl.BlockSpec((heads, parts, step, cols), lambda i: (0, 0, i, 0)),
                  pl.BlockSpec((heads, chans), lambda i: (0, 0))],
        out_specs=pl.BlockSpec((step, cols, chans), lambda i: (i, 0, 0)),
        out_shape=jax.ShapeDtypeStruct((rows, cols, chans), F32),
        compiler_params=pltpu.CompilerParams(dimension_semantics=("arbitrary",), vmem_limit_bytes=50 << 20),
    )(normed, scaled, grad, bias_weight.T)

def project_kernel(core_ref, single_ref, got_ref, cot_ref, gotc_ref, w_ref, packed_ref, tokens_ref, normed, cotan):
    half, block, width = tokens_ref.shape
    heads, _, lanes = packed_ref.shape
    size = width // heads
    rows = block // 2
    step = pl.program_id(0)
    core = core_ref[0]

    @pl.when(step == 0)
    def _():
        mine = pl.ds(pl.multiple_of(core * rows, rows), rows)
        other = pl.ds(pl.multiple_of((1 - core) * rows, rows), rows)
        for u in range(half):
            for src, far, dst in ((single_ref, got_ref, tokens_ref), (cot_ref, gotc_ref, cotan)):
                dst[u, mine, :] = src[core * half + u]
                dst[u, other, :] = far[core * half + u]
        normed[...] = unit(tokens_ref[...].reshape(lanes, width).astype(F32))[0].astype(BF)
        turned = cotan[...].reshape(lanes, width).astype(F32).T.astype(BF)
        for h in range(heads):
            packed_ref[h, 3 * size : 4 * size, :] = turned[h * size : (h + 1) * size]

    cols = w_ref.shape[1]
    out = jnp.dot(normed[...], w_ref[...], preferred_element_type=F32).T.astype(BF)
    for p in range(3):
        @pl.when(step // 2 == p)
        def _():
            base = (step % 2) * (cols // size)
            for h in range(cols // size):
                packed_ref[base + h, p * size : (p + 1) * size, :] = out[h * size : (h + 1) * size]

def project(core, single, got, cot, gotc, w_qkv, heads):
    samp, rows, width = single.shape
    half, block = samp // 2, 2 * rows
    lanes = half * block
    size = width // heads
    whole = pl.BlockSpec((samp, rows, width), lambda i, c: (0, 0, 0))
    return pl.pallas_call(
        project_kernel,
        grid_spec=pltpu.PrefetchScalarGridSpec(
            num_scalar_prefetch=1, grid=(6,),
            in_specs=[whole] * 4 + [pl.BlockSpec((width, width // 2), lambda i, c: (0, i))],
            out_specs=[pl.BlockSpec((heads, 4 * size, lanes), lambda i, c: (0, 0, 0)),
                       pl.BlockSpec((half, block, width), lambda i, c: (0, 0, 0))],
            scratch_shapes=[pltpu.VMEM((lanes, width), BF), pltpu.VMEM((half, block, width), BF)],
        ),
        out_shape=[jax.ShapeDtypeStruct((heads, 4 * size, lanes), BF), jax.ShapeDtypeStruct((half, block, width), BF)],
        compiler_params=pltpu.CompilerParams(dimension_semantics=("arbitrary",), vmem_limit_bytes=50 << 20),
    )(core, single, got, cot, gotc, w_qkv)

def transition_kernel(core_ref, tokens_ref, att_ref, wo_ref, wg_ref, wu_ref, wd_ref, mine_ref, theirs_ref, mid, normed, done):
    half, block, width = tokens_ref.shape
    rows = block // 2
    step = pl.program_id(0)

    @pl.when(step == 0)
    def _():
        attended = att_ref[...].astype(F32).T.astype(BF)
        flat = tokens_ref[...].reshape(half * block, width).astype(F32)
        flat = flat + jnp.dot(attended, wo_ref[...], preferred_element_type=F32)
        mid[...] = flat
        normed[...] = unit(flat)[0].astype(BF)

    gate = jnp.dot(normed[...], wg_ref[...], preferred_element_type=F32)
    up = jnp.dot(normed[...], wu_ref[...], preferred_element_type=F32)
    hidden = (jax.nn.silu(gate) * up).astype(BF)
    mid[...] += jnp.dot(hidden, wd_ref[...], preferred_element_type=F32)

    @pl.when(step == pl.num_programs(0) - 1)
    def _():
        done[...] = mid[...].astype(BF).reshape(half, block, width)
        core = core_ref[0]
        mine = pl.ds(pl.multiple_of(core * rows, rows), rows)
        other = pl.ds(pl.multiple_of((1 - core) * rows, rows), rows)
        for u in range(half):
            mine_ref[core * half + u] = done[u, mine, :]
            mine_ref[(1 - core) * half + u] = jnp.zeros((rows, width), BF)
            theirs_ref[u] = done[u, other, :]

def transition(core, tokens, attended_t, w_out, w_gate_up, w_down, steps=4):
    half, block, width = tokens.shape
    lanes = half * block
    inner = w_down.shape[0]
    part = inner // steps
    out = lambda n: pl.BlockSpec((n, block // 2, width), lambda i, c: (0, 0, 0))
    return pl.pallas_call(
        transition_kernel,
        grid_spec=pltpu.PrefetchScalarGridSpec(
            num_scalar_prefetch=1, grid=(steps,),
            in_specs=[pl.BlockSpec((half, block, width), lambda i, c: (0, 0, 0)),
                      pl.BlockSpec((width, lanes), lambda i, c: (0, 0)),
                      pl.BlockSpec((width, width), lambda i, c: (0, 0)),
                      pl.BlockSpec((width, part), lambda i, c: (0, i)),
                      pl.BlockSpec((width, part), lambda i, c: (0, i + steps)),
                      pl.BlockSpec((part, width), lambda i, c: (i, 0))],
            out_specs=[out(2 * half), out(half)],
            scratch_shapes=[pltpu.VMEM((lanes, width), F32), pltpu.VMEM((lanes, width), BF),
                            pltpu.VMEM((half, block, width), BF)],
        ),
        out_shape=[jax.ShapeDtypeStruct((n * half, block // 2, width), BF) for n in (2, 1)],
        compiler_params=pltpu.CompilerParams(dimension_semantics=("arbitrary",), vmem_limit_bytes=60 << 20),
    )(core, tokens, attended_t, w_out, w_gate_up, w_gate_up, w_down)

def split(v):
    high = v.astype(BF).astype(F32)
    return high, v - high

def attend_kernel(n_col, n_chip, per, size, c_ref, blk_ref, *refs):
    bias_refs = refs[: n_col // 2]
    att_ref = refs[n_col // 2]
    out_refs = refs[n_col // 2 + 1 : n_col]
    pair_refs = refs[n_col : n_col + 2]
    bias2, acc, kt, vt = refs[n_col + 2 :]
    me = c_ref[0]
    side = me // (n_col // 2)
    block = blk_ref.shape[3] // per
    wide = block * n_col
    rest = block - 2 * size

    for k in range(n_col):
        far = jnp.bitwise_xor(side, k // (n_col // 2))
        part = bias_refs[k % (n_col // 2)][:, far]
        part = part.astype(F32).reshape(bias2.shape[0], block)
        bias2[:, k * block : (k + 1) * block] = part * LOG2E
    row = lax.broadcasted_iota(jnp.int32, (rest, wide), 0)
    for h in range(2 * per):
        kt[h, 2 * size :, :] = jnp.zeros((rest, wide), BF)
        vt[h, 2 * size :, :] = jnp.where(row < 3, 1.0, 0.0).astype(BF)

    scale = LOG2E / math.sqrt(size)
    row = lax.broadcasted_iota(jnp.int32, (rest, block), 0)

    def prepare(u, h):
        for k in range(n_col):
            owner = jnp.bitwise_xor(me, k)
            cols = slice(k * block, (k + 1) * block)
            keys = blk_ref[owner, h, size : 2 * size, u * block : (u + 1) * block]
            kt[2 * u + h, :size, cols] = keys
            kt[2 * u + h, size : 2 * size, cols] = keys
            vals = blk_ref[owner, h, 2 * size : 3 * size, u * block : (u + 1) * block]
            vt[2 * u + h, :size, cols] = vals
            vt[2 * u + h, size : 2 * size, cols] = vals
        lhs = []
        for b in range(n_chip):
            high, low = split(blk_ref[b, h, :size, u * block : (u + 1) * block].astype(F32) * scale)
            lhs.append(jnp.concatenate([high, low, jnp.zeros((rest, block), F32)], axis=0).T.astype(BF))
        return jnp.concatenate(lhs, axis=0)

    def softmax(u, h, lhs):
        scores = jnp.dot(lhs, kt[2 * u + h], preferred_element_type=F32) + bias2[...]
        top = jnp.max(scores, axis=1, keepdims=True)
        return jnp.exp2(scores - top)

    def mix(u, h, probs):
        mixed = lax.dot_general(
            probs.astype(BF), vt[2 * u + h], (((1,), (1,)), ((), ())), preferred_element_type=F32
        )
        lhs = []
        for b in range(n_chip):
            mixed_t = mixed[b * block : (b + 1) * block].T
            inv = 1.0 / mixed_t[2 * size : 2 * size + 1]
            att = mixed_t[:size] * inv
            att_ref[b, h, :, u * block : (u + 1) * block] = att.astype(BF)
            cotan = blk_ref[b, h, 3 * size :, u * block : (u + 1) * block].astype(F32)
            delta = -jnp.sum(cotan * att, axis=0, keepdims=True) * inv
            high, low = split(cotan * inv)
            d0, rem = split(delta)
            d1, d2 = split(rem)
            tail = jnp.where(row == 0, d0, jnp.where(row == 1, d1, jnp.where(row == 2, d2, 0.0)))
            lhs.append(jnp.concatenate([high, low, tail], axis=0).T.astype(BF))
        return jnp.concatenate(lhs, axis=0)

    def grad(u, h, probs, lhs):
        return probs * jnp.dot(lhs, vt[2 * u + h], preferred_element_type=F32)

    for u in range(per):
        lhs = [prepare(u, h) for h in range(2)]
        probs = [softmax(u, h, lhs[h]) for h in range(2)]
        lhs = [mix(u, h, probs[h]) for h in range(2)]
        term = grad(u, 0, probs[0], lhs[0]) + grad(u, 1, probs[1], lhs[1])
        if u == 0:
            acc[...] = term
        elif u < per - 1:
            acc[...] += term
        else:
            term = (acc[...] + term).astype(BF)
            for k in range(n_col):
                part = term[:, k * block : (k + 1) * block]
                part = part.reshape(out_refs[0].shape[0], out_refs[0].shape[2], block)
                ring = k % (n_col // 2)
                if ring == 2:
                    pair_refs[k // (n_col // 2)][...] = part
                else:
                    out_ref = out_refs[min(ring, 2)]
                    out_ref[:, jnp.bitwise_xor(side, k // (n_col // 2))] = part


def attend(me, qkvc, biases, n_samp, size, limit=48):
    n_chip, _, _, lanes = qkvc.shape
    per = n_samp // 2
    block = lanes // per
    n_col = 2 * len(biases)
    tokens = n_chip * block
    wide = n_col * block
    parts = biases[0].shape
    whole = pl.BlockSpec(parts, lambda s, c: (0, 0, 0, 0))
    single = (parts[0],) + parts[2:]
    made = [whole] * 3 + [pl.BlockSpec(single, lambda s, c: (0, 0, 0))] * 2
    shapes = [parts] * 3 + [single] * 2
    spec = lambda feats: pl.BlockSpec((n_chip, 2, feats, lanes), lambda s, c: (0, 0, 0, 0))
    return pl.pallas_call(
        functools.partial(attend_kernel, n_col, n_chip, per, size),
        grid_spec=pltpu.PrefetchScalarGridSpec(
            num_scalar_prefetch=1,
            grid=(1,),
            in_specs=[spec(4 * size)] + [whole] * len(biases),
            out_specs=[spec(size)] + made,
            scratch_shapes=[
                pltpu.VMEM((tokens, wide), F32),
                pltpu.VMEM((tokens, wide), F32),
                pltpu.VMEM((n_samp, block, wide), BF),
                pltpu.VMEM((n_samp, block, wide), BF),
            ],
        ),
        out_shape=[jax.ShapeDtypeStruct((n_chip, 2, size, lanes), BF)]
        + [jax.ShapeDtypeStruct(shape, BF) for shape in shapes],
        compiler_params=pltpu.CompilerParams(
            dimension_semantics=("arbitrary",), vmem_limit_bytes=limit * 1024 * 1024
        ),
    )(me, qkvc, *biases)


def shards(n_row, n_col, pair, bias_weight, single, w_qkv, w_out, w_gate_up, w_down, cotangent):
    samp, rows, width = single.shape
    heads = bias_weight.shape[1]
    size = width // heads
    half = samp // 2
    block = 2 * rows
    n_chip = n_row // 2
    core = lax.rem(lax.axis_index("row"), 2).astype(jnp.int32)
    me = lax.axis_index("col").astype(jnp.int32).reshape(1)
    cores = [(i, i ^ 1) for i in range(n_row)]
    flip = lambda k: [(i, i ^ k) for i in range(n_col)]

    got = lax.ppermute(single, "row", cores)
    got_cot = lax.ppermute(cotangent, "row", cores)
    groups = [[r * n_col + z * (n_col // 2) + y for r in range(n_row) for z in range(2)] for y in range(n_col // 2)]
    share = lambda v: lax.all_to_all(
        v.reshape(2 * n_row, rows, pair.shape[1]), ("row", "col"), 0, 0, tiled=True, axis_index_groups=groups
    ).reshape(n_row, 2, rows, pair.shape[1])
    bias = share(pair_bias(pair, bias_weight, 32))
    packed, tokens = project(core.reshape(1), single, got, cotangent, got_cot, w_qkv, heads)
    biases = [bias] + [lax.ppermute(bias, "col", flip(k)) for k in range(1, n_col // 2)]

    later, _ = lax.optimization_barrier((pair, bias))
    stats = pair_stats(later, 16)
    packed = lax.all_to_all(packed, "row", 0, 0, tiled=True)
    packed, stats = lax.optimization_barrier((packed, stats))
    packed = packed.reshape(n_chip, 2, 4 * size, half * block)
    attended, *grads = attend(me, packed, biases, samp, size)
    mine, one, three, two, far = grads
    far = lax.ppermute(far, "col", flip(n_col // 2))
    one = lax.ppermute(one, "col", flip(1))
    three = lax.ppermute(three, "col", flip(3))
    attended = attended.reshape(n_row, size, half * block)
    attended = lax.all_to_all(attended, "row", 0, 0, tiled=True)
    two = lax.ppermute((two.astype(F32) + far.astype(F32)).astype(BF), "col", flip(2))
    side = lax.broadcasted_iota(jnp.int32, mine.shape, 1) == me[0] // (n_col // 2)
    total = mine.astype(F32) + one.astype(F32) + three.astype(F32)
    total = total + jnp.where(side, two.astype(F32)[:, None], 0.0)
    attended, total = lax.optimization_barrier((attended, total.astype(BF)))
    total = share(total)
    mine, theirs = transition(
        core.reshape(1), tokens, attended.reshape(width, half * block), w_out, w_gate_up, w_down
    )
    mine, theirs, total = lax.optimization_barrier((mine, theirs, total))
    got = lax.ppermute(theirs, "row", cores)
    updated = lax.dynamic_update_slice_in_dim(mine, got, (1 - core) * half, 0)
    pair_grad = pair_back(stats, total, bias_weight, 16)
    return (updated, pair_grad)


def solution(mesh):
    sizes = dict(mesh.shape)
    return jax.shard_map(
        functools.partial(shards, sizes["row"], sizes["col"]),
        mesh=mesh,
        in_specs=(
            P("row", "col", None),
            P(),
            P("col", "row", None),
            P(),
            P(),
            P(),
            P(),
            P("col", "row", None),
        ),
        out_specs=(P("col", "row", None), P("row", "col", None)),
        check_vma=False,
    )
```
